32 devices in a mesh: seq: 2 (over x), fsdp: 16 (over z, y, core).
Axes of the slice: x: 2, y: 2, z: 4, core: 2. Of those that a mesh axis runs over, the one named last changes fastest.
Arguments:
- tokens: bfloat16 [4096, 1024], P(('fsdp', 'seq')), may hold values from -6 to 6
- cotangent: bfloat16 [4096, 1024], P(('fsdp', 'seq')), may hold values from -6 to 6
- documents: int32 [16, 256], P('fsdp'), may hold values from 0 to 3, never falling along the last dimension, each value on 1 to 128 neighbouring positions
- in_weight: bfloat16 [1024, 4384], P('fsdp'), may hold values from -0.1875 to 0.1875
- kernel_taps: float32 [4, 2304], replicated, may hold values from -3 to 3
- kernel_bias: float32 [2304], replicated, may hold values from -0.5 to 0.5
- step_bias: float32 [32], replicated, may hold values from -6 to -2
- decay_log: float32 [32], replicated, may hold values from 0 to 2.77
- skip_gain: float32 [32], replicated, may hold values from 0.5 to 1.5
- pre_gain: float32 [1024], replicated, may hold values from 0.5 to 1.5
- norm_gain: float32 [2048], replicated, may hold values from 0.5 to 1.5
- out_weight: bfloat16 [2048, 1024], P('fsdp'), may hold values from -0.125 to 0.125
Outputs:
- block_output: bfloat16 [4096, 1024], P(('fsdp', 'seq'))
- tokens_grad: float32 [4096, 1024], P(('fsdp', 'seq'))
- in_weight_grad: float32 [1024, 4384], P('fsdp')
- kernel_taps_grad: float32 [4, 2304], replicated
- kernel_bias_grad: float32 [2304], replicated
- step_bias_grad: float32 [32], replicated
- decay_log_grad: float32 [32], replicated
- skip_gain_grad: float32 [32], replicated
- pre_gain_grad: float32 [1024], replicated
- norm_gain_grad: float32 [2048], replicated
- out_weight_grad: float32 [2048, 1024], P('fsdp')
The draws below stay inside these ranges and needn't reach their ends.
Inputs may be any that keep to these rules, and one draw needn't show every extreme that they name: `documents`: in every sequence the ids start at 0 and never fall; each id marks one document of consecutive tokens, and every id of 0 to 3 occurs.
All inputs are finite; a program needn't handle non-finite values.
Results may differ from the reference program's by a relative error of at most 0.011.
Values may be sent and summed in bfloat16 or wider, within the bound.
A program may use at most 128 MiB of HBM per device.

```python
import math
from functools import partial
import jax
import jax.numpy as jnp
import numpy as np
from jax import lax

D = 1024
HEADS = 32
HEAD_DIM = 64
STATE = 128
CONV = 4
SPAN = 256
DOCS = 4
INNER = 2048
CONV_CH = 2304
PROJ = 4384
SEQ_LEN = 256
SEQS = 16
TOKENS = 4096


def shard_levels(stream_key, extent, pieces, least, high):
    factor_of, own = 1.0, jax.random.fold_in(stream_key, 6)
    for axis_at, blocks in pieces:
        steps = jnp.exp(jax.random.uniform(jax.random.fold_in(own, axis_at), (blocks,), jnp.float32, least / len(pieces), high / len(pieces)))
        factor_of = factor_of * jnp.repeat(steps, extent[axis_at] // blocks).reshape([-1 if axis == axis_at else 1 for axis in range(len(extent))])
    return factor_of


def profile(amount, total, most, lean):
    weights = [(1 << 20) // math.isqrt(standing ** lean) + 1 for standing in range(2, amount + 1)]
    surplus, counts = total - most - (amount - 1), [1] * (amount - 1)
    while surplus > 0:
        free = [i for i in range(amount - 1) if counts[i] < most]
        mass, left = sum([weights[i] for i in free]), surplus
        for i in free:
            extra = min(most - counts[i], max(1, left * weights[i] // mass), surplus)
            counts[i] = counts[i] + extra
            surplus = surplus - extra
    return np.array([most] + counts)


def ragged(rng, number_of, total, most, skew):
    if number_of == 2:
        one = jax.random.randint(rng, (), max(1, total - most), min(most, total - 1) + 1)
        return jnp.stack([one, total - one])
    tallies = jnp.asarray(profile(number_of, total, most, skew), jnp.int32)
    twos = (number_of - 1) // 2
    source_of, sink = tallies[1:1 + 2 * twos:2], tallies[2:2 + 2 * twos:2]
    room = jnp.minimum(source_of - 1, most - sink)
    moved = jax.random.randint(jax.random.fold_in(rng, 1), (twos,), 0, 1 << 20) % (room + 1)
    tallies = tallies.at[1:1 + 2 * twos:2].set(source_of - moved).at[2:2 + 2 * twos:2].set(sink + moved)
    return tallies[jax.random.permutation(jax.random.fold_in(rng, 2), number_of)]


def normal_values(rng, shape, spread, reach, pieces=(), kind=jnp.bfloat16):
    drawn = jax.random.normal(rng, shape, jnp.float32) * spread
    if len(pieces) > 0:
        drawn = shard_levels(rng, shape, pieces, -0.22, 0.18) * drawn
    return jnp.clip(drawn, min=-reach, max=reach).astype(kind)


def setup_inputs(seed: int = 0) -> dict:
    key_of = jax.random.split(jax.random.key(seed), 13)
    return {
        "tokens": normal_values(key_of[0], (TOKENS, D), 1.0, 6.0, ((0, 32),)),
        "cotangent": normal_values(key_of[1], (TOKENS, D), 1.0, 6.0, ((0, 32),)),
        "documents": jax.vmap(lambda own: jnp.searchsorted(jnp.cumsum(ragged(own, DOCS, SEQ_LEN, SEQ_LEN // 2, 1)), jnp.arange(SEQ_LEN), side="right"))(jax.random.split(key_of[2], SEQS)).reshape((SEQS, SEQ_LEN)).astype(jnp.int32),
        "in_weight": normal_values(key_of[3], (D, PROJ), D ** -0.5, 0.1875, ((0, 16),)),
        "kernel_taps": normal_values(key_of[4], (CONV, CONV_CH), CONV ** -0.5, 3.0, (), jnp.float32),
        "kernel_bias": jnp.clip(jax.random.uniform(key_of[5], (CONV_CH,), jnp.float32, -0.5, 0.5), -0.5, 0.5),
        "step_bias": jnp.clip(jax.random.uniform(key_of[6], (HEADS,), jnp.float32, -6.0, -2.0), -6.0, -2.0),
        "decay_log": jnp.clip(jax.random.uniform(key_of[7], (HEADS,), jnp.float32, 0.0, 2.77), 0.0, 2.77),
        "skip_gain": jnp.clip(jax.random.uniform(key_of[8], (HEADS,), jnp.float32, 0.5, 1.5), 0.5, 1.5),
        "pre_gain": jnp.clip(1.0 + 0.1 * jax.random.normal(key_of[9], (D,), jnp.float32), 0.5, 1.5),
        "norm_gain": jnp.clip(1.0 + 0.1 * jax.random.normal(key_of[10], (INNER,), jnp.float32), 0.5, 1.5),
        "out_weight": normal_values(key_of[11], (INNER, D), INNER ** -0.5, 0.125, ((0, 16),)),
    }


norm_epsilon = 1e-05

def pre_norm(values, gain):
    scale = lax.rsqrt(lax.optimization_barrier(jnp.mean(values * values, axis=-1, keepdims=True)) + norm_epsilon)
    return values * scale * gain

def gate_norm(mixed, gates, gain):
    gated = mixed * jax.nn.silu(gates)
    scale = lax.rsqrt(lax.optimization_barrier(jnp.mean(gated * gated, axis=-1, keepdims=True)) + norm_epsilon)
    return gated * scale * gain

def block_step(state, block):
    scaled, input_matrix, output_matrix, log_block, seg_block, prev_last = block
    width = seg_block.shape[0]
    cumul = jnp.cumsum(log_block, axis=0).T
    places = jnp.arange(width)
    causal = (places[:, None] >= places[None, :]) & (seg_block[:, None] == seg_block[None, :])
    log_gap = cumul[:, :, None] - cumul[:, None, :]
    decay = jnp.where(causal[None], jnp.exp(jnp.where(causal[None], log_gap, 0.0)), 0.0)
    scores = jnp.dot(output_matrix, input_matrix.T, precision=lax.Precision.HIGHEST)
    inside = jnp.einsum('hij,jhp->ihp', decay * scores[None], scaled, precision=lax.Precision.HIGHEST)
    entering = jnp.exp(cumul) * (seg_block == prev_last).astype(jnp.float32)[None]
    carried = jnp.einsum('in,hnp->ihp', output_matrix, state, precision=lax.Precision.HIGHEST) * entering.T[:, :, None]
    final = cumul[:, -1]
    leaving = jnp.exp(final[:, None] - cumul) * (seg_block == seg_block[-1]).astype(jnp.float32)[None]
    fresh = jnp.einsum('hj,jn,jhp->hnp', leaving, input_matrix, scaled, precision=lax.Precision.HIGHEST)
    keeping = jnp.exp(final) * (seg_block[-1] == prev_last).astype(jnp.float32)
    new_state = keeping[:, None, None] * state + fresh
    return (new_state, inside + carried)

def mixer(segment, conv_in, step_raw, taps, tap_bias, bias_steps, log_rates, skips):
    length, channels = conv_in.shape
    heads = step_raw.shape[1]
    width = heads * HEAD_DIM
    summed = tap_bias + conv_in * taps[CONV - 1]
    for offset in range(1, CONV):
        shifted = jnp.concatenate([jnp.zeros((offset, channels), jnp.float32), conv_in[:length - offset]], axis=0)
        matched = jnp.concatenate([jnp.zeros((offset,), jnp.float32), (segment[offset:] == segment[:length - offset]).astype(jnp.float32)])
        summed = summed + taps[CONV - 1 - offset] * shifted * matched[:, None]
    active = jax.nn.silu(summed)
    values = active[:, :width].reshape(length, heads, HEAD_DIM)
    input_matrix = active[:, width:width + STATE]
    output_matrix = active[:, width + STATE:]
    steps_taken = jax.nn.softplus(step_raw + bias_steps)
    log_decay = steps_taken * -jnp.exp(log_rates)
    scaled = values * steps_taken[:, :, None]
    blocks = length // SPAN
    seg_blocks = segment.reshape(blocks, SPAN)
    prev_last = jnp.concatenate([seg_blocks[:1, 0], seg_blocks[:-1, -1]])
    initial = jnp.zeros((heads, STATE, HEAD_DIM), jnp.float32)
    _, outputs = lax.scan(block_step, initial, (scaled.reshape(blocks, SPAN, heads, HEAD_DIM), input_matrix.reshape(blocks, SPAN, STATE), output_matrix.reshape(blocks, SPAN, STATE), log_decay.reshape(blocks, SPAN, heads), seg_blocks, prev_last))
    result = outputs.reshape(length, heads, HEAD_DIM) + values * skips[None, :, None]
    return result.reshape(length, width)

def reference(tokens, cotangent, documents, in_weight, kernel_taps, kernel_bias, step_bias, decay_log, skip_gain, pre_gain, norm_gain, out_weight):

    def sequence_pass(carry, inputs):
        tokens_seq, cot_seq, segment = inputs
        floats = tokens_seq.astype(jnp.float32)
        normed_in = pre_norm(floats, pre_gain).astype(jnp.bfloat16)
        projected = jnp.dot(normed_in, in_weight, preferred_element_type=jnp.float32).astype(jnp.bfloat16)
        gates = projected[:, :INNER]
        conv_in = projected[:, INNER:INNER + CONV_CH]
        step_raw = projected[:, INNER + CONV_CH:]
        mixed, mixer_back = jax.vjp(partial(mixer, segment), conv_in.astype(jnp.float32), step_raw.astype(jnp.float32), kernel_taps, kernel_bias, step_bias, decay_log, skip_gain)
        mixed_bf = mixed.astype(jnp.bfloat16)
        normed_out, norm_back = jax.vjp(gate_norm, mixed_bf.astype(jnp.float32), gates.astype(jnp.float32), norm_gain)
        normed_bf = normed_out.astype(jnp.bfloat16)
        branch = jnp.dot(normed_bf, out_weight, preferred_element_type=jnp.float32)
        block_out = (floats + branch).astype(jnp.bfloat16)
        back_normed = jnp.dot(cot_seq, out_weight.T, preferred_element_type=jnp.float32)
        out_grad = jnp.dot(normed_bf.T, cot_seq, preferred_element_type=jnp.float32)
        back_mixed, back_gates, gain_two = norm_back(back_normed)
        back_mixed_bf = back_mixed.astype(jnp.bfloat16)
        grads = mixer_back(back_mixed_bf.astype(jnp.float32))
        back_projected = jnp.concatenate([back_gates.astype(jnp.bfloat16), grads[0].astype(jnp.bfloat16), grads[1].astype(jnp.bfloat16)], axis=1)
        back_normed_in = jnp.dot(back_projected, in_weight.T, preferred_element_type=jnp.float32)
        in_grad = jnp.dot(normed_in.T, back_projected, preferred_element_type=jnp.float32)
        _, pre_back = jax.vjp(pre_norm, floats, pre_gain)
        back_floats, gain_one = pre_back(back_normed_in)
        token_grad = cot_seq.astype(jnp.float32) + back_floats
        updates = (in_grad, grads[2], grads[3], grads[4], grads[5], grads[6], gain_one, gain_two, out_grad)
        carry = tuple((total + part for total, part in zip(carry, updates)))
        return (carry, (block_out, token_grad))
    initial = (jnp.zeros((D, PROJ), jnp.float32), jnp.zeros((CONV, CONV_CH), jnp.float32), jnp.zeros((CONV_CH,), jnp.float32), jnp.zeros((HEADS,), jnp.float32), jnp.zeros((HEADS,), jnp.float32), jnp.zeros((HEADS,), jnp.float32), jnp.zeros((D,), jnp.float32), jnp.zeros((INNER,), jnp.float32), jnp.zeros((INNER, D), jnp.float32))
    totals, (outputs, token_grads) = lax.scan(sequence_pass, initial, (tokens.reshape(SEQS, SEQ_LEN, D), cotangent.reshape(SEQS, SEQ_LEN, D), documents))
    return (outputs.reshape(TOKENS, D), token_grads.reshape(TOKENS, D), totals[0], totals[1], totals[2], totals[3], totals[4], totals[5], totals[6], totals[7], totals[8])
```

```python
import functools
import math

import jax
import jax.numpy as jnp
from jax import lax
from jax.experimental import pallas as pl
from jax.experimental.pallas import tpu as pltpu
from jax.sharding import PartitionSpec as P

HEAD_DIM = 64
STATE = 128
CONV = 4
SPAN = 256

norm_epsilon = 1e-05
bf16 = jnp.bfloat16
f32 = jnp.float32
contract_rows = (((1,), (1,)), ((), ()))
contract_tokens = (((0,), (0,)), ((), ()))


def dot(left, right, dims=(((1,), (0,)), ((), ()))):
    return lax.dot_general(left, right, dims, preferred_element_type=f32)


def pre_norm(values, gain):
    scale = lax.rsqrt(jnp.mean(values * values, axis=-1, keepdims=True) + norm_epsilon)
    return values * scale * gain


def product(spec, left, right):
    return jnp.einsum(spec, left.astype(bf16), right.astype(bf16), preferred_element_type=f32)


def mixer(segment, conv_in, step_raw, taps, tap_bias, bias_steps, log_rates, skips):
    length, channels = conv_in.shape
    heads = step_raw.shape[1]
    width = heads * HEAD_DIM
    summed = tap_bias + conv_in * taps[CONV - 1]
    for offset in range(1, CONV):
        shifted = jnp.concatenate(
            [jnp.zeros((offset, channels), f32), conv_in[: length - offset]], axis=0
        )
        matched = jnp.concatenate(
            [
                jnp.zeros((offset,), f32),
                (segment[offset:] == segment[: length - offset]).astype(f32),
            ]
        )
        summed = summed + taps[CONV - 1 - offset] * shifted * matched[:, None]
    active = jax.nn.silu(summed)
    values = active[:, :width].reshape(length, heads, HEAD_DIM).transpose(1, 0, 2)
    input_matrix = active[:, width : width + STATE]
    output_matrix = active[:, width + STATE :]
    steps_taken = jax.nn.softplus(step_raw + bias_steps)
    log_decay = (steps_taken * -jnp.exp(log_rates)).T
    scaled = values * steps_taken.T[:, :, None]
    span = min(SPAN, length)
    blocks = length // span
    places = jnp.arange(span)
    state = None
    outputs = []
    for block in range(blocks):
        at = slice(block * span, (block + 1) * span)
        seg = segment[at]
        cumul = jnp.cumsum(log_decay[:, at], axis=1)
        causal = (places[:, None] >= places[None, :]) & (seg[:, None] == seg[None, :])
        log_gap = cumul[:, :, None] - cumul[:, None, :]
        decay = jnp.where(causal[None], jnp.exp(jnp.where(causal[None], log_gap, 0.0)), 0.0)
        scores = product("in,jn->ij", output_matrix[at], input_matrix[at])
        inside = product("hij,hjp->hip", decay * scores[None], scaled[:, at])
        if state is not None:
            previous = segment[block * span - 1]
            entering = jnp.exp(cumul) * (seg == previous).astype(f32)[None]
            inside = inside + product("in,hnp->hip", output_matrix[at], state) * entering[:, :, None]
        if block + 1 < blocks:
            final = cumul[:, -1]
            leaving = jnp.exp(final[:, None] - cumul) * (seg == seg[-1]).astype(f32)[None]
            fresh = product("jn,hjp->hnp", input_matrix[at], scaled[:, at] * leaving[:, :, None])
            if state is None:
                state = fresh
            else:
                keeping = jnp.exp(final) * (seg[-1] == previous).astype(f32)
                state = keeping[:, None, None] * state + fresh
        outputs.append(inside)
    whole = outputs[0] if blocks == 1 else jnp.concatenate(outputs, axis=1)
    result = whole + values * skips[:, None, None]
    return result.transpose(1, 0, 2).reshape(length, width)

MESH = pl.DeviceIdType.MESH
VMEM_LIMIT = 60 * 1024 * 1024


def factors(shards):
    rest = shards // 2
    mid = 1 << (int(math.log2(rest)) // 2)
    return rest // mid, mid


def position(top, mid):
    me = lax.axis_index("fsdp")
    return me, me // (2 * mid), lax.rem(me // 2, mid), lax.rem(me, 2)


def slot_of(t, m, core, mid):
    return (t * mid + m) * 2 + core


def greet(groups, top, mid):
    me, t, m, core = position(top, mid)
    group = lax.axis_index("seq")
    peers = [{"fsdp": slot_of(lax.rem(t + d, top), m, core, mid)} for d in range(1, top)]
    peers += [{"fsdp": slot_of(t, lax.rem(m + e, mid), core, mid)} for e in range(1, mid)]
    peers += [{"fsdp": slot_of(t, m, 1 - core, mid)}]
    peers += [{"seq": lax.rem(group + k, groups)} for k in range(1, groups)]
    barrier = pltpu.get_barrier_semaphore()
    for peer in peers:
        pl.semaphore_signal(barrier, inc=1, device_id=peer, device_id_type=MESH)
    pl.semaphore_wait(barrier, len(peers))


def remote(source, target, send, receive, device):
    copy = pltpu.make_async_remote_copy(
        src_ref=source,
        dst_ref=target,
        send_sem=send,
        recv_sem=receive,
        device_id=device,
        device_id_type=MESH,
    )
    copy.start()
    return copy


def gather_kernel(groups, top, mid, count, *refs):
    rows, shards = refs[0], refs[1 : 1 + count]
    all_rows, wholes = refs[1 + count], refs[2 + count : 2 + 2 * count]
    send, receive, row_send, row_receive = refs[2 + 2 * count :]
    me, t, m, core = position(top, mid)
    group = lax.axis_index("seq")
    greet(groups, top, mid)
    copies = {}

    def launch(a, key, source, slot, device):
        copies[(a,) + key] = remote(
            source, wholes[a].at[slot], send.at[(a,) + key], receive.at[(a,) + key], device
        )

    other = {"fsdp": slot_of(t, m, 1 - core, mid)}
    for a in range(count):
        for d in range(1, top):
            peer = {"fsdp": slot_of(lax.rem(t + d, top), m, core, mid)}
            launch(a, (d, 0, 0), shards[a], me, peer)
        for e in range(1, mid):
            peer = {"fsdp": slot_of(t, lax.rem(m + e, mid), core, mid)}
            launch(a, (0, e, 0), shards[a], me, peer)
        launch(a, (0, 0, 1), shards[a], me, other)
    for k in range(1, groups):
        copies[("rows", k)] = remote(
            rows,
            all_rows.at[group],
            row_send.at[k],
            row_receive.at[k],
            {"seq": lax.rem(group + k, groups)},
        )
    for a in range(count):
        wholes[a][me] = shards[a][...]
    all_rows[group] = rows[...]
    for a in range(count):
        for d in range(1, top):
            copies[(a, d, 0, 0)].wait_recv()
            slot = slot_of(lax.rem(t - d + top, top), m, core, mid)
            for e in range(1, mid):
                peer = {"fsdp": slot_of(t, lax.rem(m + e, mid), core, mid)}
                launch(a, (d, e, 0), wholes[a].at[slot], slot, peer)
            launch(a, (d, 0, 1), wholes[a].at[slot], slot, other)
    for a in range(count):
        for d in range(top):
            for e in range(1, mid):
                copies[(a, d, e, 0)].wait_recv()
                slot = slot_of(lax.rem(t - d + top, top), lax.rem(m - e + mid, mid), core, mid)
                launch(a, (d, e, 1), wholes[a].at[slot], slot, other)
    for key, copy in copies.items():
        copy.wait_send()
        if key[0] == "rows" or key[3] == 1:
            copy.wait_recv()


def gather_all(groups, shards, rows, arrays):
    top, mid = factors(shards)
    count = len(arrays)
    vmem = pl.BlockSpec(memory_space=pltpu.VMEM)
    out = [jax.ShapeDtypeStruct((groups,) + rows.shape, rows.dtype)]
    out += [jax.ShapeDtypeStruct((shards,) + array.shape, array.dtype) for array in arrays]
    return pl.pallas_call(
        functools.partial(gather_kernel, groups, top, mid, count),
        out_shape=out,
        in_specs=[vmem] * (1 + count),
        out_specs=[vmem] * (1 + count),
        scratch_shapes=[
            pltpu.SemaphoreType.DMA((count, top, mid, 2)),
            pltpu.SemaphoreType.DMA((count, top, mid, 2)),
            pltpu.SemaphoreType.DMA((groups,)),
            pltpu.SemaphoreType.DMA((groups,)),
        ],
        compiler_params=pltpu.CompilerParams(
            collective_id=0, has_side_effects=True, vmem_limit_bytes=VMEM_LIMIT
        ),
    )(rows, *arrays)


CHUNKS = 2


def add(left, right):
    return (left.astype(f32) + right.astype(f32)).astype(bf16)


def scatter_kernel(groups, top, mid, count, *refs):
    partial, flat, grads = refs[0], refs[1], refs[2 : 2 + count]
    refs = refs[2 + count :]
    summed, total, owned = refs[0], refs[1], refs[2 : 2 + count]
    refs = refs[2 + count :]
    pair = refs[:count]
    middle = refs[count : 2 * count]
    line = refs[2 * count : 3 * count]
    far = refs[3 * count : 4 * count]
    flat_pair, flat_mid, flat_top, flat_group, send, receive, flat_send, flat_receive, sum_sems = (
        refs[4 * count :]
    )
    me, t, m, core = position(top, mid)
    group = lax.axis_index("seq")
    greet(groups, top, mid)
    other = {"fsdp": slot_of(t, m, 1 - core, mid)}
    to_mid = [{"fsdp": slot_of(t, lax.rem(m + e, mid), core, mid)} for e in range(mid)]
    to_top = [{"fsdp": slot_of(lax.rem(t + d, top), m, core, mid)} for d in range(top)]
    to_group = [{"seq": lax.rem(group + k, groups)} for k in range(groups)]
    copies = []

    def launch(source, target, index, device):
        copy = remote(source, target, send.at[index], receive.at[index], device)
        copies.append(copy)
        return copy

    def launch_flat(stage, buffer, own, peers):
        started = []
        for k in range(1, len(peers)):
            copy = remote(
                buffer.at[own],
                buffer.at[own],
                flat_send.at[stage, k],
                flat_receive.at[stage, k],
                peers[k],
            )
            started.append(copy)
            copies.append(copy)
        return started

    def total_of(buffer, started):
        for copy in started:
            copy.wait_recv()
        value = buffer[0]
        for k in range(1, buffer.shape[0]):
            value = value + buffer[k]
        return value

    work = [(a, r) for a in range(count) for r in range(CHUNKS)]
    rows_of = [grads[a].shape[3] // CHUNKS for a in range(count)]

    def part(a, r):
        return pl.ds(r * rows_of[a], rows_of[a])

    flat_pair[core] = flat[...]
    stage_flat = launch_flat(0, flat_pair, core, [None, other])
    stage = {}
    for n, (a, r) in enumerate(work):
        stage[n] = launch(
            grads[a].at[:, :, 1 - core, part(a, r)], pair[a].at[:, :, part(a, r)], (n, 0), other
        )
    sums = []
    for k in range(1, groups):
        copy = remote(
            partial.at[lax.rem(group + k, groups)],
            summed.at[group],
            sum_sems.at[0, k],
            sum_sems.at[1, k],
            to_group[k],
        )
        sums.append(copy)
    summed[group] = partial[group]

    stage_mid = {}
    for n, (a, r) in enumerate(work):
        stage[n].wait_recv()

        @pl.loop(0, top)
        def _(i):
            for j in range(mid):
                at = part(a, r)
                pair[a][i, j, at] = add(pair[a][i, j, at], grads[a][i, j, core, at])

        for e in range(1, mid):
            stage_mid[n, e] = launch(
                pair[a].at[:, lax.rem(m + e, mid), part(a, r)],
                middle[a].at[e - 1, :, part(a, r)],
                (n, e),
                to_mid[e],
            )
        if n == 0:
            flat_mid[m] = total_of(flat_pair, stage_flat)
            stage_flat = launch_flat(1, flat_mid, m, to_mid)
    stage_top = {}
    for n, (a, r) in enumerate(work):
        for e in range(1, mid):
            stage_mid[n, e].wait_recv()

        @pl.loop(0, top)
        def _(i):
            at = part(a, r)
            value = pair[a][i, m, at].astype(f32)
            for e in range(1, mid):
                value = value + middle[a][e - 1, i, at].astype(f32)
            line[a][i, at] = value.astype(bf16)

        for d in range(1, top):
            stage_top[n, d] = launch(
                line[a].at[lax.rem(t + d, top), part(a, r)],
                far[a].at[d - 1, part(a, r)],
                (n, mid + d - 1),
                to_top[d],
            )
        if n == 0:
            flat_top[t] = total_of(flat_mid, stage_flat)
            stage_flat = launch_flat(2, flat_top, t, to_top)
    last = []
    for n, (a, r) in enumerate(work):
        at = part(a, r)
        for d in range(1, top):
            stage_top[n, d].wait_recv()
        value = line[a][t, at].astype(f32)
        for d in range(1, top):
            value = value + far[a][d - 1, at].astype(f32)
        owned[a][group, at] = value.astype(bf16)
        for k in range(1, groups):
            last.append(
                launch(
                    owned[a].at[group, at],
                    owned[a].at[group, at],
                    (n, mid + top - 2 + k),
                    to_group[k],
                )
            )
        if n == 0:
            flat_group[group] = total_of(flat_top, stage_flat)
            stage_flat = launch_flat(3, flat_group, group, to_group)
    total[...] = total_of(flat_group, stage_flat)
    for copy in last:
        copy.wait_recv()
    for copy in sums:
        copy.wait()
    for copy in copies:
        copy.wait_send()


def scatter_all(groups, shards, partial, flat, grads):
    top, mid = factors(shards)
    count = len(grads)
    vmem = pl.BlockSpec(memory_space=pltpu.VMEM)
    grads = [grad.reshape(top, mid, 2, grad.shape[0] // shards, grad.shape[1]) for grad in grads]
    shapes = [grad.shape[3:] for grad in grads]
    out = [
        jax.ShapeDtypeStruct(partial.shape, bf16),
        jax.ShapeDtypeStruct(flat.shape, f32),
    ] + [jax.ShapeDtypeStruct((groups,) + shape, bf16) for shape in shapes]
    most = max(2, mid, top, groups)
    stages = mid + top + groups - 2
    return pl.pallas_call(
        functools.partial(scatter_kernel, groups, top, mid, count),
        out_shape=out,
        in_specs=[vmem] * (2 + count),
        out_specs=[vmem] * (2 + count),
        scratch_shapes=[pltpu.VMEM((top, mid) + shape, bf16) for shape in shapes]
        + [pltpu.VMEM((max(1, mid - 1), top) + shape, bf16) for shape in shapes]
        + [pltpu.VMEM((top,) + shape, bf16) for shape in shapes]
        + [pltpu.VMEM((max(1, top - 1),) + shape, bf16) for shape in shapes]
        + [pltpu.VMEM((size,) + flat.shape, f32) for size in (2, mid, top, groups)]
        + [
            pltpu.SemaphoreType.DMA((count * CHUNKS, stages)),
            pltpu.SemaphoreType.DMA((count * CHUNKS, stages)),
            pltpu.SemaphoreType.DMA((4, most)),
            pltpu.SemaphoreType.DMA((4, most)),
            pltpu.SemaphoreType.DMA((2, groups)),
        ],
        compiler_params=pltpu.CompilerParams(
            collective_id=1, has_side_effects=True, vmem_limit_bytes=VMEM_LIMIT
        ),
    )(partial, flat, *grads)


def general(
    tokens,
    cotangent,
    documents,
    in_weight,
    kernel_taps,
    kernel_bias,
    step_bias,
    decay_log,
    skip_gain,
    pre_gain,
    norm_gain,
    out_weight,
):
    groups = lax.axis_size("seq")
    shards = lax.axis_size("fsdp")
    group = lax.axis_index("seq")
    heads = step_bias.shape[0]
    inner = norm_gain.shape[0]
    states = kernel_bias.shape[0] - inner
    half = inner // groups
    spread = out_weight.shape[0] % (HEAD_DIM * groups) == 0
    parts = shards if spread else 1

    def pick(array, axis):
        size = array.shape[axis]
        lead, tail = array.shape[:axis], array.shape[axis + 1 :]
        split = array.reshape(lead + (parts, groups, size // (parts * groups)) + tail)
        chosen = lax.dynamic_index_in_dim(split, group, axis + 1, keepdims=False)
        return chosen.reshape(lead + (size // groups,) + tail)

    def place(array):
        size = array.shape[-1] * groups
        lead = array.shape[:-1]
        split = array.reshape(lead + (parts, 1, size // (parts * groups)))
        blank = jnp.zeros(lead + (parts, groups, size // (parts * groups)), array.dtype)
        full = lax.dynamic_update_slice_in_dim(blank, split, group, len(lead) + 1)
        return full.reshape(lead + (size,))

    def unite(array):
        rows, width = array.shape[1:]
        split = array.reshape(groups, rows, parts, width // parts)
        return split.transpose(1, 2, 0, 3).reshape(rows, width * groups)

    conv_end = inner + inner + states
    conv_shard = jnp.concatenate(
        [
            pick(in_weight[:, inner : 2 * inner], 1),
            in_weight[:, 2 * inner : conv_end],
            pick(in_weight[:, conv_end:], 1),
        ],
        axis=1,
    )
    gate_shard = pick(in_weight[:, :inner], 1)
    out_rows = out_weight
    if spread:
        split = out_weight.reshape(groups, out_weight.shape[0] // groups, out_weight.shape[1])
        out_rows = lax.dynamic_index_in_dim(split, group, 0, keepdims=False)
    floats = tokens.astype(f32)
    normed_own = pre_norm(floats, pre_gain).astype(bf16)
    count, width = tokens.shape
    joined, conv_weight, gate_weight, out_part = gather_all(
        groups,
        shards,
        jnp.concatenate([normed_own, cotangent], axis=1),
        [conv_shard, gate_shard, out_rows],
    )
    joined = joined.reshape(groups * count, 2 * width)
    conv_weight = conv_weight.reshape(width, -1)
    gate_weight = gate_weight.reshape(width, -1)
    out_part = out_part.reshape(-1, width)
    if not spread:
        out_part = lax.dynamic_slice_in_dim(out_part, group * half, half, 0)
    normed_in, cot = joined[:, :width], joined[:, width:]

    projected = dot(normed_in, conv_weight).astype(bf16).astype(f32)
    segment = documents[0]
    taps = jnp.concatenate([pick(kernel_taps[:, :inner], 1), kernel_taps[:, inner:]], axis=1)
    tap_bias = jnp.concatenate([pick(kernel_bias[:inner], 0), kernel_bias[inner:]], axis=0)
    mixed, mixer_back = jax.vjp(
        lambda *given: mixer(segment, *given),
        projected[:, : half + states],
        projected[:, half + states :],
        taps,
        tap_bias,
        pick(step_bias, 0),
        pick(decay_log, 0),
        pick(skip_gain, 0),
    )
    gain = pick(norm_gain, 0)
    gates = dot(normed_in, gate_weight).astype(bf16).astype(f32)
    mixed = mixed.astype(bf16).astype(f32)
    back_normed = dot(cot, out_part, contract_rows)
    sigmoid = jax.nn.sigmoid(gates)
    silu = gates * sigmoid
    gated = mixed * silu
    back_gain = back_normed * gain
    sums = lax.psum(
        jnp.stack([jnp.sum(gated * gated, axis=1), jnp.sum(gated * back_gain, axis=1)]), "seq"
    )
    scale = lax.rsqrt(sums[0] / inner + norm_epsilon)
    unit = gated * scale[:, None]
    normed_bf = (unit * gain).astype(bf16)
    norm_gain_part = jnp.sum(back_normed * unit, axis=0)
    back_gated = scale[:, None] * (back_gain - unit * (scale * sums[1] / inner)[:, None])
    back_mixed = (back_gated * silu).astype(bf16).astype(f32)
    back_gates = (back_gated * mixed * sigmoid * (1.0 + gates * (1.0 - sigmoid))).astype(bf16)

    outward = dot(normed_bf, cot, contract_tokens).astype(bf16)
    gate_grad = dot(normed_in, back_gates, contract_tokens).astype(bf16)
    if not spread:
        blank = jnp.zeros((inner, width), bf16)
        outward = lax.dynamic_update_slice_in_dim(blank, outward, group * half, 0)
    branch = dot(normed_bf, out_part).astype(bf16)

    back_conv, back_steps, taps_part, bias_part, step_part, decay_part, skip_part = mixer_back(
        back_mixed
    )
    back_projected = jnp.concatenate([back_conv, back_steps], axis=1).astype(bf16)
    conv_grad = dot(normed_in, back_projected, contract_tokens).astype(bf16)
    back_in = dot(back_projected, conv_weight, contract_rows) + dot(
        back_gates, gate_weight, contract_rows
    )
    pre_gain_part = jnp.sum(back_in * normed_in.astype(f32), axis=0) / pre_gain

    pieces = (
        jnp.concatenate([place(taps_part[:, :half]), taps_part[:, half:]], axis=1),
        jnp.concatenate([place(bias_part[:half]), bias_part[half:]], axis=0),
        place(step_part),
        place(decay_part),
        place(skip_part),
        pre_gain_part,
        place(norm_gain_part),
    )
    flat = jnp.concatenate([piece.reshape(-1) for piece in pieces])
    padded = jnp.pad(flat, (0, -flat.size % 1024)).reshape(-1, 128)
    partial = jnp.concatenate(
        [
            back_in.astype(bf16).reshape(groups, count, width),
            branch.reshape(groups, count, width),
        ],
        axis=1,
    )
    partial, padded, conv_all, gate_all, out_all = scatter_all(
        groups, shards, partial, padded, [conv_grad, gate_grad, outward]
    )
    partial = jnp.sum(partial.astype(f32), axis=0)
    block_output = (floats + partial[count:]).astype(bf16)
    _, pre_back = jax.vjp(lambda given: pre_norm(given, pre_gain), floats)
    tokens_grad = cotangent.astype(f32) + pre_back(partial[:count])[0]
    conv_all, gate_all, out_all = (
        conv_all.astype(f32),
        gate_all.astype(f32),
        out_all.astype(f32),
    )
    if spread:
        outward_grad = out_all.reshape(-1, width)
    else:
        outward_grad = jnp.sum(out_all, axis=0)
    inward_grad = jnp.concatenate(
        [
            unite(gate_all),
            unite(conv_all[:, :, :half]),
            jnp.sum(conv_all[:, :, half : half + states], axis=0),
            unite(conv_all[:, :, half + states :]),
        ],
        axis=1,
    )
    flat = padded.reshape(-1)
    totals = []
    start = 0
    for piece in pieces:
        totals.append(flat[start : start + piece.size].reshape(piece.shape))
        start += piece.size
    return (
        block_output,
        tokens_grad,
        inward_grad,
        totals[0],
        totals[1],
        totals[2],
        totals[3],
        totals[4],
        totals[5],
        totals[6],
        outward_grad,
    )


LANES = 128
FAR = -1e30
exact = lax.Precision.HIGHEST


def sharp(left, right, dims=(((1,), (0,)), ((), ()))):
    return lax.dot_general(left, right, dims, precision=exact, preferred_element_type=f32)


def iota(shape, axis):
    return lax.broadcasted_iota(jnp.int32, shape, axis)


def span_of(index, size):
    return pl.ds(pl.multiple_of(index * size, size), size)


class Courier:
    def __init__(self, send):
        self.send = send
        self.count = 0
        self.made = []

    def start(self, source, target, receive, device, when=None):
        slot = self.count
        self.count += 1

        def make():
            return pltpu.make_async_remote_copy(
                src_ref=source(),
                dst_ref=target(),
                send_sem=self.send.at[slot],
                recv_sem=receive(),
                device_id=device(),
                device_id_type=MESH,
            )

        self.made.append((make, when))
        self.run(lambda: make().start(), when)

    def run(self, act, when):
        if when is None:
            act()
        else:
            pl.when(when)(act)

    def arrive(self, target, receive, device):
        pltpu.make_async_remote_copy(
            src_ref=target,
            dst_ref=target,
            send_sem=self.send.at[0],
            recv_sem=receive,
            device_id=device,
            device_id_type=MESH,
        ).wait_recv()

    def finish(self):
        for make, when in self.made:
            self.run(lambda make=make: make().wait_send(), when)


def fused_kernel(top, *refs):
    (
        tokens, cotangent, documents, in_weight, taps, tap_bias, params, pre_gain, norm_gain, out_weight,
        block_output, tokens_grad, in_grad, taps_grad, bias_grad, heads_grad, pre_grad, norm_grad, out_grad,
        nall, call, docs, conv_pack, gate_pack, conv_all, gate_all, out_all,
        proj, act, dact, mk, bias_mask, step, ldec, sgate, cum, cum_t, cum_b, step_e, skip_e, scaled,
        scores, decay, weigh, inside, mixed, gates, bnorm, gain_own, sums, sums_all, totals,
        normed_bf, bmixed, bgates, norm_part, part_b, part_i, dscore, x1, x2, dz, skip_part, bproj, pre_part,
        gr_out, gr_gate, gr_conv, y_out, y_gate, y_conv, line_out, line_gate, line_conv,
        low_out, low_gate, low_conv, high_out, high_gate, high_conv,
        own_out, own_gate, own_conv, flat, flat_y, flat_z, flat_all, got_b, got_i,
        send, r_rows, r_docs, r_conv, r_gate, r_out, r_sums, r_part,
        ry_out, ry_gate, ry_conv, rl_out, rl_gate, rl_conv, rh_out, rh_gate, rh_conv,
        ro_out, ro_gate, ro_conv, r_flat,
    ) = refs
    mid = 2
    me, t, m, c = position(top, mid)
    g = lax.axis_index("seq")
    count, width = tokens.shape
    length = documents.shape[1]
    seqs = 2
    total = seqs * length
    rows = in_weight.shape[0]
    inner = norm_gain.shape[1]
    quarter = inner // 4
    tiles = quarter // LANES
    states = taps.shape[1] - inner
    conv_tiles = tiles + states // LANES
    active = conv_tiles * LANES
    conv_cols = active + LANES
    heads = params_heads(inner)
    local_heads = heads // 4
    mail = Courier(send)

    def dev(tt, mm, cc):
        return lambda: {"fsdp": slot_of(tt, mm, cc, mid)}

    def dev_g(gg, tt, mm, cc):
        return lambda: {"seq": gg, "fsdp": slot_of(tt, mm, cc, mid)}

    here = {"fsdp": slot_of(t, m, 1 - c, mid)}
    group = [
        (2 * (1 - c) + g, dev_g(g, t, m, 1 - c)),
        (2 * c + 1 - g, dev_g(1 - g, t, m, c)),
        (2 * (1 - c) + 1 - g, dev_g(1 - g, t, m, 1 - c)),
    ]
    mine = 2 * c + g

    barrier = pltpu.get_barrier_semaphore()
    greeted = [d() for _, d in group]
    greeted += [{"fsdp": slot_of(t, 1 - m, cc, mid)} for cc in range(2)]
    greeted += [
        {"fsdp": slot_of(lax.rem(t + d, top), m, cc, mid)} for d in range(1, top) for cc in range(2)
    ]
    for peer in greeted:
        pl.semaphore_signal(barrier, inc=1, device_id=peer, device_id_type=MESH)

    def tile_of(n, cc):
        return 4 * n + 2 * cc + g

    def selector(cc):
        glob, loc = iota((LANES, LANES), 0), iota((LANES, LANES), 1)
        wanted = 8 * (loc // 2) + 4 * cc + 2 * g + loc % 2
        return jnp.where((glob == wanted) & (loc < local_heads), 1.0, 0.0)

    def pack(conv, gate, cc):
        for n in range(tiles):
            at = span_of(tile_of(n, cc) + inner // LANES, LANES)
            conv[:, n * LANES : (n + 1) * LANES] = in_weight[:, at]
        conv[:, quarter:active] = in_weight[:, 2 * inner : 2 * inner + states]
        picked = dot(in_weight[:, 2 * inner + states :], selector(cc)[:heads].astype(bf16))
        conv[:, active:] = picked.astype(bf16)

    def pack_gate(gate, cc):
        for n in range(tiles):
            gate[:, n * LANES : (n + 1) * LANES] = in_weight[:, span_of(tile_of(n, cc), LANES)]

    pack(conv_all.at[me], None, c)
    pack(conv_pack, None, 1 - c)
    pl.semaphore_wait(barrier, len(greeted))

    def spread(mine_ref, pack_ref, all_ref, receive):
        for src, cc in ((mine_ref, c), (lambda: pack_ref, 1 - c)):
            for up in (1, -1):
                ok = (t + 1 < top) if up == 1 else (t >= 1)
                mail.start(
                    src, lambda: all_ref.at[me], lambda: receive.at[me],
                    dev(t + up, m, cc), ok,
                )
            mail.start(
                src, lambda: all_ref.at[me], lambda: receive.at[me], dev(t, 1 - m, cc)
            )
        mail.start(lambda: pack_ref, lambda: all_ref.at[me], lambda: receive.at[me], dev(t, m, 1 - c))

    def relay(all_ref, receive, d):
        for up in (1, -1):
            ok = (t >= d) if up == 1 else (t + d < top)
            onward = ok & ((t + 1 < top) if up == 1 else (t >= 1))
            from_t = jnp.clip(t - up * d, 0, top - 1)
            for cc in range(2):
                slot = slot_of(from_t, m, cc, mid)
                mail.run(lambda slot=slot: mail.arrive(all_ref.at[slot], receive.at[slot], here), ok)
                block = lambda slot=slot: all_ref.at[slot]
                sem = lambda slot=slot: receive.at[slot]
                mail.start(block, block, sem, dev(t + up, m, c), onward)
                mail.start(block, block, sem, dev(t, 1 - m, c), ok)

    def settle(all_ref, receive):
        slot = slot_of(t, m, 1 - c, mid)
        mail.arrive(all_ref.at[slot], receive.at[slot], here)
        for tt in range(top):
            for cc in range(2):
                slot = slot_of(tt, 1 - m, cc, mid)
                mail.arrive(all_ref.at[slot], receive.at[slot], here)

    spread(lambda: conv_all.at[me], conv_pack, conv_all, r_conv)

    floats = tokens[...].astype(f32)
    nall[mine] = pre_norm(floats, pre_gain[...]).astype(bf16)
    for k, (_, device) in enumerate(group):
        mail.start(lambda: nall.at[mine], lambda: nall.at[mine], lambda: r_rows.at[0, mine], device)
    docs[c] = jnp.broadcast_to(documents[...].astype(f32), (8, length))
    mail.start(lambda: docs.at[c], lambda: docs.at[c], lambda: r_docs.at[0], dev(t, m, 1 - c))

    pack_gate(gate_all.at[me], c)
    pack_gate(gate_pack, 1 - c)
    relay(conv_all, r_conv, 1)
    spread(lambda: gate_all.at[me], gate_pack, gate_all, r_gate)

    holder = c == g
    keeper = c == m
    mail.run(lambda: out_all.__setitem__(t, out_weight[...]), holder & keeper)
    row_block = lambda: out_weight
    row_target = lambda: out_all.at[t]
    row_sem = lambda: r_out.at[t]
    mail.start(row_block, row_target, row_sem, dev(t + 1, m, m), holder & (t + 1 < top))
    mail.start(row_block, row_target, row_sem, dev(t - 1, m, m), holder & (t >= 1))
    mail.start(row_block, row_target, row_sem, dev(t, 1 - m, m), holder)
    mail.start(row_block, row_target, row_sem, dev(t, m, 1 - c), holder & (c != m))

    def relay_rows(d):
        for up in (1, -1):
            ok = keeper & ((t >= d) if up == 1 else (t + d < top))
            onward = ok & ((t + 1 < top) if up == 1 else (t >= 1))
            slot = jnp.clip(t - up * d, 0, top - 1)
            mail.run(lambda: mail.arrive(out_all.at[slot], r_out.at[slot], here), ok)
            block = lambda slot=slot: out_all.at[slot]
            sem = lambda slot=slot: r_out.at[slot]
            mail.start(block, block, sem, dev(t + up, m, c), onward)
            mail.start(block, block, sem, dev(t, 1 - m, c), ok)

    def settle_rows():
        mail.run(lambda: mail.arrive(out_all.at[t], r_out.at[t], here), keeper & (c != g))
        for tt in range(top):
            mail.run(lambda tt=tt: mail.arrive(out_all.at[tt], r_out.at[tt], here), c != m)

    call[mine] = cotangent[...]
    for k, (_, device) in enumerate(group):
        mail.start(lambda: call.at[mine], lambda: call.at[mine], lambda: r_rows.at[1, mine], device)

    for slot, _ in group:
        mail.arrive(nall.at[slot], r_rows.at[0, slot], here)
    mail.arrive(docs.at[1 - c], r_docs.at[0], here)

    @pl.loop(0, seqs)
    def _(s):
        row = docs[s][:1]
        column = jnp.broadcast_to(row, (LANES, length)).T
        wide = jnp.concatenate([column] * (length // LANES), axis=1)
        ahead = iota((length, length), 0) >= iota((length, length), 1)
        bias_mask[s] = jnp.where(ahead & (wide == row), 0.0, FAR)
        place = iota((length, LANES), 0)
        for k in range(1, CONV):
            same = (pltpu.roll(column, k, 0) == column) & (place >= k)
            mk[s, k - 1] = jnp.where(same, 1.0, 0.0)

    for n in range(tiles):
        gain_own[:, n * LANES : (n + 1) * LANES] = norm_gain[:, span_of(tile_of(n, c), LANES)]

    for d in range(2, top):
        relay(conv_all, r_conv, d)
    settle(conv_all, r_conv)

    def tall(ref):
        return ref[...].reshape(total, width)

    def weights(ref, cols):
        return ref[:, :, cols].reshape(width, cols.size)

    wide_cols = 256

    @pl.loop(0, conv_cols // wide_cols)
    def _(n):
        at = span_of(n, wide_cols)
        proj[:, at] = dot(tall(nall), weights(conv_all, at)).astype(bf16)

    if conv_cols % wide_cols:
        rest = pl.ds(conv_cols - LANES, LANES)
        proj[:, rest] = dot(tall(nall), weights(conv_all, rest)).astype(bf16)

    relay(gate_all, r_gate, 1)
    relay_rows(1)

    chosen = sharp(params[...], selector(c))
    rate = jnp.exp(chosen[1:2])
    raw = proj[:, active:].astype(f32) + chosen[:1]
    step[...] = jnp.maximum(raw, 0.0) + jnp.log1p(jnp.exp(-jnp.abs(raw)))
    sgate[...] = jax.nn.sigmoid(raw)
    ldec[...] = step[...] * -rate
    to_channels = jnp.where(iota((LANES, quarter), 1) // HEAD_DIM == iota((LANES, quarter), 0), 1.0, 0.0)
    to_heads = jnp.where(iota((quarter, LANES), 0) // HEAD_DIM == iota((quarter, LANES), 1), 1.0, 0.0)
    step_e[...] = sharp(step[...], to_channels)
    skip_e[...] = sharp(chosen, to_channels)
    lower = jnp.where(iota((length, length), 0) >= iota((length, length), 1), 1.0, 0.0)
    for s in range(seqs):
        at = slice(s * length, (s + 1) * length)
        cum[at] = sharp(lower, ldec[at])
        cum_t[s] = cum[at].T
    for h in range(local_heads):
        cum_b[h] = jnp.broadcast_to(cum[:, h : h + 1], (total, LANES))

    def conv_tile(n):
        return jnp.where(n < tiles, tile_of(n, c), n - tiles + inner // LANES)

    @pl.loop(0, seqs * conv_tiles)
    def _(i):
        s, n = i // conv_tiles, i % conv_tiles
        at, cols = span_of(s, length), span_of(n, LANES)
        where = span_of(conv_tile(n), LANES)
        x = proj[at, cols].astype(f32)
        tap = taps[:, where]
        z = tap_bias[:, where] + x * tap[CONV - 1 : CONV]
        for k in range(1, CONV):
            z = z + tap[CONV - 1 - k : CONV - k] * (pltpu.roll(x, k, 0) * mk[s, k - 1])
        sig = jax.nn.sigmoid(z)
        act[at, cols] = z * sig
        dact[at, cols] = sig * (1.0 + z * (1.0 - sig))

    relay(gate_all, r_gate, 2)
    relay_rows(2)

    def matrices(s):
        at = span_of(s, length)
        return (
            act[at, quarter : quarter + STATE].astype(bf16),
            act[at, quarter + STATE : active].astype(bf16),
        )

    @pl.loop(0, seqs)
    def _(s):
        b_in, c_out = matrices(s)
        scores[s] = dot(c_out, b_in, contract_rows)

    half_of = lambda: iota((length, LANES), 1) // HEAD_DIM

    @pl.loop(0, seqs * tiles)
    def _(i):
        s, n = i // tiles, i % tiles
        at, cols = span_of(s, length), span_of(n, LANES)
        vals = act[at, cols]
        sc = (vals * step_e[at, cols]).astype(bf16)
        scaled[at, cols] = sc
        y = jnp.zeros((length, LANES), f32)
        for b in range(2):
            h = 2 * n + b
            col = cum_b[h, at]
            gap = jnp.concatenate([col] * (length // LANES), axis=1) - cum_t[s, pl.ds(h, 1)]
            d = jnp.exp(gap + bias_mask[s])
            decay[s * local_heads + h] = d
            w = (d * scores[s]).astype(bf16)
            weigh[s * local_heads + h] = w
            y = y + dot(w, jnp.where(half_of() == b, sc, jnp.zeros_like(sc)))
        inside[at, cols] = y
        mixed[at, cols] = (y + vals * skip_e[2:3, cols]).astype(bf16)

    for d in range(3, top):
        relay(gate_all, r_gate, d)
        relay_rows(d)
    settle(gate_all, r_gate)

    @pl.loop(0, quarter // wide_cols)
    def _(n):
        at = span_of(n, wide_cols)
        gates[:, at] = dot(tall(nall), weights(gate_all, at)).astype(bf16)

    settle_rows()
    for slot, _ in group:
        mail.arrive(call.at[slot], r_rows.at[1, slot], here)

    @pl.loop(0, tiles // 2)
    def _(n):
        w = out_all[pl.ds(2 * n, 2)].reshape(2 * LANES, width)
        bnorm[:, span_of(n, 2 * LANES)] = dot(tall(call), w, contract_rows)

    strip = 64

    @pl.loop(0, total // strip)
    def _(i):
        at = span_of(i, strip)
        gate = gates[at].astype(f32)
        gated = mixed[at].astype(f32) * (gate * jax.nn.sigmoid(gate))
        first = jnp.sum(gated * gated, axis=1, keepdims=True)
        second = jnp.sum(gated * (bnorm[at] * gain_own[...]), axis=1, keepdims=True)
        lane = iota((strip, LANES), 1)
        sums[at] = jnp.where(lane == 0, first, jnp.where(lane == 1, second, 0.0))

    sums_all[mine] = sums[...].T[:8]
    for k, (_, device) in enumerate(group):
        mail.start(lambda: sums_all.at[mine], lambda: sums_all.at[mine], lambda: r_sums.at[mine], device)
    for slot, _ in group:
        mail.arrive(sums_all.at[slot], r_sums.at[slot], here)
    summed = (sums_all[0] + sums_all[1]) + (sums_all[2] + sums_all[3])
    totals[...] = jnp.concatenate([summed, jnp.zeros((LANES - 8, total), f32)], axis=0).T

    norm_part[...] = jnp.zeros_like(norm_part)

    @pl.loop(0, total // strip)
    def _(i):
        at = span_of(i, strip)
        gate = gates[at].astype(f32)
        mix = mixed[at].astype(f32)
        sig = jax.nn.sigmoid(gate)
        silu = gate * sig
        gated = mix * silu
        gain = gain_own[...]
        scale = lax.rsqrt(totals[at, 0:1] / inner + norm_epsilon)
        unit = gated * scale
        back = bnorm[at]
        normed_bf[at] = (unit * gain).astype(bf16)
        norm_part[...] += jnp.sum(back * unit, axis=0, keepdims=True)
        back_gated = scale * (back * gain - unit * (scale * totals[at, 1:2] / inner))
        bmixed[at] = (back_gated * silu).astype(bf16)
        bgates[at] = (back_gated * mix * sig * (1.0 + gate * (1.0 - sig))).astype(bf16)

    def tall_cols(ref, at):
        return ref[:, :, at].reshape(total, at.size)

    order = []
    for k in range(top // 2):
        order += [top - 1 - k, k]

    for tt in order:
        cols = slice(tt * LANES, (tt + 1) * LANES)
        gr_out[tt] = dot(normed_bf[:, cols], tall(call), contract_tokens).astype(bf16)
        mail.start(
            lambda tt=tt: gr_out.at[tt], lambda tt=tt: y_out.at[tt], lambda tt=tt: ry_out.at[tt],
            dev(t, 1 - m, c), c != m,
        )

    block = width // top
    for tt in order:
        got = dot(tall_cols(nall, pl.ds(tt * block, block)), bgates[...], contract_tokens).astype(bf16)
        gr_gate[tt] = got.reshape(gr_gate.shape[1:])
        mail.start(
            lambda tt=tt: gr_gate.at[tt, 1 - m], lambda tt=tt: y_gate.at[tt], lambda tt=tt: ry_gate.at[tt],
            dev(t, 1 - m, c),
        )

    @pl.loop(0, width // wide_cols)
    def _(n):
        at = span_of(n, wide_cols)
        w = out_all[:, :, at].reshape(quarter, wide_cols)
        part_b[:, :, at] = dot(normed_bf[...], w).astype(bf16).reshape(4, count, wide_cols)

    for slot, device in group:
        mail.start(
            lambda slot=slot: part_b.at[slot], lambda: got_b.at[mine], lambda: r_part.at[0, mine], device
        )

    skip_part[...] = jnp.zeros_like(skip_part)
    dscore[...] = jnp.zeros_like(dscore)

    @pl.loop(0, seqs * tiles)
    def _(i):
        s, n = i // tiles, i % tiles
        at, cols = span_of(s, length), span_of(n, LANES)
        back = bmixed[at, cols]
        sc = scaled[at, cols]
        ds = jnp.zeros((length, LANES), f32)
        gather = dscore[s]
        for b in range(2):
            h = s * local_heads + 2 * n + b
            one = jnp.where(half_of() == b, back, jnp.zeros_like(back))
            gather = gather + decay[h] * dot(one, sc, contract_rows)
            ds = ds + dot(weigh[h], one, contract_tokens)
        dscore[s] = gather
        back = back.astype(f32)
        vals = act[at, cols]
        x1[at, cols] = back * inside[at, cols] - sc.astype(f32) * ds
        x2[at, cols] = ds * vals
        dz[at, cols] = (back * skip_e[2:3, cols] + ds * step_e[at, cols]) * dact[at, cols]
        skip_part[:, cols] += jnp.sum(back * vals, axis=0, keepdims=True)

    @pl.loop(0, seqs)
    def _(s):
        at = span_of(s, length)
        b_in, c_out = matrices(s)
        ds = dscore[s].astype(bf16)
        b_cols, c_cols = slice(quarter, quarter + STATE), slice(quarter + STATE, active)
        dz[at, b_cols] = dot(ds, c_out, contract_tokens) * dact[at, b_cols]
        dz[at, c_cols] = dot(ds, b_in) * dact[at, c_cols]

    back_cum = sharp(x1[...], to_heads)
    back_step = sharp(x2[...], to_heads)
    upper = jnp.where(iota((length, length), 0) <= iota((length, length), 1), 1.0, 0.0)
    back_decay = jnp.concatenate(
        [sharp(upper, back_cum[s * length : (s + 1) * length]) for s in range(seqs)], axis=0
    )
    back_raw = (back_step - back_decay * rate) * sgate[...]
    bproj[:, active:] = back_raw.astype(bf16)
    flat[conv_tiles] = jnp.concatenate(
        [norm_part[:1, n * LANES : (n + 1) * LANES] for n in range(tiles)]
        + [
            jnp.sum(back_raw, axis=0, keepdims=True),
            jnp.sum(back_decay * ldec[...], axis=0, keepdims=True),
            sharp(skip_part[...], to_heads)[:1],
            jnp.zeros((8 - tiles - 3, LANES), f32),
        ],
        axis=0,
    )

    @pl.loop(0, conv_tiles)
    def _(n):
        cols, where = span_of(n, LANES), span_of(conv_tile(n), LANES)
        tap = taps[:, where]
        grads = [jnp.zeros((1, LANES), f32) for _ in range(CONV + 1)]
        for s in range(seqs):
            at = slice(s * length, (s + 1) * length)
            x = proj[at, cols].astype(f32)
            back = dz[at, cols]
            dx = back * tap[CONV - 1 : CONV]
            grads[CONV] += jnp.sum(back, axis=0, keepdims=True)
            grads[CONV - 1] += jnp.sum(back * x, axis=0, keepdims=True)
            for k in range(1, CONV):
                kept = back * mk[s, k - 1]
                dx = dx + tap[CONV - 1 - k : CONV - k] * pltpu.roll(kept, length - k, 0)
                grads[CONV - 1 - k] += jnp.sum(kept * pltpu.roll(x, k, 0), axis=0, keepdims=True)
            bproj[at, cols] = dx.astype(bf16)
        flat[n] = jnp.concatenate(grads + [jnp.zeros((8 - CONV - 1, LANES), f32)], axis=0)

    for tt in order:
        got = dot(tall_cols(nall, pl.ds(tt * block, block)), bproj[...], contract_tokens).astype(bf16)
        gr_conv[tt] = got.reshape(gr_conv.shape[1:])
        mail.start(
            lambda tt=tt: gr_conv.at[tt, 1 - m], lambda tt=tt: y_conv.at[tt], lambda tt=tt: ry_conv.at[tt],
            dev(t, 1 - m, c),
        )

    def add_blocks(target, left, right):
        *lead, tall_rows, cols = target.shape
        piece = 32
        for at in [()] if not lead else [(i,) for i in range(lead[0])]:

            @pl.loop(0, tall_rows // piece)
            def _(i, at=at):
                where = at + (span_of(i, piece),)
                target[where] = add(left[where], right[where])

    def reduce_line(own, y_got, y_sem, line, low, low_sem, high, high_sem, ok=None):
        def both(a, b):
            return b if a is None else a & b

        def pair(tt):
            def act_():
                mail.arrive(y_got.at[tt], y_sem.at[tt], here)
                add_blocks(line.at[tt], own(tt), y_got.at[tt])

            mail.run(act_, ok)

        for tt in order:
            pair(tt)
            up = tt >= top // 2
            for direction in ((1, -1) if up else (-1, 1)):
                if direction == 1 and tt > 0:
                    inward = both(ok, (t < tt) & (t > 0))

                    def take(tt=tt):
                        mail.arrive(low.at[tt], low_sem.at[tt], here)
                        add_blocks(line.at[tt], line.at[tt], low.at[tt])

                    mail.run(take, inward)
                    mail.start(
                        lambda tt=tt: line.at[tt], lambda tt=tt: low.at[tt], lambda tt=tt: low_sem.at[tt],
                        dev(t + 1, m, c), both(ok, t < tt),
                    )
                if direction == -1 and tt < top - 1:
                    inward = both(ok, (t > tt) & (t < top - 1))

                    def take(tt=tt):
                        mail.arrive(high.at[tt], high_sem.at[tt], here)
                        add_blocks(line.at[tt], line.at[tt], high.at[tt])

                    mail.run(take, inward)
                    mail.start(
                        lambda tt=tt: line.at[tt], lambda tt=tt: high.at[tt], lambda tt=tt: high_sem.at[tt],
                        dev(t - 1, m, c), both(ok, t > tt),
                    )

        def last_low():
            mail.arrive(low.at[t], low_sem.at[t], here)
            add_blocks(line.at[t], line.at[t], low.at[t])

        def last_high():
            mail.arrive(high.at[t], high_sem.at[t], here)
            add_blocks(line.at[t], line.at[t], high.at[t])

        mail.run(last_low, both(ok, t > 0))
        mail.run(last_high, both(ok, t < top - 1))

    def hand_over(line, own, receive):
        own[g, c] = line[t, c]
        for gg, cc in ((g, 1 - c), (1 - g, c), (1 - g, 1 - c)):
            mail.start(
                lambda cc=cc: line.at[t, cc], lambda: own.at[g, c], lambda: receive.at[g, c],
                dev_g(gg, t, m, cc),
            )

    def take_over(own, receive):
        for gg, cc in ((g, 1 - c), (1 - g, c), (1 - g, 1 - c)):
            mail.arrive(own.at[gg, cc], receive.at[gg, cc], here)

    reduce_line(
        lambda tt: gr_out.at[tt], y_out, ry_out, line_out, low_out, rl_out, high_out, rh_out, keeper
    )
    mail.run(lambda: own_out.__setitem__(Ellipsis, line_out[t]), keeper & holder)
    mail.start(
        lambda: line_out.at[t], lambda: own_out, lambda: ro_out.at[0], dev_g(g, t, m, 1 - c),
        keeper & (c != g),
    )
    mail.start(
        lambda: line_out.at[t], lambda: own_out, lambda: ro_out.at[0], dev_g(1 - g, t, m, g), keeper
    )
    reduce_line(
        lambda tt: gr_gate.at[tt, m], y_gate, ry_gate, line_gate, low_gate, rl_gate, high_gate, rh_gate
    )
    hand_over(line_gate, own_gate, ro_gate)

    @pl.loop(0, width // wide_cols)
    def _(n):
        at = span_of(n, wide_cols)
        slots = pl.ds(n * (wide_cols // rows), wide_cols // rows)
        value = dot(bproj[...], conv_all[slots].reshape(wide_cols, conv_cols), contract_rows)
        value = value + dot(bgates[...], gate_all[slots].reshape(wide_cols, quarter), contract_rows)
        part_i[:, :, at] = value.astype(bf16).reshape(4, count, wide_cols)
        seen = tall_cols(nall, at).astype(f32)
        pre_part[:, at] = jnp.broadcast_to(
            jnp.sum(value * seen, axis=0, keepdims=True) / pre_gain[:, at], (8, wide_cols)
        )

    for slot, device in group:
        mail.start(
            lambda slot=slot: part_i.at[slot], lambda: got_i.at[mine], lambda: r_part.at[1, mine], device
        )
    flat[conv_tiles + 1] = jnp.concatenate(
        [pre_part[:1, n * LANES : (n + 1) * LANES] for n in range(width // LANES)], axis=0
    )
    mail.start(lambda: flat, lambda: flat_y, lambda: r_flat.at[0, 0], dev(t, 1 - m, c))

    reduce_line(
        lambda tt: gr_conv.at[tt, m], y_conv, ry_conv, line_conv, low_conv, rl_conv, high_conv, rh_conv
    )
    hand_over(line_conv, own_conv, ro_conv)

    mail.arrive(flat_y, r_flat.at[0, 0], here)
    flat_z[t] = flat[...] + flat_y[...]
    for d in range(1, top):
        mail.start(
            lambda: flat_z.at[t], lambda: flat_z.at[t], lambda: r_flat.at[1, t],
            dev(lax.rem(t + d, top), m, c),
        )

    got_b[mine] = part_b[mine]
    got_i[mine] = part_i[mine]
    for k in range(2):
        for slot, _ in group:
            mail.arrive((got_b, got_i)[k].at[slot], r_part.at[k, slot], here)

    @pl.loop(0, count // 16)
    def _(i):
        at = span_of(i, 16)
        x = tokens[at].astype(f32)
        branch = sum(got_b[q, at].astype(f32) for q in range(4))
        back = sum(got_i[q, at].astype(f32) for q in range(4)) * pre_gain[...]
        block_output[at] = (x + branch).astype(bf16)
        scale = lax.rsqrt(jnp.mean(x * x, axis=1, keepdims=True) + norm_epsilon)
        shared = jnp.mean(x * back, axis=1, keepdims=True) * (scale * scale * scale)
        tokens_grad[at] = cotangent[at].astype(f32) + back * scale - x * shared

    for d in range(1, top):
        slot = lax.rem(t - d + top, top)
        mail.arrive(flat_z.at[slot], r_flat.at[1, slot], here)
    value = flat_z[0]
    for k in range(1, top):
        value = value + flat_z[k]
    flat_all[mine] = value
    for slot, device in group:
        mail.start(lambda: flat_all.at[mine], lambda: flat_all.at[mine], lambda: r_flat.at[2, mine], device)

    mail.run(lambda: mail.arrive(own_out, ro_out.at[0], here), jnp.logical_not(holder & keeper))
    out_grad[...] = own_out[...].astype(f32)

    def put_tiles(base, own, first, number):
        for gg in range(2):
            for cc in range(2):
                for n in range(number):
                    j = base + 4 * n + 2 * cc + gg
                    in_grad[:, j * LANES : (j + 1) * LANES] = own[
                        gg, cc, :, n * LANES : (n + 1) * LANES
                    ].astype(f32)

    take_over(own_gate, ro_gate)
    put_tiles(0, own_gate, 0, tiles)

    for slot, _ in group:
        mail.arrive(flat_all.at[slot], r_flat.at[2, slot], here)
    parts = [(gg, cc, flat_all.at[2 * cc + gg]) for gg in range(2) for cc in range(2)]

    def selector_of(gg, cc):
        loc, glob = iota((LANES, LANES), 0), iota((LANES, LANES), 1)
        wanted = 8 * (loc // 2) + 4 * cc + 2 * gg + loc % 2
        return jnp.where((glob == wanted) & (loc < local_heads), 1.0, 0.0)

    for gg, cc, part in parts:
        for n in range(tiles):
            j = 4 * n + 2 * cc + gg
            at = slice(j * LANES, (j + 1) * LANES)
            taps_grad[:, at] = part[n, :CONV]
            bias_grad[:, at] = part[n, CONV : CONV + 1]
            norm_grad[:, at] = part[conv_tiles, n : n + 1]
    for n in range(tiles, conv_tiles):
        j = n - tiles + inner // LANES
        at = slice(j * LANES, (j + 1) * LANES)
        value = sum(part[n] for _, _, part in parts)
        taps_grad[:, at] = value[:CONV]
        bias_grad[:, at] = value[CONV : CONV + 1]
    heads_grad[...] = sum(
        sharp(part[conv_tiles], selector_of(gg, cc)) for gg, cc, part in parts
    )
    value = sum(part[conv_tiles + 1] for _, _, part in parts)
    for n in range(width // LANES):
        pre_grad[:, n * LANES : (n + 1) * LANES] = value[n : n + 1]

    take_over(own_conv, ro_conv)
    put_tiles(inner // LANES, own_conv, 0, tiles)
    shared = sum(own_conv[gg, cc, :, quarter:active].astype(f32) for gg, cc, _ in parts)
    in_grad[:, 2 * inner : 2 * inner + states] = shared
    ends = sum(dot(own_conv[gg, cc, :, active:], selector_of(gg, cc).astype(bf16)) for gg, cc, _ in parts)
    in_grad[:, 2 * inner + states :] = ends[:, :heads]
    mail.finish()


def params_heads(inner):
    return inner // HEAD_DIM


def fused(
    tokens, cotangent, documents, in_weight, kernel_taps, kernel_bias, step_bias, decay_log, skip_gain,
    pre_gain, norm_gain, out_weight,
):
    shards = lax.axis_size("fsdp")
    top, mid = factors(shards)
    count, width = tokens.shape
    length = documents.shape[1]
    total = 2 * length
    rows, columns = in_weight.shape
    inner = norm_gain.shape[0]
    channels = kernel_bias.shape[0]
    quarter = inner // 4
    tiles = quarter // LANES
    conv_tiles = tiles + (channels - inner) // LANES
    conv_cols = (conv_tiles + 1) * LANES
    active = conv_tiles * LANES
    heads = step_bias.shape[0]
    local_heads = heads // 4
    own_rows = out_weight.shape[0]
    params = jnp.pad(jnp.stack([step_bias, decay_log, skip_gain]), ((0, 5), (0, LANES - heads)))
    vmem = pl.BlockSpec(memory_space=pltpu.VMEM)
    V = pltpu.VMEM
    dma = pltpu.SemaphoreType.DMA
    shape = jax.ShapeDtypeStruct
    outs = [
        shape((count, width), bf16), shape((count, width), f32), shape((rows, columns), f32),
        shape((CONV, channels), f32), shape((1, channels), f32), shape((8, LANES), f32),
        shape((1, width), f32), shape((1, inner), f32), shape((own_rows, width), f32),
    ]
    line_shapes = [(own_rows, width), (2, rows, quarter), (2, rows, conv_cols)]
    scratch = [
        V((4, count, width), bf16), V((4, count, width), bf16), V((2, 8, length), f32),
        V((rows, conv_cols), bf16), V((rows, quarter), bf16),
        V((shards, rows, conv_cols), bf16), V((shards, rows, quarter), bf16), V((top, own_rows, width), bf16),
        V((total, conv_cols), bf16), V((total, active), f32), V((total, active), f32),
        V((2, CONV - 1, length, LANES), f32), V((2, length, length), f32),
        V((total, LANES), f32), V((total, LANES), f32), V((total, LANES), f32),
        V((total, LANES), f32), V((2, LANES, length), f32), V((local_heads, total, LANES), f32),
        V((total, quarter), f32), V((8, quarter), f32), V((total, quarter), bf16),
        V((2, length, length), f32), V((2 * local_heads, length, length), f32),
        V((2 * local_heads, length, length), bf16), V((total, quarter), f32), V((total, quarter), bf16),
        V((total, quarter), bf16), V((total, quarter), f32), V((1, quarter), f32),
        V((total, LANES), f32), V((4, 8, total), f32), V((total, LANES), f32),
        V((total, quarter), bf16), V((total, quarter), bf16), V((total, quarter), bf16),
        V((8, quarter), f32), V((4, count, width), bf16), V((4, count, width), bf16),
        V((2, length, length), f32), V((total, quarter), f32), V((total, quarter), f32),
        V((total, active), f32), V((8, quarter), f32), V((total, conv_cols), bf16), V((8, width), f32),
        V((top, own_rows, width), bf16), V((top, 2, 2, rows, quarter), bf16),
        V((top, 2, 2, rows, conv_cols), bf16),
    ]
    for _ in range(4):
        scratch += [V((top,) + item, bf16) for item in line_shapes]
    flat_shape = (conv_tiles + 2, 8, LANES)
    scratch += [
        V((own_rows, width), bf16), V((2, 2, rows, quarter), bf16), V((2, 2, rows, conv_cols), bf16),
        V(flat_shape, f32), V(flat_shape, f32), V((top,) + flat_shape, f32), V((4,) + flat_shape, f32),
        V((4, count, width), bf16), V((4, count, width), bf16),
        dma((400,)), dma((2, 4)), dma((1,)), dma((shards,)), dma((shards,)), dma((top,)), dma((4,)),
        dma((2, 4)),
    ]
    scratch += [dma((top,)) for _ in range(9)]
    scratch += [dma((1,)), dma((2, 2)), dma((2, 2)), dma((3, max(4, top)))]
    results = pl.pallas_call(
        functools.partial(fused_kernel, top),
        out_shape=outs,
        in_specs=[vmem] * 10,
        out_specs=[vmem] * len(outs),
        scratch_shapes=scratch,
        compiler_params=pltpu.CompilerParams(
            collective_id=2, has_side_effects=True, vmem_limit_bytes=VMEM_LIMIT
        ),
    )(
        tokens, cotangent, documents, in_weight, kernel_taps, kernel_bias.reshape(1, -1), params,
        pre_gain.reshape(1, -1), norm_gain.reshape(1, -1), out_weight,
    )
    block_output, tokens_grad, in_grad, taps_grad, bias_grad, heads_grad, pre_grad, norm_grad, out_grad = results
    return (
        block_output, tokens_grad, in_grad, taps_grad, bias_grad.reshape(-1),
        heads_grad[4, :heads], heads_grad[5, :heads], heads_grad[6, :heads],
        pre_grad.reshape(-1), norm_grad.reshape(-1), out_grad,
    )


def fits(tokens, documents, in_weight, norm_gain, out_weight):
    groups, shards = lax.axis_size("seq"), lax.axis_size("fsdp")
    top, mid = factors(shards)
    length, inner = documents.shape[1], norm_gain.shape[0]
    heads = inner // HEAD_DIM
    return (
        groups == 2 and mid == 2 and top % 2 == 0 and length == min(SPAN, length)
        and tokens.shape[0] * groups == length and length % LANES == 0
        and out_weight.shape[0] == LANES and inner == shards * LANES
        and inner // 4 == top * LANES and heads % 32 == 0 and heads <= LANES
        and in_weight.shape[0] * shards == tokens.shape[1]
    )


def local(*arrays):
    tokens, _, documents, in_weight = arrays[:4]
    if fits(tokens, documents, in_weight, arrays[10], arrays[11]):
        return fused(*arrays)
    return general(*arrays)


def solution(mesh):
    rows = P(("fsdp", "seq"), None)
    split = P("fsdp", None)
    return jax.shard_map(
        local,
        mesh=mesh,
        in_specs=(rows, rows, split, split) + (P(),) * 7 + (split,),
        out_specs=(rows, rows, split) + (P(),) * 7 + (split,),
        check_vma=False,
    )
```

```python
import functools
import math

import jax
import jax.numpy as jnp
from jax import lax
from jax.experimental import pallas as pl
from jax.experimental.pallas import tpu as pltpu
from jax.sharding import PartitionSpec as P

HEAD_DIM = 64
STATE = 128
CONV = 4
SPAN = 256

norm_epsilon = 1e-05
bf16 = jnp.bfloat16
f32 = jnp.float32
contract_rows = (((1,), (1,)), ((), ()))
contract_tokens = (((0,), (0,)), ((), ()))


def dot(left, right, dims=(((1,), (0,)), ((), ()))):
    return lax.dot_general(left, right, dims, preferred_element_type=f32)


def pre_norm(values, gain):
    scale = lax.rsqrt(jnp.mean(values * values, axis=-1, keepdims=True) + norm_epsilon)
    return values * scale * gain


def product(spec, left, right):
    return jnp.einsum(spec, left.astype(bf16), right.astype(bf16), preferred_element_type=f32)


def mixer(segment, conv_in, step_raw, taps, tap_bias, bias_steps, log_rates, skips):
    length, channels = conv_in.shape
    heads = step_raw.shape[1]
    width = heads * HEAD_DIM
    summed = tap_bias + conv_in * taps[CONV - 1]
    for offset in range(1, CONV):
        shifted = jnp.concatenate(
            [jnp.zeros((offset, channels), f32), conv_in[: length - offset]], axis=0
        )
        matched = jnp.concatenate(
            [
                jnp.zeros((offset,), f32),
                (segment[offset:] == segment[: length - offset]).astype(f32),
            ]
        )
        summed = summed + taps[CONV - 1 - offset] * shifted * matched[:, None]
    active = jax.nn.silu(summed)
    values = active[:, :width].reshape(length, heads, HEAD_DIM).transpose(1, 0, 2)
    input_matrix = active[:, width : width + STATE]
    output_matrix = active[:, width + STATE :]
    steps_taken = jax.nn.softplus(step_raw + bias_steps)
    log_decay = (steps_taken * -jnp.exp(log_rates)).T
    scaled = values * steps_taken.T[:, :, None]
    span = min(SPAN, length)
    blocks = length // span
    places = jnp.arange(span)
    state = None
    outputs = []
    for block in range(blocks):
        at = slice(block * span, (block + 1) * span)
        seg = segment[at]
        cumul = jnp.cumsum(log_decay[:, at], axis=1)
        causal = (places[:, None] >= places[None, :]) & (seg[:, None] == seg[None, :])
        log_gap = cumul[:, :, None] - cumul[:, None, :]
        decay = jnp.where(causal[None], jnp.exp(jnp.where(causal[None], log_gap, 0.0)), 0.0)
        scores = product("in,jn->ij", output_matrix[at], input_matrix[at])
        inside = product("hij,hjp->hip", decay * scores[None], scaled[:, at])
        if state is not None:
            previous = segment[block * span - 1]
            entering = jnp.exp(cumul) * (seg == previous).astype(f32)[None]
            inside = inside + product("in,hnp->hip", output_matrix[at], state) * entering[:, :, None]
        if block + 1 < blocks:
            final = cumul[:, -1]
            leaving = jnp.exp(final[:, None] - cumul) * (seg == seg[-1]).astype(f32)[None]
            fresh = product("jn,hjp->hnp", input_matrix[at], scaled[:, at] * leaving[:, :, None])
            if state is None:
                state = fresh
            else:
                keeping = jnp.exp(final) * (seg[-1] == previous).astype(f32)
                state = keeping[:, None, None] * state + fresh
        outputs.append(inside)
    whole = outputs[0] if blocks == 1 else jnp.concatenate(outputs, axis=1)
    result = whole + values * skips[:, None, None]
    return result.transpose(1, 0, 2).reshape(length, width)

MESH = pl.DeviceIdType.MESH
VMEM_LIMIT = 60 * 1024 * 1024


def factors(shards):
    rest = shards // 2
    mid = 1 << (int(math.log2(rest)) // 2)
    return rest // mid, mid


def position(top, mid):
    me = lax.axis_index("fsdp")
    return me, me // (2 * mid), lax.rem(me // 2, mid), lax.rem(me, 2)


def slot_of(t, m, core, mid):
    return (t * mid + m) * 2 + core


def greet(groups, top, mid):
    me, t, m, core = position(top, mid)
    group = lax.axis_index("seq")
    peers = [{"fsdp": slot_of(lax.rem(t + d, top), m, core, mid)} for d in range(1, top)]
    peers += [{"fsdp": slot_of(t, lax.rem(m + e, mid), core, mid)} for e in range(1, mid)]
    peers += [{"fsdp": slot_of(t, m, 1 - core, mid)}]
    peers += [{"seq": lax.rem(group + k, groups)} for k in range(1, groups)]
    barrier = pltpu.get_barrier_semaphore()
    for peer in peers:
        pl.semaphore_signal(barrier, inc=1, device_id=peer, device_id_type=MESH)
    pl.semaphore_wait(barrier, len(peers))


def remote(source, target, send, receive, device):
    copy = pltpu.make_async_remote_copy(
        src_ref=source,
        dst_ref=target,
        send_sem=send,
        recv_sem=receive,
        device_id=device,
        device_id_type=MESH,
    )
    copy.start()
    return copy


def gather_kernel(groups, top, mid, count, *refs):
    rows, shards = refs[0], refs[1 : 1 + count]
    all_rows, wholes = refs[1 + count], refs[2 + count : 2 + 2 * count]
    send, receive, row_send, row_receive = refs[2 + 2 * count :]
    me, t, m, core = position(top, mid)
    group = lax.axis_index("seq")
    greet(groups, top, mid)
    copies = {}

    def launch(a, key, source, slot, device):
        copies[(a,) + key] = remote(
            source, wholes[a].at[slot], send.at[(a,) + key], receive.at[(a,) + key], device
        )

    other = {"fsdp": slot_of(t, m, 1 - core, mid)}
    for a in range(count):
        for d in range(1, top):
            peer = {"fsdp": slot_of(lax.rem(t + d, top), m, core, mid)}
            launch(a, (d, 0, 0), shards[a], me, peer)
        for e in range(1, mid):
            peer = {"fsdp": slot_of(t, lax.rem(m + e, mid), core, mid)}
            launch(a, (0, e, 0), shards[a], me, peer)
        launch(a, (0, 0, 1), shards[a], me, other)
    for k in range(1, groups):
        copies[("rows", k)] = remote(
            rows,
            all_rows.at[group],
            row_send.at[k],
            row_receive.at[k],
            {"seq": lax.rem(group + k, groups)},
        )
    for a in range(count):
        wholes[a][me] = shards[a][...]
    all_rows[group] = rows[...]
    for a in range(count):
        for d in range(1, top):
            copies[(a, d, 0, 0)].wait_recv()
            slot = slot_of(lax.rem(t - d + top, top), m, core, mid)
            for e in range(1, mid):
                peer = {"fsdp": slot_of(t, lax.rem(m + e, mid), core, mid)}
                launch(a, (d, e, 0), wholes[a].at[slot], slot, peer)
            launch(a, (d, 0, 1), wholes[a].at[slot], slot, other)
    for a in range(count):
        for d in range(top):
            for e in range(1, mid):
                copies[(a, d, e, 0)].wait_recv()
                slot = slot_of(lax.rem(t - d + top, top), lax.rem(m - e + mid, mid), core, mid)
                launch(a, (d, e, 1), wholes[a].at[slot], slot, other)
    for key, copy in copies.items():
        copy.wait_send()
        if key[0] == "rows" or key[3] == 1:
            copy.wait_recv()


def gather_all(groups, shards, rows, arrays):
    top, mid = factors(shards)
    count = len(arrays)
    vmem = pl.BlockSpec(memory_space=pltpu.VMEM)
    out = [jax.ShapeDtypeStruct((groups,) + rows.shape, rows.dtype)]
    out += [jax.ShapeDtypeStruct((shards,) + array.shape, array.dtype) for array in arrays]
    return pl.pallas_call(
        functools.partial(gather_kernel, groups, top, mid, count),
        out_shape=out,
        in_specs=[vmem] * (1 + count),
        out_specs=[vmem] * (1 + count),
        scratch_shapes=[
            pltpu.SemaphoreType.DMA((count, top, mid, 2)),
            pltpu.SemaphoreType.DMA((count, top, mid, 2)),
            pltpu.SemaphoreType.DMA((groups,)),
            pltpu.SemaphoreType.DMA((groups,)),
        ],
        compiler_params=pltpu.CompilerParams(
            collective_id=0, has_side_effects=True, vmem_limit_bytes=VMEM_LIMIT
        ),
    )(rows, *arrays)


CHUNKS = 2


def add(left, right):
    return (left.astype(f32) + right.astype(f32)).astype(bf16)


def scatter_kernel(groups, top, mid, count, *refs):
    partial, flat, grads = refs[0], refs[1], refs[2 : 2 + count]
    refs = refs[2 + count :]
    summed, total, owned = refs[0], refs[1], refs[2 : 2 + count]
    refs = refs[2 + count :]
    pair = refs[:count]
    middle = refs[count : 2 * count]
    line = refs[2 * count : 3 * count]
    far = refs[3 * count : 4 * count]
    flat_pair, flat_mid, flat_top, flat_group, send, receive, flat_send, flat_receive, sum_sems = (
        refs[4 * count :]
    )
    me, t, m, core = position(top, mid)
    group = lax.axis_index("seq")
    greet(groups, top, mid)
    other = {"fsdp": slot_of(t, m, 1 - core, mid)}
    to_mid = [{"fsdp": slot_of(t, lax.rem(m + e, mid), core, mid)} for e in range(mid)]
    to_top = [{"fsdp": slot_of(lax.rem(t + d, top), m, core, mid)} for d in range(top)]
    to_group = [{"seq": lax.rem(group + k, groups)} for k in range(groups)]
    copies = []

    def launch(source, target, index, device):
        copy = remote(source, target, send.at[index], receive.at[index], device)
        copies.append(copy)
        return copy

    def launch_flat(stage, buffer, own, peers):
        started = []
        for k in range(1, len(peers)):
            copy = remote(
                buffer.at[own],
                buffer.at[own],
                flat_send.at[stage, k],
                flat_receive.at[stage, k],
                peers[k],
            )
            started.append(copy)
            copies.append(copy)
        return started

    def total_of(buffer, started):
        for copy in started:
            copy.wait_recv()
        value = buffer[0]
        for k in range(1, buffer.shape[0]):
            value = value + buffer[k]
        return value

    work = [(a, r) for a in range(count) for r in range(CHUNKS)]
    rows_of = [grads[a].shape[3] // CHUNKS for a in range(count)]

    def part(a, r):
        return pl.ds(r * rows_of[a], rows_of[a])

    flat_pair[core] = flat[...]
    stage_flat = launch_flat(0, flat_pair, core, [None, other])
    stage = {}
    for n, (a, r) in enumerate(work):
        stage[n] = launch(
            grads[a].at[:, :, 1 - core, part(a, r)], pair[a].at[:, :, part(a, r)], (n, 0), other
        )
    sums = []
    for k in range(1, groups):
        copy = remote(
            partial.at[lax.rem(group + k, groups)],
            summed.at[group],
            sum_sems.at[0, k],
            sum_sems.at[1, k],
            to_group[k],
        )
        sums.append(copy)
    summed[group] = partial[group]

    stage_mid = {}
    for n, (a, r) in enumerate(work):
        stage[n].wait_recv()

        @pl.loop(0, top)
        def _(i):
            for j in range(mid):
                at = part(a, r)
                pair[a][i, j, at] = add(pair[a][i, j, at], grads[a][i, j, core, at])

        for e in range(1, mid):
            stage_mid[n, e] = launch(
                pair[a].at[:, lax.rem(m + e, mid), part(a, r)],
                middle[a].at[e - 1, :, part(a, r)],
                (n, e),
                to_mid[e],
            )
        if n == 0:
            flat_mid[m] = total_of(flat_pair, stage_flat)
            stage_flat = launch_flat(1, flat_mid, m, to_mid)
    stage_top = {}
    for n, (a, r) in enumerate(work):
        for e in range(1, mid):
            stage_mid[n, e].wait_recv()

        @pl.loop(0, top)
        def _(i):
            at = part(a, r)
            value = pair[a][i, m, at].astype(f32)
            for e in range(1, mid):
                value = value + middle[a][e - 1, i, at].astype(f32)
            line[a][i, at] = value.astype(bf16)

        for d in range(1, top):
            stage_top[n, d] = launch(
                line[a].at[lax.rem(t + d, top), part(a, r)],
                far[a].at[d - 1, part(a, r)],
                (n, mid + d - 1),
                to_top[d],
            )
        if n == 0:
            flat_top[t] = total_of(flat_mid, stage_flat)
            stage_flat = launch_flat(2, flat_top, t, to_top)
    last = []
    for n, (a, r) in enumerate(work):
        at = part(a, r)
        for d in range(1, top):
            stage_top[n, d].wait_recv()
        value = line[a][t, at].astype(f32)
        for d in range(1, top):
            value = value + far[a][d - 1, at].astype(f32)
        owned[a][group, at] = value.astype(bf16)
        for k in range(1, groups):
            last.append(
                launch(
                    owned[a].at[group, at],
                    owned[a].at[group, at],
                    (n, mid + top - 2 + k),
                    to_group[k],
                )
            )
        if n == 0:
            flat_group[group] = total_of(flat_top, stage_flat)
            stage_flat = launch_flat(3, flat_group, group, to_group)
    total[...] = total_of(flat_group, stage_flat)
    for copy in last:
        copy.wait_recv()
    for copy in sums:
        copy.wait()
    for copy in copies:
        copy.wait_send()


def scatter_all(groups, shards, partial, flat, grads):
    top, mid = factors(shards)
    count = len(grads)
    vmem = pl.BlockSpec(memory_space=pltpu.VMEM)
    grads = [grad.reshape(top, mid, 2, grad.shape[0] // shards, grad.shape[1]) for grad in grads]
    shapes = [grad.shape[3:] for grad in grads]
    out = [
        jax.ShapeDtypeStruct(partial.shape, bf16),
        jax.ShapeDtypeStruct(flat.shape, f32),
    ] + [jax.ShapeDtypeStruct((groups,) + shape, bf16) for shape in shapes]
    most = max(2, mid, top, groups)
    stages = mid + top + groups - 2
    return pl.pallas_call(
        functools.partial(scatter_kernel, groups, top, mid, count),
        out_shape=out,
        in_specs=[vmem] * (2 + count),
        out_specs=[vmem] * (2 + count),
        scratch_shapes=[pltpu.VMEM((top, mid) + shape, bf16) for shape in shapes]
        + [pltpu.VMEM((max(1, mid - 1), top) + shape, bf16) for shape in shapes]
        + [pltpu.VMEM((top,) + shape, bf16) for shape in shapes]
        + [pltpu.VMEM((max(1, top - 1),) + shape, bf16) for shape in shapes]
        + [pltpu.VMEM((size,) + flat.shape, f32) for size in (2, mid, top, groups)]
        + [
            pltpu.SemaphoreType.DMA((count * CHUNKS, stages)),
            pltpu.SemaphoreType.DMA((count * CHUNKS, stages)),
            pltpu.SemaphoreType.DMA((4, most)),
            pltpu.SemaphoreType.DMA((4, most)),
            pltpu.SemaphoreType.DMA((2, groups)),
        ],
        compiler_params=pltpu.CompilerParams(
            collective_id=1, has_side_effects=True, vmem_limit_bytes=VMEM_LIMIT
        ),
    )(partial, flat, *grads)


def general(
    tokens,
    cotangent,
    documents,
    in_weight,
    kernel_taps,
    kernel_bias,
    step_bias,
    decay_log,
    skip_gain,
    pre_gain,
    norm_gain,
    out_weight,
):
    groups = lax.axis_size("seq")
    shards = lax.axis_size("fsdp")
    group = lax.axis_index("seq")
    heads = step_bias.shape[0]
    inner = norm_gain.shape[0]
    states = kernel_bias.shape[0] - inner
    half = inner // groups
    spread = out_weight.shape[0] % (HEAD_DIM * groups) == 0
    parts = shards if spread else 1

    def pick(array, axis):
        size = array.shape[axis]
        lead, tail = array.shape[:axis], array.shape[axis + 1 :]
        split = array.reshape(lead + (parts, groups, size // (parts * groups)) + tail)
        chosen = lax.dynamic_index_in_dim(split, group, axis + 1, keepdims=False)
        return chosen.reshape(lead + (size // groups,) + tail)

    def place(array):
        size = array.shape[-1] * groups
        lead = array.shape[:-1]
        split = array.reshape(lead + (parts, 1, size // (parts * groups)))
        blank = jnp.zeros(lead + (parts, groups, size // (parts * groups)), array.dtype)
        full = lax.dynamic_update_slice_in_dim(blank, split, group, len(lead) + 1)
        return full.reshape(lead + (size,))

    def unite(array):
        rows, width = array.shape[1:]
        split = array.reshape(groups, rows, parts, width // parts)
        return split.transpose(1, 2, 0, 3).reshape(rows, width * groups)

    conv_end = inner + inner + states
    conv_shard = jnp.concatenate(
        [
            pick(in_weight[:, inner : 2 * inner], 1),
            in_weight[:, 2 * inner : conv_end],
            pick(in_weight[:, conv_end:], 1),
        ],
        axis=1,
    )
    gate_shard = pick(in_weight[:, :inner], 1)
    out_rows = out_weight
    if spread:
        split = out_weight.reshape(groups, out_weight.shape[0] // groups, out_weight.shape[1])
        out_rows = lax.dynamic_index_in_dim(split, group, 0, keepdims=False)
    floats = tokens.astype(f32)
    normed_own = pre_norm(floats, pre_gain).astype(bf16)
    count, width = tokens.shape
    joined, conv_weight, gate_weight, out_part = gather_all(
        groups,
        shards,
        jnp.concatenate([normed_own, cotangent], axis=1),
        [conv_shard, gate_shard, out_rows],
    )
    joined = joined.reshape(groups * count, 2 * width)
    conv_weight = conv_weight.reshape(width, -1)
    gate_weight = gate_weight.reshape(width, -1)
    out_part = out_part.reshape(-1, width)
    if not spread:
        out_part = lax.dynamic_slice_in_dim(out_part, group * half, half, 0)
    normed_in, cot = joined[:, :width], joined[:, width:]

    projected = dot(normed_in, conv_weight).astype(bf16).astype(f32)
    segment = documents[0]
    taps = jnp.concatenate([pick(kernel_taps[:, :inner], 1), kernel_taps[:, inner:]], axis=1)
    tap_bias = jnp.concatenate([pick(kernel_bias[:inner], 0), kernel_bias[inner:]], axis=0)
    mixed, mixer_back = jax.vjp(
        lambda *given: mixer(segment, *given),
        projected[:, : half + states],
        projected[:, half + states :],
        taps,
        tap_bias,
        pick(step_bias, 0),
        pick(decay_log, 0),
        pick(skip_gain, 0),
    )
    gain = pick(norm_gain, 0)
    gates = dot(normed_in, gate_weight).astype(bf16).astype(f32)
    mixed = mixed.astype(bf16).astype(f32)
    back_normed = dot(cot, out_part, contract_rows)
    sigmoid = jax.nn.sigmoid(gates)
    silu = gates * sigmoid
    gated = mixed * silu
    back_gain = back_normed * gain
    sums = lax.psum(
        jnp.stack([jnp.sum(gated * gated, axis=1), jnp.sum(gated * back_gain, axis=1)]), "seq"
    )
    scale = lax.rsqrt(sums[0] / inner + norm_epsilon)
    unit = gated * scale[:, None]
    normed_bf = (unit * gain).astype(bf16)
    norm_gain_part = jnp.sum(back_normed * unit, axis=0)
    back_gated = scale[:, None] * (back_gain - unit * (scale * sums[1] / inner)[:, None])
    back_mixed = (back_gated * silu).astype(bf16).astype(f32)
    back_gates = (back_gated * mixed * sigmoid * (1.0 + gates * (1.0 - sigmoid))).astype(bf16)

    outward = dot(normed_bf, cot, contract_tokens).astype(bf16)
    gate_grad = dot(normed_in, back_gates, contract_tokens).astype(bf16)
    if not spread:
        blank = jnp.zeros((inner, width), bf16)
        outward = lax.dynamic_update_slice_in_dim(blank, outward, group * half, 0)
    branch = dot(normed_bf, out_part).astype(bf16)

    back_conv, back_steps, taps_part, bias_part, step_part, decay_part, skip_part = mixer_back(
        back_mixed
    )
    back_projected = jnp.concatenate([back_conv, back_steps], axis=1).astype(bf16)
    conv_grad = dot(normed_in, back_projected, contract_tokens).astype(bf16)
    back_in = dot(back_projected, conv_weight, contract_rows) + dot(
        back_gates, gate_weight, contract_rows
    )
    pre_gain_part = jnp.sum(back_in * normed_in.astype(f32), axis=0) / pre_gain

    pieces = (
        jnp.concatenate([place(taps_part[:, :half]), taps_part[:, half:]], axis=1),
        jnp.concatenate([place(bias_part[:half]), bias_part[half:]], axis=0),
        place(step_part),
        place(decay_part),
        place(skip_part),
        pre_gain_part,
        place(norm_gain_part),
    )
    flat = jnp.concatenate([piece.reshape(-1) for piece in pieces])
    padded = jnp.pad(flat, (0, -flat.size % 1024)).reshape(-1, 128)
    partial = jnp.concatenate(
        [
            back_in.astype(bf16).reshape(groups, count, width),
            branch.reshape(groups, count, width),
        ],
        axis=1,
    )
    partial, padded, conv_all, gate_all, out_all = scatter_all(
        groups, shards, partial, padded, [conv_grad, gate_grad, outward]
    )
    partial = jnp.sum(partial.astype(f32), axis=0)
    block_output = (floats + partial[count:]).astype(bf16)
    _, pre_back = jax.vjp(lambda given: pre_norm(given, pre_gain), floats)
    tokens_grad = cotangent.astype(f32) + pre_back(partial[:count])[0]
    conv_all, gate_all, out_all = (
        conv_all.astype(f32),
        gate_all.astype(f32),
        out_all.astype(f32),
    )
    if spread:
        outward_grad = out_all.reshape(-1, width)
    else:
        outward_grad = jnp.sum(out_all, axis=0)
    inward_grad = jnp.concatenate(
        [
            unite(gate_all),
            unite(conv_all[:, :, :half]),
            jnp.sum(conv_all[:, :, half : half + states], axis=0),
            unite(conv_all[:, :, half + states :]),
        ],
        axis=1,
    )
    flat = padded.reshape(-1)
    totals = []
    start = 0
    for piece in pieces:
        totals.append(flat[start : start + piece.size].reshape(piece.shape))
        start += piece.size
    return (
        block_output,
        tokens_grad,
        inward_grad,
        totals[0],
        totals[1],
        totals[2],
        totals[3],
        totals[4],
        totals[5],
        totals[6],
        outward_grad,
    )


LANES = 128
FAR = -1e30
SENDS = 130
exact = lax.Precision.HIGHEST


def sharp(left, right, dims=(((1,), (0,)), ((), ()))):
    return lax.dot_general(left, right, dims, precision=exact, preferred_element_type=f32)


def iota(shape, axis):
    return lax.broadcasted_iota(jnp.int32, shape, axis)


def span_of(index, size):
    return pl.ds(pl.multiple_of(index * size, size), size)


class Courier:
    def __init__(self, send):
        self.send = send
        self.count = 0
        self.made = []
        self.stays = []

    def start(self, source, target, receive, device, when=None):
        slot = self.count
        self.count += 1

        def make():
            return pltpu.make_async_remote_copy(
                src_ref=source(),
                dst_ref=target(),
                send_sem=self.send.at[slot],
                recv_sem=receive(),
                device_id=device(),
                device_id_type=MESH,
            )

        self.made.append((make, when))
        self.run(lambda: make().start(), when)

    def run(self, act, when):
        if when is None:
            act()
        else:
            pl.when(when)(act)

    def arrive(self, target, receive, device):
        pltpu.make_async_remote_copy(
            src_ref=target,
            dst_ref=target,
            send_sem=self.send.at[0],
            recv_sem=receive,
            device_id=device,
            device_id_type=MESH,
        ).wait_recv()

    def local(self, source, target, sem, when=None):
        make = lambda: pltpu.make_async_copy(source(), target(), sem)
        self.stays.append((make, when))
        self.run(lambda: make().start(), when)

    def finish(self):
        for make, when in self.stays:
            self.run(lambda make=make: make().wait(), when)
        for make, when in self.made:
            self.run(lambda make=make: make().wait_send(), when)


def fused_kernel(top, *refs):
    (
        tokens, cotangent, documents, in_weight, taps, params, pre_gain, norm_gain, out_weight,
        got_b, got_i, own_out, own_gate, own_conv, flat_all,
        nall, call, docs, conv_pack, gate_pack, conv_all, gate_all, out_all,
        proj, act, dact, mk, bias_mask, step, ldec, sgate, cum, cum_t, cum_b, step_e, skip_e, scaled,
        scores, decay, weigh, inside, mixed, gates, bnorm, gain_own, sums, sums_all, totals,
        normed_bf, bmixed, bgates, norm_part, part_b, part_i, dscore, x1, x2, dz, skip_part, bproj, pre_part,
        gr_out, gr_gate, gr_conv, y_out, y_gate, y_conv, line_out, line_gate, line_conv,
        low_out, low_gate, low_conv, high_out, high_gate, high_conv,
        flat, flat_y, flat_z, flat_own,
        send, r_rows, r_docs, r_conv, r_gate, r_out, r_sums, r_part,
        ry_out, ry_gate, ry_conv, rl_out, rl_gate, rl_conv, rh_out, rh_gate, rh_conv,
        ro_out, ro_gate, ro_conv, r_flat, r_local,
    ) = refs
    mid = 2
    me, t, m, c = position(top, mid)
    g = lax.axis_index("seq")
    count, width = tokens.shape
    length = documents.shape[1]
    seqs = 2
    total = seqs * length
    rows = in_weight.shape[0]
    inner = norm_gain.shape[1]
    quarter = inner // 4
    tiles = quarter // LANES
    states = taps.shape[1] - inner
    conv_tiles = tiles + states // LANES
    active = conv_tiles * LANES
    conv_cols = active + LANES
    heads = params_heads(inner)
    local_heads = heads // 4
    mail = Courier(send)

    def dev(tt, mm, cc):
        return lambda: {"fsdp": slot_of(tt, mm, cc, mid)}

    def dev_g(gg, tt, mm, cc):
        return lambda: {"seq": gg, "fsdp": slot_of(tt, mm, cc, mid)}

    here = {"fsdp": slot_of(t, m, 1 - c, mid)}
    group = [
        (2 * (1 - c) + g, dev_g(g, t, m, 1 - c)),
        (2 * c + 1 - g, dev_g(1 - g, t, m, c)),
        (2 * (1 - c) + 1 - g, dev_g(1 - g, t, m, 1 - c)),
    ]
    mine = 2 * c + g

    barrier = pltpu.get_barrier_semaphore()
    greeted = [d() for _, d in group]
    greeted += [{"fsdp": slot_of(t, 1 - m, cc, mid)} for cc in range(2)]
    greeted += [
        {"fsdp": slot_of(lax.rem(t + d, top), m, cc, mid)} for d in range(1, top) for cc in range(2)
    ]
    for peer in greeted:
        pl.semaphore_signal(barrier, inc=1, device_id=peer, device_id_type=MESH)

    def tile_of(n, cc):
        return 4 * n + 2 * cc + g

    def selector(cc):
        glob, loc = iota((LANES, LANES), 0), iota((LANES, LANES), 1)
        wanted = 8 * (loc // 2) + 4 * cc + 2 * g + loc % 2
        return jnp.where((glob == wanted) & (loc < local_heads), 1.0, 0.0)

    def pack(conv, gate, cc):
        for n in range(tiles):
            at = span_of(tile_of(n, cc) + inner // LANES, LANES)
            conv[:, n * LANES : (n + 1) * LANES] = in_weight[:, at]
        conv[:, quarter:active] = in_weight[:, 2 * inner : 2 * inner + states]
        picked = dot(in_weight[:, 2 * inner + states :], selector(cc)[:heads].astype(bf16))
        conv[:, active:] = picked.astype(bf16)

    def pack_gate(gate, cc):
        for n in range(tiles):
            gate[:, n * LANES : (n + 1) * LANES] = in_weight[:, span_of(tile_of(n, cc), LANES)]

    pack(conv_all.at[me], None, c)
    pack(conv_pack, None, 1 - c)
    pl.semaphore_wait(barrier, len(greeted))

    near = t + 1 - 2 * lax.rem(t, 2)
    far = lax.rem(t + top // 2, top)
    last = lax.rem(near + top // 2, top)

    def spread(mine_ref, pack_ref, all_ref, receive):
        for src, cc in ((mine_ref, c), (lambda: pack_ref, 1 - c)):
            for up in (1, -1):
                ok = (t + 1 < top) if up == 1 else (t >= 1)
                mail.start(
                    src, lambda: all_ref.at[me], lambda: receive.at[me],
                    dev(t + up, m, cc), ok,
                )
            mail.start(
                src, lambda: all_ref.at[me], lambda: receive.at[me], dev(t, 1 - m, cc)
            )
        mail.start(lambda: pack_ref, lambda: all_ref.at[me], lambda: receive.at[me], dev(t, m, 1 - c))

    def relay(all_ref, receive, d):
        for up in (1, -1):
            ok = (t >= d) if up == 1 else (t + d < top)
            onward = ok & ((t + 1 < top) if up == 1 else (t >= 1))
            from_t = jnp.clip(t - up * d, 0, top - 1)
            for cc in range(2):
                slot = slot_of(from_t, m, cc, mid)
                mail.run(lambda slot=slot: mail.arrive(all_ref.at[slot], receive.at[slot], here), ok)
                block = lambda slot=slot: all_ref.at[slot]
                sem = lambda slot=slot: receive.at[slot]
                mail.start(block, block, sem, dev(t + up, m, c), onward)
                mail.start(block, block, sem, dev(t, 1 - m, c), ok)

    def settle(all_ref, receive):
        slot = slot_of(t, m, 1 - c, mid)
        mail.arrive(all_ref.at[slot], receive.at[slot], here)
        for tt in range(top):
            for cc in range(2):
                slot = slot_of(tt, 1 - m, cc, mid)
                mail.arrive(all_ref.at[slot], receive.at[slot], here)

    spread(lambda: conv_all.at[me], conv_pack, conv_all, r_conv)

    floats = tokens[...].astype(f32)
    nall[mine] = pre_norm(floats, pre_gain[...]).astype(bf16)
    for k, (_, device) in enumerate(group):
        mail.start(lambda: nall.at[mine], lambda: nall.at[mine], lambda: r_rows.at[0, mine], device)
    docs[c] = jnp.broadcast_to(documents[...].astype(f32), (8, length))
    mail.start(lambda: docs.at[c], lambda: docs.at[c], lambda: r_docs.at[0], dev(t, m, 1 - c))

    pack_gate(gate_all.at[me], c)
    pack_gate(gate_pack, 1 - c)
    relay(conv_all, r_conv, 1)
    spread(lambda: gate_all.at[me], gate_pack, gate_all, r_gate)

    holder = c == g
    keeper = c == m
    mail.run(lambda: out_all.__setitem__(t, out_weight[...]), holder & keeper)
    row_block = lambda: out_weight
    row_target = lambda: out_all.at[t]
    row_sem = lambda: r_out.at[t]
    mail.start(row_block, row_target, row_sem, dev(t + 1, m, m), holder & (t + 1 < top))
    mail.start(row_block, row_target, row_sem, dev(t - 1, m, m), holder & (t >= 1))
    mail.start(row_block, row_target, row_sem, dev(t, 1 - m, m), holder)
    mail.start(row_block, row_target, row_sem, dev(t, m, 1 - c), holder & (c != m))

    def relay_rows(d):
        for up in (1, -1):
            ok = keeper & ((t >= d) if up == 1 else (t + d < top))
            onward = ok & ((t + 1 < top) if up == 1 else (t >= 1))
            slot = jnp.clip(t - up * d, 0, top - 1)
            mail.run(lambda: mail.arrive(out_all.at[slot], r_out.at[slot], here), ok)
            block = lambda slot=slot: out_all.at[slot]
            sem = lambda slot=slot: r_out.at[slot]
            mail.start(block, block, sem, dev(t + up, m, c), onward)
            mail.start(block, block, sem, dev(t, 1 - m, c), ok)

    def settle_rows():
        mail.run(lambda: mail.arrive(out_all.at[t], r_out.at[t], here), keeper & (c != g))
        for tt in range(top):
            mail.run(lambda tt=tt: mail.arrive(out_all.at[tt], r_out.at[tt], here), c != m)

    call[mine] = cotangent[...]
    for k, (_, device) in enumerate(group):
        mail.start(lambda: call.at[mine], lambda: call.at[mine], lambda: r_rows.at[1, mine], device)

    for slot, _ in group:
        mail.arrive(nall.at[slot], r_rows.at[0, slot], here)
    mail.arrive(docs.at[1 - c], r_docs.at[0], here)

    @pl.loop(0, seqs)
    def _(s):
        row = docs[s][:1]
        column = jnp.broadcast_to(row, (LANES, length)).T
        wide = jnp.concatenate([column] * (length // LANES), axis=1)
        ahead = iota((length, length), 0) >= iota((length, length), 1)
        bias_mask[s] = jnp.where(ahead & (wide == row), 0.0, FAR)
        place = iota((length, LANES), 0)
        for k in range(1, CONV):
            same = (pltpu.roll(column, k, 0) == column) & (place >= k)
            mk[s, k - 1] = jnp.where(same, 1.0, 0.0)

    for n in range(tiles):
        gain_own[:, n * LANES : (n + 1) * LANES] = norm_gain[:, span_of(tile_of(n, c), LANES)]

    for d in range(2, top):
        relay(conv_all, r_conv, d)
    settle(conv_all, r_conv)

    def tall(ref):
        return ref[...].reshape(total, width)

    def weights(ref, cols):
        return ref[:, :, cols].reshape(width, cols.size)

    wide_cols = 256

    @pl.loop(0, conv_cols // wide_cols)
    def _(n):
        at = span_of(n, wide_cols)
        proj[:, at] = dot(tall(nall), weights(conv_all, at)).astype(bf16)

    if conv_cols % wide_cols:
        rest = pl.ds(conv_cols - LANES, LANES)
        proj[:, rest] = dot(tall(nall), weights(conv_all, rest)).astype(bf16)

    relay(gate_all, r_gate, 1)
    relay_rows(1)

    chosen = sharp(params[:8], selector(c))
    rate = jnp.exp(chosen[1:2])
    raw = proj[:, active:].astype(f32) + chosen[:1]
    step[...] = jnp.maximum(raw, 0.0) + jnp.log1p(jnp.exp(-jnp.abs(raw)))
    sgate[...] = jax.nn.sigmoid(raw)
    ldec[...] = step[...] * -rate
    to_channels = jnp.where(iota((LANES, quarter), 1) // HEAD_DIM == iota((LANES, quarter), 0), 1.0, 0.0)
    to_heads = jnp.where(iota((quarter, LANES), 0) // HEAD_DIM == iota((quarter, LANES), 1), 1.0, 0.0)
    step_e[...] = sharp(step[...], to_channels)
    skip_e[...] = sharp(chosen, to_channels)
    lower = jnp.where(iota((length, length), 0) >= iota((length, length), 1), 1.0, 0.0)
    for s in range(seqs):
        at = slice(s * length, (s + 1) * length)
        cum[at] = sharp(lower, ldec[at])
        cum_t[s] = cum[at].T
    for h in range(local_heads):
        cum_b[h] = jnp.broadcast_to(cum[:, h : h + 1], (total, LANES))

    def conv_tile(n):
        return jnp.where(n < tiles, tile_of(n, c), n - tiles + inner // LANES)

    @pl.loop(0, seqs * conv_tiles)
    def _(i):
        s, n = i // conv_tiles, i % conv_tiles
        at, cols = span_of(s, length), span_of(n, LANES)
        where = span_of(conv_tile(n), LANES)
        x = proj[at, cols].astype(f32)
        tap = taps[:, where]
        z = params[pl.ds(8 + conv_tile(n), 1)] + x * tap[CONV - 1 : CONV]
        for k in range(1, CONV):
            z = z + tap[CONV - 1 - k : CONV - k] * (pltpu.roll(x, k, 0) * mk[s, k - 1])
        sig = jax.nn.sigmoid(z)
        act[at, cols] = z * sig
        dact[at, cols] = sig * (1.0 + z * (1.0 - sig))

    relay(gate_all, r_gate, 2)
    relay_rows(2)

    def matrices(s):
        at = span_of(s, length)
        return (
            act[at, quarter : quarter + STATE].astype(bf16),
            act[at, quarter + STATE : active].astype(bf16),
        )

    @pl.loop(0, seqs)
    def _(s):
        b_in, c_out = matrices(s)
        scores[s] = dot(c_out, b_in, contract_rows)

    half_of = lambda: iota((length, LANES), 1) // HEAD_DIM

    @pl.loop(0, seqs * tiles)
    def _(i):
        s, n = i // tiles, i % tiles
        at, cols = span_of(s, length), span_of(n, LANES)
        vals = act[at, cols]
        sc = (vals * step_e[at, cols]).astype(bf16)
        scaled[at, cols] = sc
        y = jnp.zeros((length, LANES), f32)
        for b in range(2):
            h = 2 * n + b
            col = cum_b[h, at]
            gap = jnp.concatenate([col] * (length // LANES), axis=1) - cum_t[s, pl.ds(h, 1)]
            d = jnp.exp(gap + bias_mask[s])
            decay[s * local_heads + h] = d
            w = (d * scores[s]).astype(bf16)
            weigh[s * local_heads + h] = w
            y = y + dot(w, jnp.where(half_of() == b, sc, jnp.zeros_like(sc)))
        inside[at, cols] = y
        mixed[at, cols] = (y + vals * skip_e[2:3, cols]).astype(bf16)

    for d in range(3, top):
        relay(gate_all, r_gate, d)
        relay_rows(d)
    settle(gate_all, r_gate)

    @pl.loop(0, quarter // wide_cols)
    def _(n):
        at = span_of(n, wide_cols)
        gates[:, at] = dot(tall(nall), weights(gate_all, at)).astype(bf16)

    settle_rows()
    for slot, _ in group:
        mail.arrive(call.at[slot], r_rows.at[1, slot], here)

    @pl.loop(0, tiles // 2)
    def _(n):
        w = out_all[pl.ds(2 * n, 2)].reshape(2 * LANES, width)
        bnorm[:, span_of(n, 2 * LANES)] = dot(tall(call), w, contract_rows)

    strip = 64

    @pl.loop(0, total // strip)
    def _(i):
        at = span_of(i, strip)
        gate = gates[at].astype(f32)
        gated = mixed[at].astype(f32) * (gate * jax.nn.sigmoid(gate))
        first = jnp.sum(gated * gated, axis=1, keepdims=True)
        second = jnp.sum(gated * (bnorm[at] * gain_own[...]), axis=1, keepdims=True)
        lane = iota((strip, LANES), 1)
        sums[at] = jnp.where(lane == 0, first, jnp.where(lane == 1, second, 0.0))

    sums_all[mine] = sums[...].T[:8]
    for k, (_, device) in enumerate(group):
        mail.start(lambda: sums_all.at[mine], lambda: sums_all.at[mine], lambda: r_sums.at[mine], device)
    for slot, _ in group:
        mail.arrive(sums_all.at[slot], r_sums.at[slot], here)
    summed = (sums_all[0] + sums_all[1]) + (sums_all[2] + sums_all[3])
    totals[...] = jnp.concatenate([summed, jnp.zeros((LANES - 8, total), f32)], axis=0).T

    norm_part[...] = jnp.zeros_like(norm_part)

    @pl.loop(0, total // strip)
    def _(i):
        at = span_of(i, strip)
        gate = gates[at].astype(f32)
        mix = mixed[at].astype(f32)
        sig = jax.nn.sigmoid(gate)
        silu = gate * sig
        gated = mix * silu
        gain = gain_own[...]
        scale = lax.rsqrt(totals[at, 0:1] / inner + norm_epsilon)
        unit = gated * scale
        back = bnorm[at]
        normed_bf[at] = (unit * gain).astype(bf16)
        norm_part[...] += jnp.sum(back * unit, axis=0, keepdims=True)
        back_gated = scale * (back * gain - unit * (scale * totals[at, 1:2] / inner))
        bmixed[at] = (back_gated * silu).astype(bf16)
        bgates[at] = (back_gated * mix * sig * (1.0 + gate * (1.0 - sig))).astype(bf16)

    def tall_cols(ref, at):
        return ref[:, :, at].reshape(total, at.size)

    def add_blocks(target, left, right):
        *lead, tall_rows, cols = target.shape
        piece = 32
        for at in [()] if not lead else [(i,) for i in range(lead[0])]:

            @pl.loop(0, tall_rows // piece)
            def _(i, at=at):
                where = at + (span_of(i, piece),)
                target[where] = add(left[where], right[where])

    def reducer(own, y_got, y_sem, line, low, low_sem, high, high_sem, ok=None):
        def step(r):
            def take():
                mail.arrive(y_got.at[r], y_sem.at[r], here)
                add_blocks(line.at[r], own(r), y_got.at[r])
                if r >= 2:
                    mail.arrive(low.at[r - 2], low_sem.at[r - 2], here)
                    add_blocks(line.at[r], line.at[r], low.at[r - 2])
                if r == 3:
                    mail.arrive(high.at[0], high_sem.at[0], here)
                    add_blocks(line.at[r], line.at[r], high.at[0])

            mail.run(take, ok)
            if r < 2:
                mail.start(
                    lambda: line.at[r], lambda: low.at[r], lambda: low_sem.at[r], dev(near, m, c), ok
                )
            if r == 2:
                mail.start(
                    lambda: line.at[r], lambda: high.at[0], lambda: high_sem.at[0], dev(far, m, c), ok
                )

        return step

    def hand_over(line, own, receive, at):
        mail.local(lambda: line.at[3, c], lambda: own.at[g, c], r_local.at[at])
        for gg, cc in ((g, 1 - c), (1 - g, c), (1 - g, 1 - c)):
            mail.start(
                lambda cc=cc: line.at[3, cc], lambda: own.at[g, c], lambda: receive.at[g, c],
                dev_g(gg, t, m, cc),
            )

    def take_over(own, receive):
        for gg, cc in ((g, 1 - c), (1 - g, c), (1 - g, 1 - c)):
            mail.arrive(own.at[gg, cc], receive.at[gg, cc], here)

    out_step = reducer(
        lambda r: gr_out.at[r], y_out, ry_out, line_out, low_out, rl_out, high_out, rh_out, keeper
    )
    gate_step = reducer(
        lambda r: gr_gate.at[r, m], y_gate, ry_gate, line_gate, low_gate, rl_gate, high_gate, rh_gate
    )
    conv_step = reducer(
        lambda r: gr_conv.at[r, m], y_conv, ry_conv, line_conv, low_conv, rl_conv, high_conv, rh_conv
    )
    order = (last, near, far, t)
    block = width // top

    for r in range(top):
        got = dot(tall_cols(nall, span_of(order[r], block)), bgates[...], contract_tokens).astype(bf16)
        gr_gate[r] = got.reshape(gr_gate.shape[1:])
        mail.start(
            lambda r=r: gr_gate.at[r, 1 - m], lambda r=r: y_gate.at[r], lambda r=r: ry_gate.at[r],
            dev(t, 1 - m, c),
        )

    for r in range(top):
        gr_out[r] = dot(normed_bf[:, span_of(order[r], LANES)], tall(call), contract_tokens).astype(bf16)
        mail.start(
            lambda r=r: gr_out.at[r], lambda r=r: y_out.at[r], lambda r=r: ry_out.at[r],
            dev(t, 1 - m, c), c != m,
        )

    @pl.loop(0, width // wide_cols)
    def _(n):
        at = span_of(n, wide_cols)
        w = out_all[:, :, at].reshape(quarter, wide_cols)
        part_b[:, :, at] = dot(normed_bf[...], w).astype(bf16).reshape(4, count, wide_cols)

    for slot, device in group:
        mail.start(
            lambda slot=slot: part_b.at[slot], lambda: got_b.at[mine], lambda: r_part.at[0, mine], device
        )
    mail.local(lambda: part_b.at[mine], lambda: got_b.at[mine], r_local.at[3])

    skip_part[...] = jnp.zeros_like(skip_part)
    dscore[...] = jnp.zeros_like(dscore)

    @pl.loop(0, seqs * tiles)
    def _(i):
        s, n = i // tiles, i % tiles
        at, cols = span_of(s, length), span_of(n, LANES)
        back = bmixed[at, cols]
        sc = scaled[at, cols]
        ds = jnp.zeros((length, LANES), f32)
        gather = dscore[s]
        for b in range(2):
            h = s * local_heads + 2 * n + b
            one = jnp.where(half_of() == b, back, jnp.zeros_like(back))
            gather = gather + decay[h] * dot(one, sc, contract_rows)
            ds = ds + dot(weigh[h], one, contract_tokens)
        dscore[s] = gather
        back = back.astype(f32)
        vals = act[at, cols]
        x1[at, cols] = back * inside[at, cols] - sc.astype(f32) * ds
        x2[at, cols] = ds * vals
        dz[at, cols] = (back * skip_e[2:3, cols] + ds * step_e[at, cols]) * dact[at, cols]
        skip_part[:, cols] += jnp.sum(back * vals, axis=0, keepdims=True)

    gate_step(0)
    @pl.loop(0, seqs)
    def _(s):
        at = span_of(s, length)
        b_in, c_out = matrices(s)
        ds = dscore[s].astype(bf16)
        b_cols, c_cols = slice(quarter, quarter + STATE), slice(quarter + STATE, active)
        dz[at, b_cols] = dot(ds, c_out, contract_tokens) * dact[at, b_cols]
        dz[at, c_cols] = dot(ds, b_in) * dact[at, c_cols]

    back_cum = sharp(x1[...], to_heads)
    back_step = sharp(x2[...], to_heads)
    upper = jnp.where(iota((length, length), 0) <= iota((length, length), 1), 1.0, 0.0)
    back_decay = jnp.concatenate(
        [sharp(upper, back_cum[s * length : (s + 1) * length]) for s in range(seqs)], axis=0
    )
    back_raw = (back_step - back_decay * rate) * sgate[...]
    bproj[:, active:] = back_raw.astype(bf16)
    flat[conv_tiles] = jnp.concatenate(
        [norm_part[:1, n * LANES : (n + 1) * LANES] for n in range(tiles)]
        + [
            jnp.sum(back_raw, axis=0, keepdims=True),
            jnp.sum(back_decay * ldec[...], axis=0, keepdims=True),
            sharp(skip_part[...], to_heads)[:1],
            jnp.zeros((8 - tiles - 3, LANES), f32),
        ],
        axis=0,
    )

    gate_step(1)
    @pl.loop(0, conv_tiles)
    def _(n):
        cols, where = span_of(n, LANES), span_of(conv_tile(n), LANES)
        tap = taps[:, where]
        grads = [jnp.zeros((1, LANES), f32) for _ in range(CONV + 1)]
        for s in range(seqs):
            at = slice(s * length, (s + 1) * length)
            x = proj[at, cols].astype(f32)
            back = dz[at, cols]
            dx = back * tap[CONV - 1 : CONV]
            grads[CONV] += jnp.sum(back, axis=0, keepdims=True)
            grads[CONV - 1] += jnp.sum(back * x, axis=0, keepdims=True)
            for k in range(1, CONV):
                kept = back * mk[s, k - 1]
                dx = dx + tap[CONV - 1 - k : CONV - k] * pltpu.roll(kept, length - k, 0)
                grads[CONV - 1 - k] += jnp.sum(kept * pltpu.roll(x, k, 0), axis=0, keepdims=True)
            bproj[at, cols] = dx.astype(bf16)
        flat[n] = jnp.concatenate(grads + [jnp.zeros((8 - CONV - 1, LANES), f32)], axis=0)

    for r in range(top):
        got = dot(tall_cols(nall, span_of(order[r], block)), bproj[...], contract_tokens).astype(bf16)
        gr_conv[r] = got.reshape(gr_conv.shape[1:])
        mail.start(
            lambda r=r: gr_conv.at[r, 1 - m], lambda r=r: y_conv.at[r], lambda r=r: ry_conv.at[r],
            dev(t, 1 - m, c),
        )

    gate_step(2)
    out_step(0)
    @pl.loop(0, width // wide_cols)
    def _(n):
        at = span_of(n, wide_cols)
        slots = pl.ds(n * (wide_cols // rows), wide_cols // rows)
        value = dot(bproj[...], conv_all[slots].reshape(wide_cols, conv_cols), contract_rows)
        value = value + dot(bgates[...], gate_all[slots].reshape(wide_cols, quarter), contract_rows)
        part_i[:, :, at] = value.astype(bf16).reshape(4, count, wide_cols)
        seen = tall_cols(nall, at).astype(f32)
        pre_part[:, at] = jnp.broadcast_to(
            jnp.sum(value * seen, axis=0, keepdims=True) / pre_gain[:, at], (8, wide_cols)
        )

    for slot, device in group:
        mail.start(
            lambda slot=slot: part_i.at[slot], lambda: got_i.at[mine], lambda: r_part.at[1, mine], device
        )
    mail.local(lambda: part_i.at[mine], lambda: got_i.at[mine], r_local.at[4])
    flat[conv_tiles + 1] = jnp.concatenate(
        [pre_part[:1, n * LANES : (n + 1) * LANES] for n in range(width // LANES)], axis=0
    )
    mail.start(lambda: flat, lambda: flat_y, lambda: r_flat.at[0, 0], dev(t, 1 - m, c))

    gate_step(3)
    hand_over(line_gate, own_gate, ro_gate, 0)
    out_step(1)
    out_step(2)
    conv_step(0)
    conv_step(1)
    out_step(3)
    mail.local(lambda: line_out.at[3], lambda: own_out, r_local.at[2], keeper & holder)
    mail.start(
        lambda: line_out.at[3], lambda: own_out, lambda: ro_out.at[0], dev_g(g, t, m, 1 - c),
        keeper & (c != g),
    )
    mail.start(
        lambda: line_out.at[3], lambda: own_out, lambda: ro_out.at[0], dev_g(1 - g, t, m, g), keeper
    )
    conv_step(2)
    conv_step(3)
    hand_over(line_conv, own_conv, ro_conv, 1)

    mail.arrive(flat_y, r_flat.at[0, 0], here)
    flat_z[t] = flat[...] + flat_y[...]
    for d in range(1, top):
        mail.start(
            lambda: flat_z.at[t], lambda: flat_z.at[t], lambda: r_flat.at[1, t],
            dev(lax.rem(t + d, top), m, c),
        )

    for d in range(1, top):
        slot = lax.rem(t - d + top, top)
        mail.arrive(flat_z.at[slot], r_flat.at[1, slot], here)
    value = flat_z[0]
    for k in range(1, top):
        value = value + flat_z[k]
    flat_own[...] = value
    for slot, device in group:
        mail.start(lambda: flat_own, lambda: flat_all.at[mine], lambda: r_flat.at[2, mine], device)
    mail.local(lambda: flat_own, lambda: flat_all.at[mine], r_local.at[5])
    for k in range(2):
        for slot, _ in group:
            mail.arrive((got_b, got_i)[k].at[slot], r_part.at[k, slot], here)
    mail.run(lambda: mail.arrive(own_out, ro_out.at[0], here), jnp.logical_not(holder & keeper))
    take_over(own_gate, ro_gate)
    for slot, _ in group:
        mail.arrive(flat_all.at[slot], r_flat.at[2, slot], here)
    take_over(own_conv, ro_conv)
    mail.finish()


def finish_kernel(inner, heads, *refs):
    (
        tokens, cotangent, pre_gain, got_b, got_i, own_out, own_gate, own_conv, flat_all,
        *targets,
    ) = refs
    outs, scratch, sems = targets[:11], targets[11:22], targets[22]
    (
        block_output, tokens_grad, in_grad, taps_grad, bias_grad, step_grad, decay_grad, skip_grad,
        pre_grad, norm_grad, out_grad,
    ) = scratch
    count, width = tokens.shape
    quarter = inner // 4
    tiles = quarter // LANES
    states = taps_grad.shape[1] - inner
    conv_tiles = tiles + states // LANES
    active = conv_tiles * LANES
    local_heads = heads // 4

    def send(*which):
        for k in which:
            pltpu.make_async_copy(scratch[k], outs[k], sems.at[k]).start()

    parts = [(gg, cc, flat_all.at[2 * cc + gg]) for gg in range(2) for cc in range(2)]

    def selector_of(gg, cc):
        loc, glob = iota((LANES, LANES), 0), iota((LANES, LANES), 1)
        wanted = 8 * (loc // 2) + 4 * cc + 2 * gg + loc % 2
        return jnp.where((glob == wanted) & (loc < local_heads), 1.0, 0.0)

    def put_tiles(base, own):
        for gg in range(2):
            for cc in range(2):
                for n in range(tiles):
                    j = base + 4 * n + 2 * cc + gg
                    in_grad[:, j * LANES : (j + 1) * LANES] = own[
                        gg, cc, :, n * LANES : (n + 1) * LANES
                    ].astype(f32)

    put_tiles(0, own_gate)
    put_tiles(inner // LANES, own_conv)
    shared = sum(own_conv[gg, cc, :, quarter:active].astype(f32) for gg, cc, _ in parts)
    in_grad[:, 2 * inner : 2 * inner + states] = shared
    ends = sum(dot(own_conv[gg, cc, :, active:], selector_of(gg, cc).astype(bf16)) for gg, cc, _ in parts)
    in_grad[:, 2 * inner + states :] = ends[:, :heads]
    send(2)
    out_grad[...] = own_out[...].astype(f32)
    send(10)

    for gg, cc, part in parts:
        for n in range(tiles):
            j = 4 * n + 2 * cc + gg
            at = slice(j * LANES, (j + 1) * LANES)
            taps_grad[:, at] = part[n, :CONV]
            bias_grad[j : j + 1] = part[n, CONV : CONV + 1]
            norm_grad[:, at] = part[conv_tiles, n : n + 1]
    for n in range(tiles, conv_tiles):
        j = n - tiles + inner // LANES
        value = sum(part[n] for _, _, part in parts)
        taps_grad[:, j * LANES : (j + 1) * LANES] = value[:CONV]
        bias_grad[j : j + 1] = value[CONV : CONV + 1]
    by_head = sum(sharp(part[conv_tiles], selector_of(gg, cc)) for gg, cc, part in parts)
    step_grad[...] = by_head[tiles : tiles + 1, :heads]
    decay_grad[...] = by_head[tiles + 1 : tiles + 2, :heads]
    skip_grad[...] = by_head[tiles + 2 : tiles + 3, :heads]
    value = sum(part[conv_tiles + 1] for _, _, part in parts)
    for n in range(width // LANES):
        pre_grad[:, n * LANES : (n + 1) * LANES] = value[n : n + 1]
    send(3, 4, 5, 6, 7, 8, 9)

    @pl.loop(0, count // 16)
    def _(i):
        at = span_of(i, 16)
        x = tokens[at].astype(f32)
        branch = sum(got_b[q, at].astype(f32) for q in range(4))
        back = sum(got_i[q, at].astype(f32) for q in range(4)) * pre_gain[...]
        block_output[at] = (x + branch).astype(bf16)
        scale = lax.rsqrt(jnp.mean(x * x, axis=1, keepdims=True) + norm_epsilon)
        shared = jnp.mean(x * back, axis=1, keepdims=True) * (scale * scale * scale)
        tokens_grad[at] = cotangent[at].astype(f32) + back * scale - x * shared

    send(0, 1)
    for k in range(len(outs)):
        pltpu.make_async_copy(scratch[k], outs[k], sems.at[k]).wait()


def params_heads(inner):
    return inner // HEAD_DIM


def fused(
    tokens, cotangent, documents, in_weight, kernel_taps, kernel_bias, step_bias, decay_log, skip_gain,
    pre_gain, norm_gain, out_weight,
):
    shards = lax.axis_size("fsdp")
    top, mid = factors(shards)
    count, width = tokens.shape
    length = documents.shape[1]
    total = 2 * length
    rows, columns = in_weight.shape
    inner = norm_gain.shape[0]
    channels = kernel_bias.shape[0]
    quarter = inner // 4
    tiles = quarter // LANES
    conv_tiles = tiles + (channels - inner) // LANES
    conv_cols = (conv_tiles + 1) * LANES
    active = conv_tiles * LANES
    heads = step_bias.shape[0]
    local_heads = heads // 4
    own_rows = out_weight.shape[0]
    params = jnp.concatenate(
        [
            jnp.pad(jnp.stack([step_bias, decay_log, skip_gain]), ((0, 5), (0, LANES - heads))),
            kernel_bias.reshape(-1, LANES),
        ]
    )
    vmem = pl.BlockSpec(memory_space=pltpu.VMEM)
    V = pltpu.VMEM
    dma = pltpu.SemaphoreType.DMA
    shape = jax.ShapeDtypeStruct
    flat_shape = (conv_tiles + 2, 8, LANES)
    outs = [
        shape((4, count, width), bf16), shape((4, count, width), bf16), shape((own_rows, width), bf16),
        shape((2, 2, rows, quarter), bf16), shape((2, 2, rows, conv_cols), bf16),
        shape((4,) + flat_shape, f32),
    ]
    line_shapes = [(own_rows, width), (2, rows, quarter), (2, rows, conv_cols)]
    scratch = [
        V((4, count, width), bf16), V((4, count, width), bf16), V((2, 8, length), f32),
        V((rows, conv_cols), bf16), V((rows, quarter), bf16),
        V((shards, rows, conv_cols), bf16), V((shards, rows, quarter), bf16), V((top, own_rows, width), bf16),
        V((total, conv_cols), bf16), V((total, active), f32), V((total, active), f32),
        V((2, CONV - 1, length, LANES), f32), V((2, length, length), f32),
        V((total, LANES), f32), V((total, LANES), f32), V((total, LANES), f32),
        V((total, LANES), f32), V((2, LANES, length), f32), V((local_heads, total, LANES), f32),
        V((total, quarter), f32), V((8, quarter), f32), V((total, quarter), bf16),
        V((2, length, length), f32), V((2 * local_heads, length, length), f32),
        V((2 * local_heads, length, length), bf16), V((total, quarter), f32), V((total, quarter), bf16),
        V((total, quarter), bf16), V((total, quarter), f32), V((1, quarter), f32),
        V((total, LANES), f32), V((4, 8, total), f32), V((total, LANES), f32),
        V((total, quarter), bf16), V((total, quarter), bf16), V((total, quarter), bf16),
        V((8, quarter), f32), V((4, count, width), bf16), V((4, count, width), bf16),
        V((2, length, length), f32), V((total, quarter), f32), V((total, quarter), f32),
        V((total, active), f32), V((8, quarter), f32), V((total, conv_cols), bf16), V((8, width), f32),
        V((top, own_rows, width), bf16), V((top, 2, 2, rows, quarter), bf16),
        V((top, 2, 2, rows, conv_cols), bf16),
    ]
    for _ in range(4):
        scratch += [V((top,) + item, bf16) for item in line_shapes]
    scratch += [V(flat_shape, f32), V(flat_shape, f32), V((top,) + flat_shape, f32), V(flat_shape, f32)]
    scratch += [
        dma((SENDS,)), dma((2, 4)), dma((1,)), dma((shards,)), dma((shards,)), dma((top,)), dma((4,)),
        dma((2, 4)),
    ]
    scratch += [dma((top,)) for _ in range(9)]
    scratch += [dma((1,)), dma((2, 2)), dma((2, 2)), dma((3, max(4, top))), dma((6,))]
    hbm = pl.BlockSpec(memory_space=pl.ANY)
    results = pl.pallas_call(
        functools.partial(fused_kernel, top),
        out_shape=outs,
        in_specs=[vmem] * 9,
        out_specs=[hbm] * len(outs),
        scratch_shapes=scratch,
        compiler_params=pltpu.CompilerParams(
            collective_id=2, has_side_effects=True, vmem_limit_bytes=VMEM_LIMIT
        ),
    )(
        tokens, cotangent, documents, in_weight, kernel_taps, params,
        pre_gain.reshape(1, -1), norm_gain.reshape(1, -1), out_weight,
    )
    outs = [
        shape((count, width), bf16), shape((count, width), f32), shape((rows, columns), f32),
        shape((CONV, channels), f32), shape((channels // LANES, LANES), f32), shape((1, heads), f32),
        shape((1, heads), f32), shape((1, heads), f32), shape((1, width), f32), shape((1, inner), f32),
        shape((own_rows, width), f32),
    ]
    final = pl.pallas_call(
        functools.partial(finish_kernel, inner, heads),
        out_shape=outs,
        in_specs=[vmem] * 9,
        out_specs=[hbm] * len(outs),
        scratch_shapes=[V(out.shape, out.dtype) for out in outs] + [dma((len(outs),))],
        compiler_params=pltpu.CompilerParams(vmem_limit_bytes=VMEM_LIMIT),
    )(tokens, cotangent, pre_gain.reshape(1, -1), *results)
    return tuple(
        out.reshape(-1) if k in (4, 5, 6, 7, 8, 9) else out for k, out in enumerate(final)
    )


def fits(tokens, documents, in_weight, norm_gain, out_weight):
    groups, shards = lax.axis_size("seq"), lax.axis_size("fsdp")
    top, mid = factors(shards)
    length, inner = documents.shape[1], norm_gain.shape[0]
    heads = inner // HEAD_DIM
    return (
        groups == 2 and mid == 2 and top == 4 and length == min(SPAN, length)
        and tokens.shape[0] * groups == length and length % LANES == 0
        and out_weight.shape[0] == LANES and inner == shards * LANES
        and inner // 4 == top * LANES and heads % 32 == 0 and heads <= LANES
        and in_weight.shape[0] * shards == tokens.shape[1]
    )


def local(*arrays):
    tokens, _, documents, in_weight = arrays[:4]
    if fits(tokens, documents, in_weight, arrays[10], arrays[11]):
        return fused(*arrays)
    return general(*arrays)


def solution(mesh):
    rows = P(("fsdp", "seq"), None)
    split = P("fsdp", None)
    return jax.shard_map(
        local,
        mesh=mesh,
        in_specs=(rows, rows, split, split) + (P(),) * 7 + (split,),
        out_specs=(rows, rows, split) + (P(),) * 7 + (split,),
        check_vma=False,
    )
```

```python
import functools
import math

import jax
import jax.numpy as jnp
from jax import lax
from jax.experimental import pallas as pl
from jax.experimental.pallas import tpu as pltpu
from jax.sharding import PartitionSpec as P

HEAD_DIM = 64
STATE = 128
CONV = 4
SPAN = 256

norm_epsilon = 1e-05
bf16 = jnp.bfloat16
f32 = jnp.float32
contract_rows = (((1,), (1,)), ((), ()))
contract_tokens = (((0,), (0,)), ((), ()))


def dot(left, right, dims=(((1,), (0,)), ((), ()))):
    return lax.dot_general(left, right, dims, preferred_element_type=f32)


def pre_norm(values, gain):
    scale = lax.rsqrt(jnp.mean(values * values, axis=-1, keepdims=True) + norm_epsilon)
    return values * scale * gain


def product(spec, left, right):
    return jnp.einsum(spec, left.astype(bf16), right.astype(bf16), preferred_element_type=f32)


def mixer(segment, conv_in, step_raw, taps, tap_bias, bias_steps, log_rates, skips):
    length, channels = conv_in.shape
    heads = step_raw.shape[1]
    width = heads * HEAD_DIM
    summed = tap_bias + conv_in * taps[CONV - 1]
    for offset in range(1, CONV):
        shifted = jnp.concatenate(
            [jnp.zeros((offset, channels), f32), conv_in[: length - offset]], axis=0
        )
        matched = jnp.concatenate(
            [
                jnp.zeros((offset,), f32),
                (segment[offset:] == segment[: length - offset]).astype(f32),
            ]
        )
        summed = summed + taps[CONV - 1 - offset] * shifted * matched[:, None]
    active = jax.nn.silu(summed)
    values = active[:, :width].reshape(length, heads, HEAD_DIM).transpose(1, 0, 2)
    input_matrix = active[:, width : width + STATE]
    output_matrix = active[:, width + STATE :]
    steps_taken = jax.nn.softplus(step_raw + bias_steps)
    log_decay = (steps_taken * -jnp.exp(log_rates)).T
    scaled = values * steps_taken.T[:, :, None]
    span = min(SPAN, length)
    blocks = length // span
    places = jnp.arange(span)
    state = None
    outputs = []
    for block in range(blocks):
        at = slice(block * span, (block + 1) * span)
        seg = segment[at]
        cumul = jnp.cumsum(log_decay[:, at], axis=1)
        causal = (places[:, None] >= places[None, :]) & (seg[:, None] == seg[None, :])
        log_gap = cumul[:, :, None] - cumul[:, None, :]
        decay = jnp.where(causal[None], jnp.exp(jnp.where(causal[None], log_gap, 0.0)), 0.0)
        scores = product("in,jn->ij", output_matrix[at], input_matrix[at])
        inside = product("hij,hjp->hip", decay * scores[None], scaled[:, at])
        if state is not None:
            previous = segment[block * span - 1]
            entering = jnp.exp(cumul) * (seg == previous).astype(f32)[None]
            inside = inside + product("in,hnp->hip", output_matrix[at], state) * entering[:, :, None]
        if block + 1 < blocks:
            final = cumul[:, -1]
            leaving = jnp.exp(final[:, None] - cumul) * (seg == seg[-1]).astype(f32)[None]
            fresh = product("jn,hjp->hnp", input_matrix[at], scaled[:, at] * leaving[:, :, None])
            if state is None:
                state = fresh
            else:
                keeping = jnp.exp(final) * (seg[-1] == previous).astype(f32)
                state = keeping[:, None, None] * state + fresh
        outputs.append(inside)
    whole = outputs[0] if blocks == 1 else jnp.concatenate(outputs, axis=1)
    result = whole + values * skips[:, None, None]
    return result.transpose(1, 0, 2).reshape(length, width)

MESH = pl.DeviceIdType.MESH
VMEM_LIMIT = 60 * 1024 * 1024


def factors(shards):
    rest = shards // 2
    mid = 1 << (int(math.log2(rest)) // 2)
    return rest // mid, mid


def position(top, mid):
    me = lax.axis_index("fsdp")
    return me, me // (2 * mid), lax.rem(me // 2, mid), lax.rem(me, 2)


def slot_of(t, m, core, mid):
    return (t * mid + m) * 2 + core


def greet(groups, top, mid):
    me, t, m, core = position(top, mid)
    group = lax.axis_index("seq")
    peers = [{"fsdp": slot_of(lax.rem(t + d, top), m, core, mid)} for d in range(1, top)]
    peers += [{"fsdp": slot_of(t, lax.rem(m + e, mid), core, mid)} for e in range(1, mid)]
    peers += [{"fsdp": slot_of(t, m, 1 - core, mid)}]
    peers += [{"seq": lax.rem(group + k, groups)} for k in range(1, groups)]
    barrier = pltpu.get_barrier_semaphore()
    for peer in peers:
        pl.semaphore_signal(barrier, inc=1, device_id=peer, device_id_type=MESH)
    pl.semaphore_wait(barrier, len(peers))


def remote(source, target, send, receive, device):
    copy = pltpu.make_async_remote_copy(
        src_ref=source,
        dst_ref=target,
        send_sem=send,
        recv_sem=receive,
        device_id=device,
        device_id_type=MESH,
    )
    copy.start()
    return copy


def gather_kernel(groups, top, mid, count, *refs):
    rows, shards = refs[0], refs[1 : 1 + count]
    all_rows, wholes = refs[1 + count], refs[2 + count : 2 + 2 * count]
    send, receive, row_send, row_receive = refs[2 + 2 * count :]
    me, t, m, core = position(top, mid)
    group = lax.axis_index("seq")
    greet(groups, top, mid)
    copies = {}

    def launch(a, key, source, slot, device):
        copies[(a,) + key] = remote(
            source, wholes[a].at[slot], send.at[(a,) + key], receive.at[(a,) + key], device
        )

    other = {"fsdp": slot_of(t, m, 1 - core, mid)}
    for a in range(count):
        for d in range(1, top):
            peer = {"fsdp": slot_of(lax.rem(t + d, top), m, core, mid)}
            launch(a, (d, 0, 0), shards[a], me, peer)
        for e in range(1, mid):
            peer = {"fsdp": slot_of(t, lax.rem(m + e, mid), core, mid)}
            launch(a, (0, e, 0), shards[a], me, peer)
        launch(a, (0, 0, 1), shards[a], me, other)
    for k in range(1, groups):
        copies[("rows", k)] = remote(
            rows,
            all_rows.at[group],
            row_send.at[k],
            row_receive.at[k],
            {"seq": lax.rem(group + k, groups)},
        )
    for a in range(count):
        wholes[a][me] = shards[a][...]
    all_rows[group] = rows[...]
    for a in range(count):
        for d in range(1, top):
            copies[(a, d, 0, 0)].wait_recv()
            slot = slot_of(lax.rem(t - d + top, top), m, core, mid)
            for e in range(1, mid):
                peer = {"fsdp": slot_of(t, lax.rem(m + e, mid), core, mid)}
                launch(a, (d, e, 0), wholes[a].at[slot], slot, peer)
            launch(a, (d, 0, 1), wholes[a].at[slot], slot, other)
    for a in range(count):
        for d in range(top):
            for e in range(1, mid):
                copies[(a, d, e, 0)].wait_recv()
                slot = slot_of(lax.rem(t - d + top, top), lax.rem(m - e + mid, mid), core, mid)
                launch(a, (d, e, 1), wholes[a].at[slot], slot, other)
    for key, copy in copies.items():
        copy.wait_send()
        if key[0] == "rows" or key[3] == 1:
            copy.wait_recv()


def gather_all(groups, shards, rows, arrays):
    top, mid = factors(shards)
    count = len(arrays)
    vmem = pl.BlockSpec(memory_space=pltpu.VMEM)
    out = [jax.ShapeDtypeStruct((groups,) + rows.shape, rows.dtype)]
    out += [jax.ShapeDtypeStruct((shards,) + array.shape, array.dtype) for array in arrays]
    return pl.pallas_call(
        functools.partial(gather_kernel, groups, top, mid, count),
        out_shape=out,
        in_specs=[vmem] * (1 + count),
        out_specs=[vmem] * (1 + count),
        scratch_shapes=[
            pltpu.SemaphoreType.DMA((count, top, mid, 2)),
            pltpu.SemaphoreType.DMA((count, top, mid, 2)),
            pltpu.SemaphoreType.DMA((groups,)),
            pltpu.SemaphoreType.DMA((groups,)),
        ],
        compiler_params=pltpu.CompilerParams(
            collective_id=0, has_side_effects=True, vmem_limit_bytes=VMEM_LIMIT
        ),
    )(rows, *arrays)


CHUNKS = 2


def add(left, right):
    return (left.astype(f32) + right.astype(f32)).astype(bf16)


def scatter_kernel(groups, top, mid, count, *refs):
    partial, flat, grads = refs[0], refs[1], refs[2 : 2 + count]
    refs = refs[2 + count :]
    summed, total, owned = refs[0], refs[1], refs[2 : 2 + count]
    refs = refs[2 + count :]
    pair = refs[:count]
    middle = refs[count : 2 * count]
    line = refs[2 * count : 3 * count]
    far = refs[3 * count : 4 * count]
    flat_pair, flat_mid, flat_top, flat_group, send, receive, flat_send, flat_receive, sum_sems = (
        refs[4 * count :]
    )
    me, t, m, core = position(top, mid)
    group = lax.axis_index("seq")
    greet(groups, top, mid)
    other = {"fsdp": slot_of(t, m, 1 - core, mid)}
    to_mid = [{"fsdp": slot_of(t, lax.rem(m + e, mid), core, mid)} for e in range(mid)]
    to_top = [{"fsdp": slot_of(lax.rem(t + d, top), m, core, mid)} for d in range(top)]
    to_group = [{"seq": lax.rem(group + k, groups)} for k in range(groups)]
    copies = []

    def launch(source, target, index, device):
        copy = remote(source, target, send.at[index], receive.at[index], device)
        copies.append(copy)
        return copy

    def launch_flat(stage, buffer, own, peers):
        started = []
        for k in range(1, len(peers)):
            copy = remote(
                buffer.at[own],
                buffer.at[own],
                flat_send.at[stage, k],
                flat_receive.at[stage, k],
                peers[k],
            )
            started.append(copy)
            copies.append(copy)
        return started

    def total_of(buffer, started):
        for copy in started:
            copy.wait_recv()
        value = buffer[0]
        for k in range(1, buffer.shape[0]):
            value = value + buffer[k]
        return value

    work = [(a, r) for a in range(count) for r in range(CHUNKS)]
    rows_of = [grads[a].shape[3] // CHUNKS for a in range(count)]

    def part(a, r):
        return pl.ds(r * rows_of[a], rows_of[a])

    flat_pair[core] = flat[...]
    stage_flat = launch_flat(0, flat_pair, core, [None, other])
    stage = {}
    for n, (a, r) in enumerate(work):
        stage[n] = launch(
            grads[a].at[:, :, 1 - core, part(a, r)], pair[a].at[:, :, part(a, r)], (n, 0), other
        )
    sums = []
    for k in range(1, groups):
        copy = remote(
            partial.at[lax.rem(group + k, groups)],
            summed.at[group],
            sum_sems.at[0, k],
            sum_sems.at[1, k],
            to_group[k],
        )
        sums.append(copy)
    summed[group] = partial[group]

    stage_mid = {}
    for n, (a, r) in enumerate(work):
        stage[n].wait_recv()

        @pl.loop(0, top)
        def _(i):
            for j in range(mid):
                at = part(a, r)
                pair[a][i, j, at] = add(pair[a][i, j, at], grads[a][i, j, core, at])

        for e in range(1, mid):
            stage_mid[n, e] = launch(
                pair[a].at[:, lax.rem(m + e, mid), part(a, r)],
                middle[a].at[e - 1, :, part(a, r)],
                (n, e),
                to_mid[e],
            )
        if n == 0:
            flat_mid[m] = total_of(flat_pair, stage_flat)
            stage_flat = launch_flat(1, flat_mid, m, to_mid)
    stage_top = {}
    for n, (a, r) in enumerate(work):
        for e in range(1, mid):
            stage_mid[n, e].wait_recv()

        @pl.loop(0, top)
        def _(i):
            at = part(a, r)
            value = pair[a][i, m, at].astype(f32)
            for e in range(1, mid):
                value = value + middle[a][e - 1, i, at].astype(f32)
            line[a][i, at] = value.astype(bf16)

        for d in range(1, top):
            stage_top[n, d] = launch(
                line[a].at[lax.rem(t + d, top), part(a, r)],
                far[a].at[d - 1, part(a, r)],
                (n, mid + d - 1),
                to_top[d],
            )
        if n == 0:
            flat_top[t] = total_of(flat_mid, stage_flat)
            stage_flat = launch_flat(2, flat_top, t, to_top)
    last = []
    for n, (a, r) in enumerate(work):
        at = part(a, r)
        for d in range(1, top):
            stage_top[n, d].wait_recv()
        value = line[a][t, at].astype(f32)
        for d in range(1, top):
            value = value + far[a][d - 1, at].astype(f32)
        owned[a][group, at] = value.astype(bf16)
        for k in range(1, groups):
            last.append(
                launch(
                    owned[a].at[group, at],
                    owned[a].at[group, at],
                    (n, mid + top - 2 + k),
                    to_group[k],
                )
            )
        if n == 0:
            flat_group[group] = total_of(flat_top, stage_flat)
            stage_flat = launch_flat(3, flat_group, group, to_group)
    total[...] = total_of(flat_group, stage_flat)
    for copy in last:
        copy.wait_recv()
    for copy in sums:
        copy.wait()
    for copy in copies:
        copy.wait_send()


def scatter_all(groups, shards, partial, flat, grads):
    top, mid = factors(shards)
    count = len(grads)
    vmem = pl.BlockSpec(memory_space=pltpu.VMEM)
    grads = [grad.reshape(top, mid, 2, grad.shape[0] // shards, grad.shape[1]) for grad in grads]
    shapes = [grad.shape[3:] for grad in grads]
    out = [
        jax.ShapeDtypeStruct(partial.shape, bf16),
        jax.ShapeDtypeStruct(flat.shape, f32),
    ] + [jax.ShapeDtypeStruct((groups,) + shape, bf16) for shape in shapes]
    most = max(2, mid, top, groups)
    stages = mid + top + groups - 2
    return pl.pallas_call(
        functools.partial(scatter_kernel, groups, top, mid, count),
        out_shape=out,
        in_specs=[vmem] * (2 + count),
        out_specs=[vmem] * (2 + count),
        scratch_shapes=[pltpu.VMEM((top, mid) + shape, bf16) for shape in shapes]
        + [pltpu.VMEM((max(1, mid - 1), top) + shape, bf16) for shape in shapes]
        + [pltpu.VMEM((top,) + shape, bf16) for shape in shapes]
        + [pltpu.VMEM((max(1, top - 1),) + shape, bf16) for shape in shapes]
        + [pltpu.VMEM((size,) + flat.shape, f32) for size in (2, mid, top, groups)]
        + [
            pltpu.SemaphoreType.DMA((count * CHUNKS, stages)),
            pltpu.SemaphoreType.DMA((count * CHUNKS, stages)),
            pltpu.SemaphoreType.DMA((4, most)),
            pltpu.SemaphoreType.DMA((4, most)),
            pltpu.SemaphoreType.DMA((2, groups)),
        ],
        compiler_params=pltpu.CompilerParams(
            collective_id=1, has_side_effects=True, vmem_limit_bytes=VMEM_LIMIT
        ),
    )(partial, flat, *grads)


def general(
    tokens,
    cotangent,
    documents,
    in_weight,
    kernel_taps,
    kernel_bias,
    step_bias,
    decay_log,
    skip_gain,
    pre_gain,
    norm_gain,
    out_weight,
):
    groups = lax.axis_size("seq")
    shards = lax.axis_size("fsdp")
    group = lax.axis_index("seq")
    heads = step_bias.shape[0]
    inner = norm_gain.shape[0]
    states = kernel_bias.shape[0] - inner
    half = inner // groups
    spread = out_weight.shape[0] % (HEAD_DIM * groups) == 0
    parts = shards if spread else 1

    def pick(array, axis):
        size = array.shape[axis]
        lead, tail = array.shape[:axis], array.shape[axis + 1 :]
        split = array.reshape(lead + (parts, groups, size // (parts * groups)) + tail)
        chosen = lax.dynamic_index_in_dim(split, group, axis + 1, keepdims=False)
        return chosen.reshape(lead + (size // groups,) + tail)

    def place(array):
        size = array.shape[-1] * groups
        lead = array.shape[:-1]
        split = array.reshape(lead + (parts, 1, size // (parts * groups)))
        blank = jnp.zeros(lead + (parts, groups, size // (parts * groups)), array.dtype)
        full = lax.dynamic_update_slice_in_dim(blank, split, group, len(lead) + 1)
        return full.reshape(lead + (size,))

    def unite(array):
        rows, width = array.shape[1:]
        split = array.reshape(groups, rows, parts, width // parts)
        return split.transpose(1, 2, 0, 3).reshape(rows, width * groups)

    conv_end = inner + inner + states
    conv_shard = jnp.concatenate(
        [
            pick(in_weight[:, inner : 2 * inner], 1),
            in_weight[:, 2 * inner : conv_end],
            pick(in_weight[:, conv_end:], 1),
        ],
        axis=1,
    )
    gate_shard = pick(in_weight[:, :inner], 1)
    out_rows = out_weight
    if spread:
        split = out_weight.reshape(groups, out_weight.shape[0] // groups, out_weight.shape[1])
        out_rows = lax.dynamic_index_in_dim(split, group, 0, keepdims=False)
    floats = tokens.astype(f32)
    normed_own = pre_norm(floats, pre_gain).astype(bf16)
    count, width = tokens.shape
    joined, conv_weight, gate_weight, out_part = gather_all(
        groups,
        shards,
        jnp.concatenate([normed_own, cotangent], axis=1),
        [conv_shard, gate_shard, out_rows],
    )
    joined = joined.reshape(groups * count, 2 * width)
    conv_weight = conv_weight.reshape(width, -1)
    gate_weight = gate_weight.reshape(width, -1)
    out_part = out_part.reshape(-1, width)
    if not spread:
        out_part = lax.dynamic_slice_in_dim(out_part, group * half, half, 0)
    normed_in, cot = joined[:, :width], joined[:, width:]

    projected = dot(normed_in, conv_weight).astype(bf16).astype(f32)
    segment = documents[0]
    taps = jnp.concatenate([pick(kernel_taps[:, :inner], 1), kernel_taps[:, inner:]], axis=1)
    tap_bias = jnp.concatenate([pick(kernel_bias[:inner], 0), kernel_bias[inner:]], axis=0)
    mixed, mixer_back = jax.vjp(
        lambda *given: mixer(segment, *given),
        projected[:, : half + states],
        projected[:, half + states :],
        taps,
        tap_bias,
        pick(step_bias, 0),
        pick(decay_log, 0),
        pick(skip_gain, 0),
    )
    gain = pick(norm_gain, 0)
    gates = dot(normed_in, gate_weight).astype(bf16).astype(f32)
    mixed = mixed.astype(bf16).astype(f32)
    back_normed = dot(cot, out_part, contract_rows)
    sigmoid = jax.nn.sigmoid(gates)
    silu = gates * sigmoid
    gated = mixed * silu
    back_gain = back_normed * gain
    sums = lax.psum(
        jnp.stack([jnp.sum(gated * gated, axis=1), jnp.sum(gated * back_gain, axis=1)]), "seq"
    )
    scale = lax.rsqrt(sums[0] / inner + norm_epsilon)
    unit = gated * scale[:, None]
    normed_bf = (unit * gain).astype(bf16)
    norm_gain_part = jnp.sum(back_normed * unit, axis=0)
    back_gated = scale[:, None] * (back_gain - unit * (scale * sums[1] / inner)[:, None])
    back_mixed = (back_gated * silu).astype(bf16).astype(f32)
    back_gates = (back_gated * mixed * sigmoid * (1.0 + gates * (1.0 - sigmoid))).astype(bf16)

    outward = dot(normed_bf, cot, contract_tokens).astype(bf16)
    gate_grad = dot(normed_in, back_gates, contract_tokens).astype(bf16)
    if not spread:
        blank = jnp.zeros((inner, width), bf16)
        outward = lax.dynamic_update_slice_in_dim(blank, outward, group * half, 0)
    branch = dot(normed_bf, out_part).astype(bf16)

    back_conv, back_steps, taps_part, bias_part, step_part, decay_part, skip_part = mixer_back(
        back_mixed
    )
    back_projected = jnp.concatenate([back_conv, back_steps], axis=1).astype(bf16)
    conv_grad = dot(normed_in, back_projected, contract_tokens).astype(bf16)
    back_in = dot(back_projected, conv_weight, contract_rows) + dot(
        back_gates, gate_weight, contract_rows
    )
    pre_gain_part = jnp.sum(back_in * normed_in.astype(f32), axis=0) / pre_gain

    pieces = (
        jnp.concatenate([place(taps_part[:, :half]), taps_part[:, half:]], axis=1),
        jnp.concatenate([place(bias_part[:half]), bias_part[half:]], axis=0),
        place(step_part),
        place(decay_part),
        place(skip_part),
        pre_gain_part,
        place(norm_gain_part),
    )
    flat = jnp.concatenate([piece.reshape(-1) for piece in pieces])
    padded = jnp.pad(flat, (0, -flat.size % 1024)).reshape(-1, 128)
    partial = jnp.concatenate(
        [
            back_in.astype(bf16).reshape(groups, count, width),
            branch.reshape(groups, count, width),
        ],
        axis=1,
    )
    partial, padded, conv_all, gate_all, out_all = scatter_all(
        groups, shards, partial, padded, [conv_grad, gate_grad, outward]
    )
    partial = jnp.sum(partial.astype(f32), axis=0)
    block_output = (floats + partial[count:]).astype(bf16)
    _, pre_back = jax.vjp(lambda given: pre_norm(given, pre_gain), floats)
    tokens_grad = cotangent.astype(f32) + pre_back(partial[:count])[0]
    conv_all, gate_all, out_all = (
        conv_all.astype(f32),
        gate_all.astype(f32),
        out_all.astype(f32),
    )
    if spread:
        outward_grad = out_all.reshape(-1, width)
    else:
        outward_grad = jnp.sum(out_all, axis=0)
    inward_grad = jnp.concatenate(
        [
            unite(gate_all),
            unite(conv_all[:, :, :half]),
            jnp.sum(conv_all[:, :, half : half + states], axis=0),
            unite(conv_all[:, :, half + states :]),
        ],
        axis=1,
    )
    flat = padded.reshape(-1)
    totals = []
    start = 0
    for piece in pieces:
        totals.append(flat[start : start + piece.size].reshape(piece.shape))
        start += piece.size
    return (
        block_output,
        tokens_grad,
        inward_grad,
        totals[0],
        totals[1],
        totals[2],
        totals[3],
        totals[4],
        totals[5],
        totals[6],
        outward_grad,
    )


LANES = 128
FAR = -1e30
SENDS = 170
exact = lax.Precision.HIGHEST


def sharp(left, right, dims=(((1,), (0,)), ((), ()))):
    return lax.dot_general(left, right, dims, precision=exact, preferred_element_type=f32)


def iota(shape, axis):
    return lax.broadcasted_iota(jnp.int32, shape, axis)


def span_of(index, size):
    return pl.ds(pl.multiple_of(index * size, size), size)


class Courier:
    def __init__(self, send):
        self.send = send
        self.count = 0
        self.made = []
        self.stays = []

    def start(self, source, target, receive, device, when=None):
        slot = self.count
        self.count += 1

        def make():
            return pltpu.make_async_remote_copy(
                src_ref=source(),
                dst_ref=target(),
                send_sem=self.send.at[slot],
                recv_sem=receive(),
                device_id=device(),
                device_id_type=MESH,
            )

        self.made.append((make, when))
        self.run(lambda: make().start(), when)

    def run(self, act, when):
        if when is None:
            act()
        else:
            pl.when(when)(act)

    def arrive(self, target, receive, device):
        pltpu.make_async_remote_copy(
            src_ref=target,
            dst_ref=target,
            send_sem=self.send.at[0],
            recv_sem=receive,
            device_id=device,
            device_id_type=MESH,
        ).wait_recv()

    def local(self, source, target, sem, when=None):
        make = lambda: pltpu.make_async_copy(source(), target(), sem)
        self.stays.append((make, when))
        self.run(lambda: make().start(), when)

    def finish(self):
        for make, when in self.stays:
            self.run(lambda make=make: make().wait(), when)
        for make, when in self.made:
            self.run(lambda make=make: make().wait_send(), when)


def fused_kernel(top, *refs):
    (
        tokens, cotangent, documents, in_weight, taps, params, pre_gain, norm_gain, out_weight,
        got_b, got_i, own_out, own_gate, own_conv, own_sh, flat_all,
        sh_all, gr_sh, sib, line_sh, low_sh, high_sh, y_sh, fin_sh,
        r_sh, r_sib, rl_sh, rh_sh, ry_sh, ro_sh,
        nall, call, docs, conv_pack, gate_pack, conv_all, gate_all, out_all,
        proj, act, dact, mk, bias_mask, step, ldec, sgate, cum, cum_t, cum_b, step_e, skip_e, scaled,
        scores, decay, weigh, inside, mixed, gates, bnorm, gain_own, sums, sums_all, totals,
        normed_bf, bmixed, bgates, norm_part, part_b, part_i, dscore, x1, x2, dz, skip_part, bproj, pre_part,
        gr_out, gr_gate, gr_conv, y_out, y_gate, y_conv, line_out, line_gate, line_conv,
        low_out, low_gate, low_conv, high_out, high_gate, high_conv,
        flat, flat_y, flat_z, flat_own,
        send, r_rows, r_docs, r_conv, r_gate, r_out, r_sums, r_part,
        ry_out, ry_gate, ry_conv, rl_out, rl_gate, rl_conv, rh_out, rh_gate, rh_conv,
        ro_out, ro_gate, ro_conv, r_flat, r_local,
    ) = refs
    mid = 2
    me, t, m, c = position(top, mid)
    g = lax.axis_index("seq")
    count, width = tokens.shape
    length = documents.shape[1]
    seqs = 2
    total = seqs * length
    rows = in_weight.shape[0]
    inner = norm_gain.shape[1]
    quarter = inner // 4
    tiles = quarter // LANES
    states = taps.shape[1] - inner
    conv_tiles = tiles + states // LANES
    active = conv_tiles * LANES
    conv_cols = active + LANES
    heads = params_heads(inner)
    local_heads = heads // 4
    mail = Courier(send)

    def dev(tt, mm, cc):
        return lambda: {"fsdp": slot_of(tt, mm, cc, mid)}

    def dev_g(gg, tt, mm, cc):
        return lambda: {"seq": gg, "fsdp": slot_of(tt, mm, cc, mid)}

    here = {"fsdp": slot_of(t, m, 1 - c, mid)}
    group = [
        (2 * (1 - c) + g, dev_g(g, t, m, 1 - c)),
        (2 * c + 1 - g, dev_g(1 - g, t, m, c)),
        (2 * (1 - c) + 1 - g, dev_g(1 - g, t, m, 1 - c)),
    ]
    mine = 2 * c + g

    barrier = pltpu.get_barrier_semaphore()
    greeted = [d() for _, d in group]
    greeted += [{"fsdp": slot_of(t, 1 - m, cc, mid)} for cc in range(2)]
    greeted += [
        {"fsdp": slot_of(lax.rem(t + d, top), m, cc, mid)} for d in range(1, top) for cc in range(2)
    ]
    for peer in greeted:
        pl.semaphore_signal(barrier, inc=1, device_id=peer, device_id_type=MESH)

    def tile_of(n, cc):
        return 4 * n + 2 * cc + g

    def selector(cc):
        glob, loc = iota((LANES, LANES), 0), iota((LANES, LANES), 1)
        wanted = 8 * (loc // 2) + 4 * cc + 2 * g + loc % 2
        return jnp.where((glob == wanted) & (loc < local_heads), 1.0, 0.0)

    def pack(conv, gate, cc):
        for n in range(tiles):
            at = span_of(tile_of(n, cc) + inner // LANES, LANES)
            conv[:, n * LANES : (n + 1) * LANES] = in_weight[:, at]

    def pack_shared(shared):
        shared[:, :states] = in_weight[:, 2 * inner : 2 * inner + states]
        glob, loc = iota((heads, LANES), 0), iota((heads, LANES), 1)
        head = loc % local_heads
        wanted = 8 * (head // 2) + 4 * (loc // local_heads) + 2 * g + head % 2
        pick = jnp.where((glob == wanted) & (loc < 2 * local_heads), 1.0, 0.0).astype(bf16)
        shared[:, states:] = dot(in_weight[:, 2 * inner + states :], pick).astype(bf16)

    def pack_gate(gate, cc):
        for n in range(tiles):
            gate[:, n * LANES : (n + 1) * LANES] = in_weight[:, span_of(tile_of(n, cc), LANES)]

    pack_shared(sh_all.at[me])
    pack(conv_all.at[me], None, c)
    pack(conv_pack, None, 1 - c)
    pl.semaphore_wait(barrier, len(greeted))

    near = t + 1 - 2 * lax.rem(t, 2)
    far = lax.rem(t + top // 2, top)
    last = lax.rem(near + top // 2, top)

    def spread(mine_ref, pack_ref, all_ref, receive):
        for src, cc in ((mine_ref, c), (lambda: pack_ref, 1 - c)):
            for up in (1, -1):
                ok = (t + 1 < top) if up == 1 else (t >= 1)
                mail.start(
                    src, lambda: all_ref.at[me], lambda: receive.at[me],
                    dev(t + up, m, cc), ok,
                )
            mail.start(
                src, lambda: all_ref.at[me], lambda: receive.at[me], dev(t, 1 - m, cc)
            )
        mail.start(lambda: pack_ref, lambda: all_ref.at[me], lambda: receive.at[me], dev(t, m, 1 - c))

    def relay(all_ref, receive, d):
        for up in (1, -1):
            ok = (t >= d) if up == 1 else (t + d < top)
            onward = ok & ((t + 1 < top) if up == 1 else (t >= 1))
            from_t = jnp.clip(t - up * d, 0, top - 1)
            for cc in range(2):
                slot = slot_of(from_t, m, cc, mid)
                mail.run(lambda slot=slot: mail.arrive(all_ref.at[slot], receive.at[slot], here), ok)
                block = lambda slot=slot: all_ref.at[slot]
                sem = lambda slot=slot: receive.at[slot]
                mail.start(block, block, sem, dev(t + up, m, c), onward)
                mail.start(block, block, sem, dev(t, 1 - m, c), ok)

    def settle(all_ref, receive):
        slot = slot_of(t, m, 1 - c, mid)
        mail.arrive(all_ref.at[slot], receive.at[slot], here)
        for tt in range(top):
            for cc in range(2):
                slot = slot_of(tt, 1 - m, cc, mid)
                mail.arrive(all_ref.at[slot], receive.at[slot], here)

    def send_shared(slot, over_y):
        block, sem = (lambda: sh_all.at[slot]), (lambda: r_sh.at[slot])
        if over_y:
            mail.start(block, block, sem, dev(t, 1 - m, c))
        mail.start(block, block, sem, dev(t + 1, m, c), t + 1 < top)
        mail.start(block, block, sem, dev(t - 1, m, c), t >= 1)
        mail.start(block, block, sem, dev(t, m, 1 - c))

    def relay_shared(d):
        for up in (1, -1):
            ok = (t >= d) if up == 1 else (t + d < top)
            onward = ok & ((t + 1 < top) if up == 1 else (t >= 1))
            from_t = jnp.clip(t - up * d, 0, top - 1)
            for mm in range(mid):
                slot = slot_of(from_t, mm, c, mid)
                mail.run(lambda slot=slot: mail.arrive(sh_all.at[slot], r_sh.at[slot], here), ok)
                block = lambda slot=slot: sh_all.at[slot]
                sem = lambda slot=slot: r_sh.at[slot]
                mail.start(block, block, sem, dev(t + up, m, c), onward)
                mail.start(block, block, sem, dev(t, m, 1 - c), ok)

    def settle_shared():
        for tt in range(top):
            for mm in range(mid):
                slot = slot_of(tt, mm, 1 - c, mid)
                mail.arrive(sh_all.at[slot], r_sh.at[slot], here)

    send_shared(me, True)
    spread(lambda: conv_all.at[me], conv_pack, conv_all, r_conv)

    floats = tokens[...].astype(f32)
    nall[mine] = pre_norm(floats, pre_gain[...]).astype(bf16)
    for k, (_, device) in enumerate(group):
        mail.start(lambda: nall.at[mine], lambda: nall.at[mine], lambda: r_rows.at[0, mine], device)
    docs[c] = jnp.broadcast_to(documents[...].astype(f32), (8, length))
    mail.start(lambda: docs.at[c], lambda: docs.at[c], lambda: r_docs.at[0], dev(t, m, 1 - c))

    pack_gate(gate_all.at[me], c)
    pack_gate(gate_pack, 1 - c)
    other_y = slot_of(t, 1 - m, c, mid)
    mail.arrive(sh_all.at[other_y], r_sh.at[other_y], here)
    send_shared(other_y, False)
    relay_shared(1)
    relay(conv_all, r_conv, 1)
    spread(lambda: gate_all.at[me], gate_pack, gate_all, r_gate)

    holder = c == g
    keeper = c == m
    mail.run(lambda: out_all.__setitem__(t, out_weight[...]), holder & keeper)
    row_block = lambda: out_weight
    row_target = lambda: out_all.at[t]
    row_sem = lambda: r_out.at[t]
    mail.start(row_block, row_target, row_sem, dev(t + 1, m, m), holder & (t + 1 < top))
    mail.start(row_block, row_target, row_sem, dev(t - 1, m, m), holder & (t >= 1))
    mail.start(row_block, row_target, row_sem, dev(t, 1 - m, m), holder)
    mail.start(row_block, row_target, row_sem, dev(t, m, 1 - c), holder & (c != m))

    def relay_rows(d):
        for up in (1, -1):
            ok = keeper & ((t >= d) if up == 1 else (t + d < top))
            onward = ok & ((t + 1 < top) if up == 1 else (t >= 1))
            slot = jnp.clip(t - up * d, 0, top - 1)
            mail.run(lambda: mail.arrive(out_all.at[slot], r_out.at[slot], here), ok)
            block = lambda slot=slot: out_all.at[slot]
            sem = lambda slot=slot: r_out.at[slot]
            mail.start(block, block, sem, dev(t + up, m, c), onward)
            mail.start(block, block, sem, dev(t, 1 - m, c), ok)

    def settle_rows():
        mail.run(lambda: mail.arrive(out_all.at[t], r_out.at[t], here), keeper & (c != g))
        for tt in range(top):
            mail.run(lambda tt=tt: mail.arrive(out_all.at[tt], r_out.at[tt], here), c != m)

    call[mine] = cotangent[...]
    for k, (_, device) in enumerate(group):
        mail.start(lambda: call.at[mine], lambda: call.at[mine], lambda: r_rows.at[1, mine], device)

    for slot, _ in group:
        mail.arrive(nall.at[slot], r_rows.at[0, slot], here)
    mail.arrive(docs.at[1 - c], r_docs.at[0], here)

    @pl.loop(0, seqs)
    def _(s):
        row = docs[s][:1]
        column = jnp.broadcast_to(row, (LANES, length)).T
        wide = jnp.concatenate([column] * (length // LANES), axis=1)
        ahead = iota((length, length), 0) >= iota((length, length), 1)
        bias_mask[s] = jnp.where(ahead & (wide == row), 0.0, FAR)
        place = iota((length, LANES), 0)
        for k in range(1, CONV):
            same = (pltpu.roll(column, k, 0) == column) & (place >= k)
            mk[s, k - 1] = jnp.where(same, 1.0, 0.0)

    for n in range(tiles):
        gain_own[:, n * LANES : (n + 1) * LANES] = norm_gain[:, span_of(tile_of(n, c), LANES)]

    for d in range(2, top):
        relay_shared(d)
        relay(conv_all, r_conv, d)
    settle_shared()

    def tall(ref):
        return ref[...].reshape(total, width)

    def weights(ref, cols):
        return ref[:, :, cols].reshape(width, cols.size)

    wide_cols = 256
    proj[:, quarter:] = dot(tall(nall), sh_all[...].reshape(width, conv_cols - quarter)).astype(bf16)
    shift_in = jnp.where(iota((LANES, LANES), 0) == iota((LANES, LANES), 1) + local_heads * c, 1.0, 0.0)
    shift_in = jnp.where(iota((LANES, LANES), 1) < local_heads, shift_in, 0.0).astype(bf16)
    shift_out = jnp.where(iota((LANES, LANES), 1) == iota((LANES, LANES), 0) + local_heads * c, 1.0, 0.0)
    shift_out = jnp.where(iota((LANES, LANES), 0) < local_heads, shift_out, 0.0).astype(bf16)
    chosen = sharp(params[:8], selector(c))
    rate = jnp.exp(chosen[1:2])
    raw = dot(proj[:, active:], shift_in) + chosen[:1]
    step[...] = jnp.maximum(raw, 0.0) + jnp.log1p(jnp.exp(-jnp.abs(raw)))
    sgate[...] = jax.nn.sigmoid(raw)
    ldec[...] = step[...] * -rate
    to_channels = jnp.where(iota((LANES, quarter), 1) // HEAD_DIM == iota((LANES, quarter), 0), 1.0, 0.0)
    to_heads = jnp.where(iota((quarter, LANES), 0) // HEAD_DIM == iota((quarter, LANES), 1), 1.0, 0.0)
    step_e[...] = sharp(step[...], to_channels)
    skip_e[...] = sharp(chosen, to_channels)
    lower = jnp.where(iota((length, length), 0) >= iota((length, length), 1), 1.0, 0.0)
    for s in range(seqs):
        at = slice(s * length, (s + 1) * length)
        cum[at] = sharp(lower, ldec[at])
        cum_t[s] = cum[at].T
    for h in range(local_heads):
        cum_b[h] = jnp.broadcast_to(cum[:, h : h + 1], (total, LANES))

    settle(conv_all, r_conv)

    def tall(ref):
        return ref[...].reshape(total, width)

    def weights(ref, cols):
        return ref[:, :, cols].reshape(width, cols.size)


    @pl.loop(0, quarter // wide_cols)
    def _(n):
        at = span_of(n, wide_cols)
        proj[:, at] = dot(tall(nall), weights(conv_all, at)).astype(bf16)

    relay(gate_all, r_gate, 1)
    relay_rows(1)

    def conv_tile(n):
        return jnp.where(n < tiles, tile_of(n, c), n - tiles + inner // LANES)

    @pl.loop(0, seqs * conv_tiles)
    def _(i):
        s, n = i // conv_tiles, i % conv_tiles
        at, cols = span_of(s, length), span_of(n, LANES)
        where = span_of(conv_tile(n), LANES)
        x = proj[at, cols].astype(f32)
        tap = taps[:, where]
        z = params[pl.ds(8 + conv_tile(n), 1)] + x * tap[CONV - 1 : CONV]
        for k in range(1, CONV):
            z = z + tap[CONV - 1 - k : CONV - k] * (pltpu.roll(x, k, 0) * mk[s, k - 1])
        sig = jax.nn.sigmoid(z)
        act[at, cols] = z * sig
        dact[at, cols] = sig * (1.0 + z * (1.0 - sig))

    relay(gate_all, r_gate, 2)
    relay_rows(2)

    def matrices(s):
        at = span_of(s, length)
        return (
            act[at, quarter : quarter + STATE].astype(bf16),
            act[at, quarter + STATE : active].astype(bf16),
        )

    @pl.loop(0, seqs)
    def _(s):
        b_in, c_out = matrices(s)
        scores[s] = dot(c_out, b_in, contract_rows)

    half_of = lambda: iota((length, LANES), 1) // HEAD_DIM

    @pl.loop(0, seqs * tiles)
    def _(i):
        s, n = i // tiles, i % tiles
        at, cols = span_of(s, length), span_of(n, LANES)
        vals = act[at, cols]
        sc = (vals * step_e[at, cols]).astype(bf16)
        scaled[at, cols] = sc
        y = jnp.zeros((length, LANES), f32)
        for b in range(2):
            h = 2 * n + b
            col = cum_b[h, at]
            gap = jnp.concatenate([col] * (length // LANES), axis=1) - cum_t[s, pl.ds(h, 1)]
            d = jnp.exp(gap + bias_mask[s])
            decay[s * local_heads + h] = d
            w = (d * scores[s]).astype(bf16)
            weigh[s * local_heads + h] = w
            y = y + dot(w, jnp.where(half_of() == b, sc, jnp.zeros_like(sc)))
        inside[at, cols] = y
        mixed[at, cols] = (y + vals * skip_e[2:3, cols]).astype(bf16)

    for d in range(3, top):
        relay(gate_all, r_gate, d)
        relay_rows(d)
    settle(gate_all, r_gate)

    @pl.loop(0, quarter // wide_cols)
    def _(n):
        at = span_of(n, wide_cols)
        gates[:, at] = dot(tall(nall), weights(gate_all, at)).astype(bf16)

    settle_rows()
    for slot, _ in group:
        mail.arrive(call.at[slot], r_rows.at[1, slot], here)

    @pl.loop(0, tiles // 2)
    def _(n):
        w = out_all[pl.ds(2 * n, 2)].reshape(2 * LANES, width)
        bnorm[:, span_of(n, 2 * LANES)] = dot(tall(call), w, contract_rows)

    strip = 64

    @pl.loop(0, total // strip)
    def _(i):
        at = span_of(i, strip)
        gate = gates[at].astype(f32)
        gated = mixed[at].astype(f32) * (gate * jax.nn.sigmoid(gate))
        first = jnp.sum(gated * gated, axis=1, keepdims=True)
        second = jnp.sum(gated * (bnorm[at] * gain_own[...]), axis=1, keepdims=True)
        lane = iota((strip, LANES), 1)
        sums[at] = jnp.where(lane == 0, first, jnp.where(lane == 1, second, 0.0))

    sums_all[mine] = sums[...].T[:8]
    for k, (_, device) in enumerate(group):
        mail.start(lambda: sums_all.at[mine], lambda: sums_all.at[mine], lambda: r_sums.at[mine], device)
    for slot, _ in group:
        mail.arrive(sums_all.at[slot], r_sums.at[slot], here)
    summed = (sums_all[0] + sums_all[1]) + (sums_all[2] + sums_all[3])
    totals[...] = jnp.concatenate([summed, jnp.zeros((LANES - 8, total), f32)], axis=0).T

    norm_part[...] = jnp.zeros_like(norm_part)

    @pl.loop(0, total // strip)
    def _(i):
        at = span_of(i, strip)
        gate = gates[at].astype(f32)
        mix = mixed[at].astype(f32)
        sig = jax.nn.sigmoid(gate)
        silu = gate * sig
        gated = mix * silu
        gain = gain_own[...]
        scale = lax.rsqrt(totals[at, 0:1] / inner + norm_epsilon)
        unit = gated * scale
        back = bnorm[at]
        normed_bf[at] = (unit * gain).astype(bf16)
        norm_part[...] += jnp.sum(back * unit, axis=0, keepdims=True)
        back_gated = scale * (back * gain - unit * (scale * totals[at, 1:2] / inner))
        bmixed[at] = (back_gated * silu).astype(bf16)
        bgates[at] = (back_gated * mix * sig * (1.0 + gate * (1.0 - sig))).astype(bf16)

    def tall_cols(ref, at):
        return ref[:, :, at].reshape(total, at.size)

    def add_blocks(target, left, right):
        *lead, tall_rows, cols = target.shape
        piece = 32
        for at in [()] if not lead else [(i,) for i in range(lead[0])]:

            @pl.loop(0, tall_rows // piece)
            def _(i, at=at):
                where = at + (span_of(i, piece),)
                target[where] = add(left[where], right[where])

    def reducer(own, y_got, y_sem, line, low, low_sem, high, high_sem, ok=None):
        def step(r):
            def take():
                mail.arrive(y_got.at[r], y_sem.at[r], here)
                add_blocks(line.at[r], own(r), y_got.at[r])
                if r >= 2:
                    mail.arrive(low.at[r - 2], low_sem.at[r - 2], here)
                    add_blocks(line.at[r], line.at[r], low.at[r - 2])
                if r == 3:
                    mail.arrive(high.at[0], high_sem.at[0], here)
                    add_blocks(line.at[r], line.at[r], high.at[0])

            mail.run(take, ok)
            if r < 2:
                mail.start(
                    lambda: line.at[r], lambda: low.at[r], lambda: low_sem.at[r], dev(near, m, c), ok
                )
            if r == 2:
                mail.start(
                    lambda: line.at[r], lambda: high.at[0], lambda: high_sem.at[0], dev(far, m, c), ok
                )

        return step

    def hand_over(line, own, receive, at):
        mail.local(lambda: line.at[3, c], lambda: own.at[g, c], r_local.at[at])
        for gg, cc in ((g, 1 - c), (1 - g, c), (1 - g, 1 - c)):
            mail.start(
                lambda cc=cc: line.at[3, cc], lambda: own.at[g, c], lambda: receive.at[g, c],
                dev_g(gg, t, m, cc),
            )

    def take_over(own, receive):
        for gg, cc in ((g, 1 - c), (1 - g, c), (1 - g, 1 - c)):
            mail.arrive(own.at[gg, cc], receive.at[gg, cc], here)

    out_step = reducer(
        lambda r: gr_out.at[r], y_out, ry_out, line_out, low_out, rl_out, high_out, rh_out, keeper
    )
    gate_step = reducer(
        lambda r: gr_gate.at[r, m], y_gate, ry_gate, line_gate, low_gate, rl_gate, high_gate, rh_gate
    )
    conv_step = reducer(
        lambda r: gr_conv.at[r, m], y_conv, ry_conv, line_conv, low_conv, rl_conv, high_conv, rh_conv
    )
    sh_step = reducer(
        lambda r: gr_sh.at[r, c], sib, r_sib, line_sh, low_sh, rl_sh, high_sh, rh_sh
    )
    order = (last, near, far, t)
    block = width // top

    for r in range(top):
        got = dot(tall_cols(nall, span_of(order[r], block)), bgates[...], contract_tokens).astype(bf16)
        gr_gate[r] = got.reshape(gr_gate.shape[1:])
        mail.start(
            lambda r=r: gr_gate.at[r, 1 - m], lambda r=r: y_gate.at[r], lambda r=r: ry_gate.at[r],
            dev(t, 1 - m, c),
        )

    for r in range(top):
        gr_out[r] = dot(normed_bf[:, span_of(order[r], LANES)], tall(call), contract_tokens).astype(bf16)
        mail.start(
            lambda r=r: gr_out.at[r], lambda r=r: y_out.at[r], lambda r=r: ry_out.at[r],
            dev(t, 1 - m, c), c != m,
        )

    @pl.loop(0, width // wide_cols)
    def _(n):
        at = span_of(n, wide_cols)
        w = out_all[:, :, at].reshape(quarter, wide_cols)
        part_b[:, :, at] = dot(normed_bf[...], w).astype(bf16).reshape(4, count, wide_cols)

    for slot, device in group:
        mail.start(
            lambda slot=slot: part_b.at[slot], lambda: got_b.at[mine], lambda: r_part.at[0, mine], device
        )
    mail.local(lambda: part_b.at[mine], lambda: got_b.at[mine], r_local.at[3])

    skip_part[...] = jnp.zeros_like(skip_part)
    dscore[...] = jnp.zeros_like(dscore)

    @pl.loop(0, seqs * tiles)
    def _(i):
        s, n = i // tiles, i % tiles
        at, cols = span_of(s, length), span_of(n, LANES)
        back = bmixed[at, cols]
        sc = scaled[at, cols]
        ds = jnp.zeros((length, LANES), f32)
        gather = dscore[s]
        for b in range(2):
            h = s * local_heads + 2 * n + b
            one = jnp.where(half_of() == b, back, jnp.zeros_like(back))
            gather = gather + decay[h] * dot(one, sc, contract_rows)
            ds = ds + dot(weigh[h], one, contract_tokens)
        dscore[s] = gather
        back = back.astype(f32)
        vals = act[at, cols]
        x1[at, cols] = back * inside[at, cols] - sc.astype(f32) * ds
        x2[at, cols] = ds * vals
        dz[at, cols] = (back * skip_e[2:3, cols] + ds * step_e[at, cols]) * dact[at, cols]
        skip_part[:, cols] += jnp.sum(back * vals, axis=0, keepdims=True)

    gate_step(0)
    @pl.loop(0, seqs)
    def _(s):
        at = span_of(s, length)
        b_in, c_out = matrices(s)
        ds = dscore[s].astype(bf16)
        b_cols, c_cols = slice(quarter, quarter + STATE), slice(quarter + STATE, active)
        dz[at, b_cols] = dot(ds, c_out, contract_tokens) * dact[at, b_cols]
        dz[at, c_cols] = dot(ds, b_in) * dact[at, c_cols]

    back_cum = sharp(x1[...], to_heads)
    back_step = sharp(x2[...], to_heads)
    upper = jnp.where(iota((length, length), 0) <= iota((length, length), 1), 1.0, 0.0)
    back_decay = jnp.concatenate(
        [sharp(upper, back_cum[s * length : (s + 1) * length]) for s in range(seqs)], axis=0
    )
    back_raw = (back_step - back_decay * rate) * sgate[...]
    bproj[:, active:] = dot(back_raw.astype(bf16), shift_out).astype(bf16)
    flat[conv_tiles] = jnp.concatenate(
        [norm_part[:1, n * LANES : (n + 1) * LANES] for n in range(tiles)]
        + [
            jnp.sum(back_raw, axis=0, keepdims=True),
            jnp.sum(back_decay * ldec[...], axis=0, keepdims=True),
            sharp(skip_part[...], to_heads)[:1],
            jnp.zeros((8 - tiles - 3, LANES), f32),
        ],
        axis=0,
    )

    gate_step(1)
    @pl.loop(0, conv_tiles)
    def _(n):
        cols, where = span_of(n, LANES), span_of(conv_tile(n), LANES)
        tap = taps[:, where]
        grads = [jnp.zeros((1, LANES), f32) for _ in range(CONV + 1)]
        for s in range(seqs):
            at = slice(s * length, (s + 1) * length)
            x = proj[at, cols].astype(f32)
            back = dz[at, cols]
            dx = back * tap[CONV - 1 : CONV]
            grads[CONV] += jnp.sum(back, axis=0, keepdims=True)
            grads[CONV - 1] += jnp.sum(back * x, axis=0, keepdims=True)
            for k in range(1, CONV):
                kept = back * mk[s, k - 1]
                dx = dx + tap[CONV - 1 - k : CONV - k] * pltpu.roll(kept, length - k, 0)
                grads[CONV - 1 - k] += jnp.sum(kept * pltpu.roll(x, k, 0), axis=0, keepdims=True)
            bproj[at, cols] = dx.astype(bf16)
        flat[n] = jnp.concatenate(grads + [jnp.zeros((8 - CONV - 1, LANES), f32)], axis=0)

    @pl.loop(0, width // wide_cols)
    def _(n):
        at = span_of(n, wide_cols)
        slots = pl.ds(n * (wide_cols // rows), wide_cols // rows)
        value = dot(bproj[:, :quarter], conv_all[slots].reshape(wide_cols, quarter), contract_rows)
        value = value + dot(
            bproj[:, quarter:], sh_all[slots].reshape(wide_cols, conv_cols - quarter), contract_rows
        )
        value = value + dot(bgates[...], gate_all[slots].reshape(wide_cols, quarter), contract_rows)
        part_i[:, :, at] = value.astype(bf16).reshape(4, count, wide_cols)
        seen = tall_cols(nall, at).astype(f32)
        pre_part[:, at] = jnp.broadcast_to(
            jnp.sum(value * seen, axis=0, keepdims=True) / pre_gain[:, at], (8, wide_cols)
        )

    for slot, device in group:
        mail.start(
            lambda slot=slot: part_i.at[slot], lambda: got_i.at[mine], lambda: r_part.at[1, mine], device
        )
    mail.local(lambda: part_i.at[mine], lambda: got_i.at[mine], r_local.at[4])
    flat[conv_tiles + 1] = jnp.concatenate(
        [pre_part[:1, n * LANES : (n + 1) * LANES] for n in range(width // LANES)], axis=0
    )
    mail.start(lambda: flat, lambda: flat_y, lambda: r_flat.at[0, 0], dev(t, 1 - m, c))

    for r in range(top):
        got = dot(tall_cols(nall, span_of(order[r], block)), bproj[...], contract_tokens).astype(bf16)
        gr_conv[r] = got[:, :quarter].reshape(gr_conv.shape[1:])
        for k in range(4):
            gr_sh[r, k % 2, k // 2] = got[k * rows : (k + 1) * rows, quarter:]
        mail.start(
            lambda r=r: gr_sh.at[r, 1 - c], lambda r=r: sib.at[r], lambda r=r: r_sib.at[r],
            dev(t, m, 1 - c),
        )
        mail.start(
            lambda r=r: gr_conv.at[r, 1 - m], lambda r=r: y_conv.at[r], lambda r=r: ry_conv.at[r],
            dev(t, 1 - m, c),
        )

    gate_step(2)
    out_step(0)
    gate_step(3)
    hand_over(line_gate, own_gate, ro_gate, 0)
    sh_step(0)
    sh_step(1)
    out_step(1)
    out_step(2)
    sh_step(2)
    mail.arrive(flat_y, r_flat.at[0, 0], here)
    flat_z[t] = flat[...] + flat_y[...]
    for d in range(1, top):
        mail.start(
            lambda: flat_z.at[t], lambda: flat_z.at[t], lambda: r_flat.at[1, t],
            dev(lax.rem(t + d, top), m, c),
        )

    conv_step(0)
    conv_step(1)
    sh_step(3)
    mail.start(lambda: line_sh.at[3, 1 - m], lambda: y_sh, lambda: ry_sh.at[0], dev(t, 1 - m, c))
    out_step(3)
    mail.local(lambda: line_out.at[3], lambda: own_out, r_local.at[2], keeper & holder)
    mail.start(
        lambda: line_out.at[3], lambda: own_out, lambda: ro_out.at[0], dev_g(g, t, m, 1 - c),
        keeper & (c != g),
    )
    mail.start(
        lambda: line_out.at[3], lambda: own_out, lambda: ro_out.at[0], dev_g(1 - g, t, m, g), keeper
    )
    for d in range(1, top):
        slot = lax.rem(t - d + top, top)
        mail.arrive(flat_z.at[slot], r_flat.at[1, slot], here)
    value = flat_z[0]
    for k in range(1, top):
        value = value + flat_z[k]
    flat_own[...] = value
    for slot, device in group:
        mail.start(lambda: flat_own, lambda: flat_all.at[mine], lambda: r_flat.at[2, mine], device)
    mail.local(lambda: flat_own, lambda: flat_all.at[mine], r_local.at[5])
    conv_step(2)
    mail.arrive(y_sh, ry_sh.at[0], here)
    fin_sh[...] = add(line_sh[3, m], y_sh[...])
    mail.start(lambda: fin_sh, lambda: own_sh.at[g], lambda: ro_sh.at[0], dev_g(1 - g, t, m, c))
    mail.local(lambda: fin_sh, lambda: own_sh.at[g], r_local.at[6])
    conv_step(3)
    hand_over(line_conv, own_conv, ro_conv, 1)

    for k in range(2):
        for slot, _ in group:
            mail.arrive((got_b, got_i)[k].at[slot], r_part.at[k, slot], here)
    mail.run(lambda: mail.arrive(own_out, ro_out.at[0], here), jnp.logical_not(holder & keeper))
    take_over(own_gate, ro_gate)
    for slot, _ in group:
        mail.arrive(flat_all.at[slot], r_flat.at[2, slot], here)
    mail.arrive(own_sh.at[1 - g], ro_sh.at[0], here)
    take_over(own_conv, ro_conv)
    mail.finish()


def finish_kernel(inner, heads, *refs):
    (
        tokens, cotangent, pre_gain, got_b, got_i, own_out, own_gate, own_conv, own_sh, flat_all,
        *targets,
    ) = refs
    outs, scratch, sems = targets[:11], targets[11:22], targets[22]
    (
        block_output, tokens_grad, in_grad, taps_grad, bias_grad, step_grad, decay_grad, skip_grad,
        pre_grad, norm_grad, out_grad,
    ) = scratch
    count, width = tokens.shape
    quarter = inner // 4
    tiles = quarter // LANES
    states = taps_grad.shape[1] - inner
    conv_tiles = tiles + states // LANES
    active = conv_tiles * LANES
    local_heads = heads // 4

    def send(*which):
        for k in which:
            pltpu.make_async_copy(scratch[k], outs[k], sems.at[k]).start()

    parts = [(gg, cc, flat_all.at[2 * cc + gg]) for gg in range(2) for cc in range(2)]

    def selector_of(gg, cc):
        loc, glob = iota((LANES, LANES), 0), iota((LANES, LANES), 1)
        wanted = 8 * (loc // 2) + 4 * cc + 2 * gg + loc % 2
        return jnp.where((glob == wanted) & (loc < local_heads), 1.0, 0.0)

    def put_tiles(base, own):
        for gg in range(2):
            for cc in range(2):
                for n in range(tiles):
                    j = base + 4 * n + 2 * cc + gg
                    in_grad[:, j * LANES : (j + 1) * LANES] = own[
                        gg, cc, :, n * LANES : (n + 1) * LANES
                    ].astype(f32)

    put_tiles(0, own_gate)
    put_tiles(inner // LANES, own_conv)
    shared = own_sh[0].astype(f32) + own_sh[1].astype(f32)
    in_grad[:, 2 * inner : 2 * inner + states] = shared[:, :states]

    def both_of(gg):
        loc, glob = iota((LANES, LANES), 0), iota((LANES, LANES), 1)
        head = loc % local_heads
        wanted = 8 * (head // 2) + 4 * (loc // local_heads) + 2 * gg + head % 2
        return jnp.where((glob == wanted) & (loc < 2 * local_heads), 1.0, 0.0).astype(bf16)

    ends = sum(dot(own_sh[gg, :, states:], both_of(gg)) for gg in range(2))
    in_grad[:, 2 * inner + states :] = ends[:, :heads]
    send(2)
    out_grad[...] = own_out[...].astype(f32)
    send(10)

    for gg, cc, part in parts:
        for n in range(tiles):
            j = 4 * n + 2 * cc + gg
            at = slice(j * LANES, (j + 1) * LANES)
            taps_grad[:, at] = part[n, :CONV]
            bias_grad[j : j + 1] = part[n, CONV : CONV + 1]
            norm_grad[:, at] = part[conv_tiles, n : n + 1]
    for n in range(tiles, conv_tiles):
        j = n - tiles + inner // LANES
        value = sum(part[n] for _, _, part in parts)
        taps_grad[:, j * LANES : (j + 1) * LANES] = value[:CONV]
        bias_grad[j : j + 1] = value[CONV : CONV + 1]
    by_head = sum(sharp(part[conv_tiles], selector_of(gg, cc)) for gg, cc, part in parts)
    step_grad[...] = by_head[tiles : tiles + 1, :heads]
    decay_grad[...] = by_head[tiles + 1 : tiles + 2, :heads]
    skip_grad[...] = by_head[tiles + 2 : tiles + 3, :heads]
    value = sum(part[conv_tiles + 1] for _, _, part in parts)
    for n in range(width // LANES):
        pre_grad[:, n * LANES : (n + 1) * LANES] = value[n : n + 1]
    send(3, 4, 5, 6, 7, 8, 9)

    @pl.loop(0, count // 16)
    def _(i):
        at = span_of(i, 16)
        x = tokens[at].astype(f32)
        branch = sum(got_b[q, at].astype(f32) for q in range(4))
        back = sum(got_i[q, at].astype(f32) for q in range(4)) * pre_gain[...]
        block_output[at] = (x + branch).astype(bf16)
        scale = lax.rsqrt(jnp.mean(x * x, axis=1, keepdims=True) + norm_epsilon)
        shared = jnp.mean(x * back, axis=1, keepdims=True) * (scale * scale * scale)
        tokens_grad[at] = cotangent[at].astype(f32) + back * scale - x * shared

    send(0, 1)
    for k in range(len(outs)):
        pltpu.make_async_copy(scratch[k], outs[k], sems.at[k]).wait()


def params_heads(inner):
    return inner // HEAD_DIM


def fused(
    tokens, cotangent, documents, in_weight, kernel_taps, kernel_bias, step_bias, decay_log, skip_gain,
    pre_gain, norm_gain, out_weight,
):
    shards = lax.axis_size("fsdp")
    top, mid = factors(shards)
    count, width = tokens.shape
    length = documents.shape[1]
    total = 2 * length
    rows, columns = in_weight.shape
    inner = norm_gain.shape[0]
    channels = kernel_bias.shape[0]
    quarter = inner // 4
    tiles = quarter // LANES
    conv_tiles = tiles + (channels - inner) // LANES
    conv_cols = (conv_tiles + 1) * LANES
    active = conv_tiles * LANES
    heads = step_bias.shape[0]
    local_heads = heads // 4
    own_rows = out_weight.shape[0]
    params = jnp.concatenate(
        [
            jnp.pad(jnp.stack([step_bias, decay_log, skip_gain]), ((0, 5), (0, LANES - heads))),
            kernel_bias.reshape(-1, LANES),
        ]
    )
    vmem = pl.BlockSpec(memory_space=pltpu.VMEM)
    V = pltpu.VMEM
    dma = pltpu.SemaphoreType.DMA
    shape = jax.ShapeDtypeStruct
    sh_cols = conv_cols - quarter
    flat_shape = (conv_tiles + 2, 8, LANES)
    outs = [
        shape((4, count, width), bf16), shape((4, count, width), bf16), shape((own_rows, width), bf16),
        shape((2, 2, rows, quarter), bf16), shape((2, 2, rows, quarter), bf16),
        shape((2, rows, sh_cols), bf16),
        shape((4,) + flat_shape, f32),
    ]
    line_shapes = [(own_rows, width), (2, rows, quarter), (2, rows, quarter)]
    sh = (2, rows, sh_cols)
    scratch = [
        V((shards, rows, sh_cols), bf16), V((top, 2) + sh, bf16), V((top,) + sh, bf16), V((top,) + sh, bf16),
        V((2,) + sh, bf16), V((1,) + sh, bf16), V(sh[1:], bf16), V(sh[1:], bf16),
        dma((shards,)), dma((top,)), dma((2,)), dma((1,)), dma((1,)), dma((1,)),
        V((4, count, width), bf16), V((4, count, width), bf16), V((2, 8, length), f32),
        V((rows, quarter), bf16), V((rows, quarter), bf16),
        V((shards, rows, quarter), bf16), V((shards, rows, quarter), bf16), V((top, own_rows, width), bf16),
        V((total, conv_cols), bf16), V((total, active), f32), V((total, active), f32),
        V((2, CONV - 1, length, LANES), f32), V((2, length, length), f32),
        V((total, LANES), f32), V((total, LANES), f32), V((total, LANES), f32),
        V((total, LANES), f32), V((2, LANES, length), f32), V((local_heads, total, LANES), f32),
        V((total, quarter), f32), V((8, quarter), f32), V((total, quarter), bf16),
        V((2, length, length), f32), V((2 * local_heads, length, length), f32),
        V((2 * local_heads, length, length), bf16), V((total, quarter), f32), V((total, quarter), bf16),
        V((total, quarter), bf16), V((total, quarter), f32), V((1, quarter), f32),
        V((total, LANES), f32), V((4, 8, total), f32), V((total, LANES), f32),
        V((total, quarter), bf16), V((total, quarter), bf16), V((total, quarter), bf16),
        V((8, quarter), f32), V((4, count, width), bf16), V((4, count, width), bf16),
        V((2, length, length), f32), V((total, quarter), f32), V((total, quarter), f32),
        V((total, active), f32), V((8, quarter), f32), V((total, conv_cols), bf16), V((8, width), f32),
        V((top, own_rows, width), bf16), V((top, 2, 2, rows, quarter), bf16),
        V((top, 2, 2, rows, quarter), bf16),
    ]
    for _ in range(4):
        scratch += [V((top,) + item, bf16) for item in line_shapes]
    scratch += [V(flat_shape, f32), V(flat_shape, f32), V((top,) + flat_shape, f32), V(flat_shape, f32)]
    scratch += [
        dma((SENDS,)), dma((2, 4)), dma((1,)), dma((shards,)), dma((shards,)), dma((top,)), dma((4,)),
        dma((2, 4)),
    ]
    scratch += [dma((top,)) for _ in range(9)]
    scratch += [dma((1,)), dma((2, 2)), dma((2, 2)), dma((3, max(4, top))), dma((7,))]
    hbm = pl.BlockSpec(memory_space=pl.ANY)
    results = pl.pallas_call(
        functools.partial(fused_kernel, top),
        out_shape=outs,
        in_specs=[vmem] * 9,
        out_specs=[hbm] * len(outs),
        scratch_shapes=scratch,
        compiler_params=pltpu.CompilerParams(
            collective_id=2, has_side_effects=True, vmem_limit_bytes=VMEM_LIMIT
        ),
    )(
        tokens, cotangent, documents, in_weight, kernel_taps, params,
        pre_gain.reshape(1, -1), norm_gain.reshape(1, -1), out_weight,
    )
    outs = [
        shape((count, width), bf16), shape((count, width), f32), shape((rows, columns), f32),
        shape((CONV, channels), f32), shape((channels // LANES, LANES), f32), shape((1, heads), f32),
        shape((1, heads), f32), shape((1, heads), f32), shape((1, width), f32), shape((1, inner), f32),
        shape((own_rows, width), f32),
    ]
    final = pl.pallas_call(
        functools.partial(finish_kernel, inner, heads),
        out_shape=outs,
        in_specs=[vmem] * 10,
        out_specs=[hbm] * len(outs),
        scratch_shapes=[V(out.shape, out.dtype) for out in outs] + [dma((len(outs),))],
        compiler_params=pltpu.CompilerParams(vmem_limit_bytes=VMEM_LIMIT),
    )(tokens, cotangent, pre_gain.reshape(1, -1), *results)
    return tuple(
        out.reshape(-1) if k in (4, 5, 6, 7, 8, 9) else out for k, out in enumerate(final)
    )


def fits(tokens, documents, in_weight, norm_gain, out_weight):
    groups, shards = lax.axis_size("seq"), lax.axis_size("fsdp")
    top, mid = factors(shards)
    length, inner = documents.shape[1], norm_gain.shape[0]
    heads = inner // HEAD_DIM
    return (
        groups == 2 and mid == 2 and top == 4 and length == min(SPAN, length)
        and tokens.shape[0] * groups == length and length % LANES == 0
        and out_weight.shape[0] == LANES and inner == shards * LANES
        and inner // 4 == top * LANES and heads % 32 == 0 and heads <= LANES
        and in_weight.shape[0] * shards == tokens.shape[1]
    )


def local(*arrays):
    tokens, _, documents, in_weight = arrays[:4]
    if fits(tokens, documents, in_weight, arrays[10], arrays[11]):
        return fused(*arrays)
    return general(*arrays)


def solution(mesh):
    rows = P(("fsdp", "seq"), None)
    split = P("fsdp", None)
    return jax.shard_map(
        local,
        mesh=mesh,
        in_specs=(rows, rows, split, split) + (P(),) * 7 + (split,),
        out_specs=(rows, rows, split) + (P(),) * 7 + (split,),
        check_vma=False,
    )
```
